512 devices in a mesh: row: 32 (over y, x), col: 16 (over z, core).
Axes of the slice: x: 4, y: 8, z: 8, core: 2. Of those that a mesh axis runs over, the one named last changes fastest.
Arguments:
- prior_sample_fields: float32 [128, 256, 4096], P(None, 'row', 'col'), may hold values from -6 to 6
- spreading_coefficient: float32 [256, 4096], P('row', 'col'), may hold values from 0.02 to 0.12
- transport_courant: float32 [2, 256, 4096], P(None, 'row', 'col'), may hold values from 0 to 0.18
- obs_cells: int32 [65536], P(('row', 'col')), may hold values from 0 to 2047
- obs_value: float32 [65536], P(('row', 'col')), may hold values from -6 to 6
- obs_error: float32 [65536], P(('row', 'col')), may hold values from 4 to 32
Outputs:
- analysis: float32 [128, 256, 4096], P(None, 'row', 'col')
The draws below stay inside these ranges and needn't reach their ends.
All inputs are finite; a program needn't handle non-finite values.
Results may differ from the reference program's by a relative error of at most 0.00011.
Values sent between devices are 32-bit elements; how exact they have to be, the bound alone decides.
A program may use at most 64 MiB of HBM per device.

```python
import math
import jax
import jax.numpy as jnp
from jax import lax

MEMBERS = 128
CX = 8
CY = 256
P_DEV = 128
NX = 256
NY = 4096
NOBS = 65536
N_COL = 16


def plant(array, own_key, least, largest):
    longest = array.shape.index(max(array.shape))
    spots = []
    for shift in (0, 1):
        where = [jax.random.randint(jax.random.fold_in(own_key, axis), (), 0, length) for axis, length in enumerate(array.shape)]
        where[longest] = (where[longest] + shift) % array.shape[longest]
        spots.append(tuple(where))
    return array.at[spots[0]].set(least).at[spots[1]].set(largest)


def steps_of(own_key, shape, cuts, smallest, largest):
    factor_of, own = 1.0, jax.random.fold_in(own_key, 6)
    for dim, shards_of in cuts:
        draws = jnp.exp(jax.random.uniform(jax.random.fold_in(own, dim), (shards_of,), jnp.float32, smallest / len(cuts), largest / len(cuts)))
        factor_of = factor_of * jnp.repeat(draws, shape[dim] // shards_of).reshape([-1 if axis == dim else 1 for axis in range(len(shape))])
    return factor_of


def normal_values(key, dims, width, limit, shards=(), kind=jnp.bfloat16):
    array = width * jax.random.normal(key, dims, jnp.float32)
    if shards:
        array = array * steps_of(key, dims, shards, -0.22, 0.18)
    return jnp.clip(array, -limit, limit).astype(kind)


def setup_inputs(seed: int = 0) -> dict:
    streams_of = jax.random.split(jax.random.key(seed), 7)
    prior_sample_fields = normal_values(streams_of[0], (MEMBERS, NX, NY), 1.0, 6.0, ((1, 32), (2, 16)), jnp.float32)
    spreading_coefficient = jnp.clip(jnp.exp(math.log(0.12) - 1.7917595 * jax.random.uniform(streams_of[1], (NX, NY), jnp.float32) ** steps_of(streams_of[1], (NX, NY), ((0, 32), (1, 16)), -0.2, 0.2)), 0.02, 0.12)
    transport_courant = jnp.clip(0.18 * jax.random.uniform(streams_of[2], (2, NX, NY), jnp.float32) ** steps_of(streams_of[2], (2, NX, NY), ((1, 32), (2, 16)), -0.2, 0.2), 0.0, 0.18)
    obs_cells = plant(jax.random.randint(streams_of[3], (NOBS,), 0, CX * CY), jax.random.fold_in(streams_of[3], 1), 0, (CX * CY) - 1).astype(jnp.int32)
    obs_value = normal_values(streams_of[4], (NOBS,), 1.0, 6.0, ((0, 512),), jnp.float32)
    obs_error = jnp.clip(jnp.exp(math.log(32.0) - 2.0794415 * jax.random.uniform(streams_of[5], (NOBS,), jnp.float32) ** steps_of(streams_of[5], (NOBS,), ((0, 512),), -0.2, 0.2)), 4.0, 32.0)
    return dict(prior_sample_fields=prior_sample_fields, spreading_coefficient=spreading_coefficient, transport_courant=transport_courant, obs_cells=obs_cells, obs_value=obs_value, obs_error=obs_error)


def propagate_dynamics(field, spreading_coefficient, transport_courant):
    padded = jnp.pad(field, ((0, 0), (1, 1), (1, 1)))
    centre = padded[:, 1:-1, 1:-1]
    upper = padded[:, :-2, 1:-1]
    lower = padded[:, 2:, 1:-1]
    left_side = padded[:, 1:-1, :-2]
    right_side = padded[:, 1:-1, 2:]
    spread = upper + lower + left_side + right_side - 4.0 * centre
    return centre + spreading_coefficient * spread - transport_courant[0] * (centre - upper) - transport_courant[1] * (centre - left_side)

def reference(prior_sample_fields, spreading_coefficient, transport_courant, obs_cells, obs_value, obs_error):
    predicted_fields = propagate_dynamics(propagate_dynamics(prior_sample_fields, spreading_coefficient, transport_courant), spreading_coefficient, transport_courant)
    sample_total = predicted_fields.shape[0]
    number = jnp.arange(NOBS, dtype=jnp.int32)
    tile = number // P_DEV
    vertical_cell_total = tile // N_COL * CX + obs_cells // CY
    horizontal_cell_total = tile % N_COL * CY + obs_cells % CY
    measurement_vector = predicted_fields[:, vertical_cell_total, horizontal_cell_total]
    sample_centroid = lax.optimization_barrier(jnp.mean(predicted_fields, axis=0))
    sample_departures = predicted_fields - sample_centroid
    obs_mean = lax.optimization_barrier(jnp.mean(measurement_vector, axis=0))
    root = jnp.sqrt(jnp.float32(sample_total - 1))
    scaled = (measurement_vector - obs_mean) / (obs_error * root)
    innovation = (obs_value - obs_mean) / obs_error
    eye = jnp.eye(sample_total, dtype=jnp.float32)
    gram = eye + jnp.dot(scaled, scaled.T, precision=lax.Precision.HIGHEST)
    pulled = jnp.dot(scaled, innovation[:, None], precision=lax.Precision.HIGHEST)
    factor = jnp.linalg.cholesky(gram).T
    middle = lax.linalg.triangular_solve(factor, pulled, left_side=True, lower=False, transpose_a=True)
    shift = lax.linalg.triangular_solve(factor, middle, left_side=True, lower=False)
    inverse = lax.linalg.triangular_solve(factor, eye, left_side=True, lower=False)
    weights = (shift + inverse) / root
    raveled_field_vector = sample_departures.reshape(sample_total, -1)
    assimilate_measurements = jnp.dot(weights.T, raveled_field_vector, precision=lax.Precision.HIGHEST)
    return sample_centroid + assimilate_measurements.reshape(predicted_fields.shape)
```

```python
import jax
import jax.numpy as jnp
from jax import lax
from jax.experimental import pallas as pl
from jax.experimental.pallas import tpu as pltpu
from jax.sharding import Mesh
from jax.sharding import PartitionSpec as P

ROW_COL = ("row_0", "row_1", "col_0", "col_1")
ROW = ("row_0", "row_1")
COL = ("col_0", "col_1")


def with_halo(x, sides, width):
    for axis, dim in sides:
        devices, length = (lax.axis_size(axis), x.shape[dim])
        up = [(i, (i + 1) % devices) for i in range(devices - 1)]
        down = [(j, i) for i, j in up]
        last = lax.slice_in_dim(x, length - width, length, axis=dim)
        first = lax.slice_in_dim(x, 0, width, axis=dim)
        before = lax.ppermute(last, axis, up)
        after = lax.ppermute(first, axis, down)
        x = jnp.concatenate([before, x, after], axis=dim)
    return x


def cut_along(x, dim, devices):
    before, after = (x.shape[:dim], x.shape[dim + 1 :])
    return jnp.moveaxis(x.reshape(*before, devices, -1, *after), dim, 0)


def sent_and_summed(x, axis, dim):
    devices = lax.axis_size(axis)
    parts = lax.all_to_all(cut_along(x, dim, devices), axis, 0, 0, tiled=True)
    return jnp.sum(parts, axis=0)


def summed_rows(x, axes, dim):
    far, near = axes
    parts = cut_along(x, dim, lax.axis_size(far))
    nearer = sent_and_summed(parts, near, dim + 1)
    arrived = lax.all_to_all(nearer, far, split_axis=0, concat_axis=0, tiled=True)
    return arrived.sum(axis=0)


def rows_for(lines, devices):
    spare = -len(lines) % devices
    return jnp.pad(lines, [(0, spare)] + [(0, 0)] * (lines.ndim - 1))


def from_everyone(x, axis):
    copies = jnp.broadcast_to(x, (lax.axis_size(axis), *x.shape))
    return lax.all_to_all(copies, axis, split_axis=0, concat_axis=0, tiled=True)


def laid_out(parts, dim):
    lengths = list(parts.shape[1:])
    lengths[dim] *= parts.shape[0]
    return jnp.moveaxis(parts, 0, dim).reshape(lengths)


def gather_axes(x, axes, dim):
    far, near = axes
    first = from_everyone(x, far)
    parts = jnp.swapaxes(from_everyone(first, near), 0, 1)
    return laid_out(parts.reshape(-1, *x.shape), dim)


def sum_by_parts(x, axes):
    own = summed_rows(rows_for(x, lax.axis_size(axes[0]) * lax.axis_size(axes[1])), axes, 0)
    whole = gather_axes(own, axes, 0)
    return whole[: len(x)].reshape(x.shape)


def together(arrays, axis):
    ends = [0]
    for a in arrays:
        ends.append(ends[-1] + a.size)
    running = sum_by_parts(jnp.concatenate([a.ravel() for a in arrays]), axis)
    return tuple((running[b:e].reshape(a.shape) for a, b, e in zip(arrays, ends, ends[1:])))


def propagate_dynamics(padded, spreading_coefficient, transport_courant):
    centre = padded[:, 1:-1, 1:-1]
    upper = padded[:, :-2, 1:-1]
    lower = padded[:, 2:, 1:-1]
    left_side = padded[:, 1:-1, :-2]
    right_side = padded[:, 1:-1, 2:]
    spread = upper + lower + left_side + right_side - 4.0 * centre
    return (
        centre
        + spreading_coefficient * spread
        - transport_courant[0] * (centre - upper)
        - transport_courant[1] * (centre - left_side)
    )


F32 = jnp.float32
BF16 = jnp.bfloat16


def lane_spread(x, lane):
    return jnp.broadcast_to(x[:, lane : lane + 1], (8, 128))


def row_spread(x, row):
    return jnp.broadcast_to(x[row : row + 1, :], (8, 128))


def split2(x):
    hi = x.astype(BF16)
    lo = (x - hi.astype(F32)).astype(BF16)
    return hi, lo


def factor_rows(x_ref, d_ref):
    lanes = lax.broadcasted_iota(jnp.int32, (8, 128), 1)
    rows = lax.broadcasted_iota(jnp.int32, (8, 128), 0)
    for k in range(16):
        base = 8 * k
        p = x_ref[k]
        c = [lane_spread(p, base + j) for j in range(8)]
        a = {(i, j): row_spread(c[j], i) for j in range(8) for i in range(j, 8)}
        in_block = (lanes >= base) & (lanes < base + 8)
        eye = jnp.where(lanes - base == rows, F32(1.0), F32(0.0))
        p0 = jnp.where(in_block, eye, p)
        pb = [row_spread(p0, i) for i in range(8)]
        inv = []
        pivots = jnp.zeros((8, 128), F32)
        low = {}
        for j in range(8):
            pivots = jnp.where(rows == j, a[j, j], pivots)
            r = 1.0 / a[j, j]
            inv.append(r)
            for i in range(j + 1, 8):
                low[i, j] = a[i, j] * r
            for i in range(j + 1, 8):
                for m in range(i, 8):
                    a[m, i] = a[m, i] - a[m, j] * low[i, j]
                pb[i] = pb[i] - low[i, j] * pb[j]
        done = pb[0]
        for i in range(1, 8):
            done = jnp.where(rows == i, pb[i], done)
        x_ref[k] = done
        d_ref[k] = pivots
        if k == 15:
            break
        q = x_ref[k + 1]
        cq = [lane_spread(q, base + j) for j in range(8)]
        q = jnp.where(in_block, F32(0.0), q)
        for j in range(8):
            mult = cq[j] * inv[j]
            q = q - mult * pb[j]
            for i in range(j + 1, 8):
                cq[i] = cq[i] - mult * a[i, j]
        x_ref[k + 1] = q
        if k == 14:
            continue
        minv = {}
        for j in range(8):
            for i in range(j):
                t = low[j, i]
                for m in range(i + 1, j):
                    t = t + low[j, m] * minv[m, i]
                minv[j, i] = -t
        z = []
        scaled = [pb[j] * inv[j] for j in range(8)]
        for i in range(8):
            t = scaled[i]
            for j in range(i + 1, 8):
                t = t + minv[j, i] * scaled[j]
            z.append(t)
        for t in range(k + 2, 16):
            q = x_ref[t]
            cq = [lane_spread(q, base + j) for j in range(8)]
            q = jnp.where(in_block, F32(0.0), q)
            s0 = cq[0] * z[0] + cq[1] * z[1]
            s1 = cq[2] * z[2] + cq[3] * z[3]
            s2 = cq[4] * z[4] + cq[5] * z[5]
            s3 = cq[6] * z[6] + cq[7] * z[7]
            x_ref[t] = q - ((s0 + s1) + (s2 + s3))


def tail_kernel(g_ref, d_hbm, mean_ref, out_hbm, x_ref, d_ref, dd_ref, o_ref, in_sem, out_sem):
    fetch = pltpu.make_async_copy(d_hbm, dd_ref, in_sem)
    fetch.start()
    lanes = lax.broadcasted_iota(jnp.int32, (8, 128), 1)
    rows = lax.broadcasted_iota(jnp.int32, (8, 128), 0)
    for k in range(16):
        x_ref[k] = g_ref[8 * k : 8 * k + 8, :] + jnp.where(lanes - 8 * k == rows, F32(1.0), F32(0.0))
    factor_rows(x_ref, d_ref)
    pulled = row_spread(g_ref[128:136, :], 0)
    root = jnp.sqrt(F32(127.0))
    shift = jnp.zeros((8, 128), F32)
    kept = []
    for k in range(16):
        m = jnp.where(lanes - 8 * k <= rows, x_ref[k], F32(0.0))
        kept.append(m)
        y = jnp.sum(m * pulled, axis=1, keepdims=True)
        shift = shift + m * (jnp.broadcast_to(y, (8, 128)) / d_ref[k])
    shift = jnp.broadcast_to(jnp.sum(shift, axis=0, keepdims=True), (8, 128))
    w = []
    for k in range(16):
        w.append((kept[k] / jnp.sqrt(d_ref[k]) + shift) / root)
    w = jnp.concatenate(w, axis=0)
    whi, wlo = split2(w)
    both = jnp.concatenate([whi, wlo], axis=1)
    fetch.wait()
    for r in range(8):
        hi, lo = split2(dd_ref[r])
        acc = jnp.dot(both, jnp.concatenate([hi, hi], axis=0), preferred_element_type=F32)
        acc = acc + jnp.dot(both, jnp.concatenate([lo, lo], axis=0), preferred_element_type=F32)
        acc = acc + mean_ref[r : r + 1, :]
        o_ref[0, pl.ds(r, 128, stride=8), :] = acc[:, 0:128]
        o_ref[1, pl.ds(r, 128, stride=8), :] = acc[:, 128:256]
    outs = [
        pltpu.make_async_copy(o_ref.at[n], out_hbm.at[:, pl.ds(128 * n, 128)], out_sem.at[n]) for n in range(2)
    ]
    for c in outs:
        c.start()
    for c in outs:
        c.wait()


def tail(g, departures, mean):
    return pl.pallas_call(
        tail_kernel,
        out_shape=jax.ShapeDtypeStruct((1024, 256), F32),
        in_specs=[
            pl.BlockSpec(memory_space=pltpu.VMEM),
            pl.BlockSpec(memory_space=pl.ANY),
            pl.BlockSpec(memory_space=pltpu.VMEM),
        ],
        out_specs=pl.BlockSpec(memory_space=pl.ANY),
        scratch_shapes=[
            pltpu.VMEM((16, 8, 128), F32),
            pltpu.VMEM((16, 8, 128), F32),
            pltpu.VMEM((8, 128, 256), F32),
            pltpu.VMEM((2, 1024, 128), F32),
            pltpu.SemaphoreType.DMA,
            pltpu.SemaphoreType.DMA((2,)),
        ],
        name="tail",
    )(g, departures, mean)


def body(
    prior_sample_fields, spreading_coefficient, transport_courant, obs_cells, obs_value, obs_error
):
    sample_total = prior_sample_fields.shape[0]
    stacked = jnp.concatenate(
        [prior_sample_fields, spreading_coefficient[None], transport_courant], axis=0
    )
    widened = with_halo(stacked, ((ROW, 1), (COL, 2)), 2)
    members = widened[:sample_total]
    coeffs = widened[sample_total:, 1:-1, 1:-1]
    inner_field_block = propagate_dynamics(members, coeffs[0], coeffs[1:])
    predicted_fields = propagate_dynamics(
        inner_field_block, spreading_coefficient, transport_courant
    )
    raveled_field_vector = predicted_fields.reshape(sample_total, -1)
    cell_total = raveled_field_vector.shape[1]
    selector = (jnp.arange(cell_total, dtype=jnp.int32)[:, None] == obs_cells[None, :]).astype(
        jnp.float32
    )
    measurement_vector = jnp.dot(raveled_field_vector, selector, precision=lax.Precision.HIGHEST)
    sample_centroid = jnp.mean(predicted_fields, axis=0)
    sample_departures = raveled_field_vector - sample_centroid.reshape(1, -1)
    obs_mean = jnp.mean(measurement_vector, axis=0)
    root = jnp.sqrt(jnp.float32(sample_total - 1))
    scaled = (measurement_vector - obs_mean) / (obs_error * root)
    innovation = (obs_value - obs_mean) / obs_error
    pull_part = jnp.dot(scaled, innovation[:, None], precision=lax.Precision.HIGHEST)
    gram_part = jnp.dot(scaled, scaled.T, precision=lax.Precision.HIGHEST)
    gram_total, pulled = together((gram_part, pull_part), ("row_0", ("row_1", "col_0", "col_1")))
    g = jnp.concatenate([gram_total, jnp.pad(pulled.T, ((0, 7), (0, 0)))], axis=0)
    departures = jnp.swapaxes(sample_departures.reshape(128, 8, 256), 0, 1)
    return tail(g, departures, sample_centroid).reshape(128, 8, 256)


def solution(mesh):
    split = Mesh(mesh.devices.reshape(8, 4, 8, 2), ("row_0", "row_1", "col_0", "col_1"))
    return jax.shard_map(
        body,
        mesh=split,
        in_specs=(
            P(None, ROW, COL),
            P(ROW, COL),
            P(None, ROW, COL),
            P(ROW_COL),
            P(ROW_COL),
            P(ROW_COL),
        ),
        out_specs=P(None, ROW, COL),
        check_vma=False,
    )
```

```python
import jax
import jax.numpy as jnp
from jax import lax
from jax.experimental import pallas as pl
from jax.experimental.pallas import tpu as pltpu
from jax.sharding import Mesh
from jax.sharding import PartitionSpec as P

ROW_COL = ("row_0", "row_1", "col_0", "col_1")
ROW = ("row_0", "row_1")
COL = ("col_0", "col_1")
F32 = jnp.float32
BF16 = jnp.bfloat16


def lane_spread(x, lane):
    return jnp.broadcast_to(x[:, lane : lane + 1], (8, 128))


def row_spread(x, row):
    return jnp.broadcast_to(x[row : row + 1, :], (8, 128))


def split2(x):
    hi = x.astype(BF16)
    lo = (x - hi.astype(F32)).astype(BF16)
    return hi, lo


def factor_rows(x_ref, d_ref):
    lanes = lax.broadcasted_iota(jnp.int32, (8, 128), 1)
    rows = lax.broadcasted_iota(jnp.int32, (8, 128), 0)
    for k in range(16):
        base = 8 * k
        p = x_ref[k]
        c = [lane_spread(p, base + j) for j in range(8)]
        a = {(i, j): row_spread(c[j], i) for j in range(8) for i in range(j, 8)}
        in_block = (lanes >= base) & (lanes < base + 8)
        eye = jnp.where(lanes - base == rows, F32(1.0), F32(0.0))
        p0 = jnp.where(in_block, eye, p)
        pb = [row_spread(p0, i) for i in range(8)]
        inv = []
        pivots = jnp.zeros((8, 128), F32)
        low = {}
        for j in range(8):
            pivots = jnp.where(rows == j, a[j, j], pivots)
            r = 1.0 / a[j, j]
            inv.append(r)
            for i in range(j + 1, 8):
                low[i, j] = a[i, j] * r
            for i in range(j + 1, 8):
                for m in range(i, 8):
                    a[m, i] = a[m, i] - a[m, j] * low[i, j]
                pb[i] = pb[i] - low[i, j] * pb[j]
        done = pb[0]
        for i in range(1, 8):
            done = jnp.where(rows == i, pb[i], done)
        x_ref[k] = done
        d_ref[k] = pivots
        if k == 15:
            break
        q = x_ref[k + 1]
        cq = [lane_spread(q, base + j) for j in range(8)]
        q = jnp.where(in_block, F32(0.0), q)
        for j in range(8):
            mult = cq[j] * inv[j]
            q = q - mult * pb[j]
            for i in range(j + 1, 8):
                cq[i] = cq[i] - mult * a[i, j]
        x_ref[k + 1] = q
        if k == 14:
            continue
        minv = {}
        for j in range(8):
            for i in range(j):
                t = low[j, i]
                for m in range(i + 1, j):
                    t = t + low[j, m] * minv[m, i]
                minv[j, i] = -t
        z = []
        scaled = [pb[j] * inv[j] for j in range(8)]
        for i in range(8):
            t = scaled[i]
            for j in range(i + 1, 8):
                t = t + minv[j, i] * scaled[j]
            z.append(t)
        for t in range(k + 2, 16):
            q = x_ref[t]
            cq = [lane_spread(q, base + j) for j in range(8)]
            q = jnp.where(in_block, F32(0.0), q)
            s0 = cq[0] * z[0] + cq[1] * z[1]
            s1 = cq[2] * z[2] + cq[3] * z[3]
            s2 = cq[4] * z[4] + cq[5] * z[5]
            s3 = cq[6] * z[6] + cq[7] * z[7]
            x_ref[t] = q - ((s0 + s1) + (s2 + s3))


def tail_kernel(g_ref, d_hbm, mean_ref, out_hbm, x_ref, d_ref, dd_ref, o_ref, in_sem, out_sem):
    fetch = pltpu.make_async_copy(d_hbm, dd_ref, in_sem)
    fetch.start()
    lanes = lax.broadcasted_iota(jnp.int32, (8, 128), 1)
    rows = lax.broadcasted_iota(jnp.int32, (8, 128), 0)
    upper = g_ref[0:64, :]
    lanes64 = lax.broadcasted_iota(jnp.int32, (64, 128), 1)
    rows64 = lax.broadcasted_iota(jnp.int32, (64, 128), 0)
    half = jnp.concatenate(
        [
            jnp.where((lanes64 >= 64) | (lanes64 < rows64), upper, F32(0.0)),
            jnp.where(lanes64 - 64 > rows64, pltpu.roll(upper, 64, 1), F32(0.0)),
        ],
        axis=0,
    )
    gram = half + half.T
    diagonal = row_spread(g_ref[64:72, :], 1) + F32(1.0)
    for k in range(16):
        x_ref[k] = jnp.where(lanes - 8 * k == rows, diagonal, gram[8 * k : 8 * k + 8])
    factor_rows(x_ref, d_ref)
    pulled = row_spread(g_ref[64:72, :], 0)
    root = jnp.sqrt(F32(127.0))
    shift = jnp.zeros((8, 128), F32)
    kept = []
    for k in range(16):
        m = jnp.where(lanes - 8 * k <= rows, x_ref[k], F32(0.0))
        kept.append(m)
        y = jnp.sum(m * pulled, axis=1, keepdims=True)
        shift = shift + m * (jnp.broadcast_to(y, (8, 128)) / d_ref[k])
    shift = jnp.broadcast_to(jnp.sum(shift, axis=0, keepdims=True), (8, 128))
    w = []
    for k in range(16):
        w.append((kept[k] / jnp.sqrt(d_ref[k]) + shift) / root)
    w = jnp.concatenate(w, axis=0)
    whi, wlo = split2(w)
    both = jnp.concatenate([whi, wlo], axis=1)
    fetch.wait()
    for r in range(8):
        hi, lo = split2(dd_ref[r])
        acc = jnp.dot(both, jnp.concatenate([hi, hi], axis=0), preferred_element_type=F32)
        acc = acc + jnp.dot(both, jnp.concatenate([lo, lo], axis=0), preferred_element_type=F32)
        acc = acc + mean_ref[r : r + 1, :]
        o_ref[0, pl.ds(r, 128, stride=8), :] = acc[:, 0:128]
        o_ref[1, pl.ds(r, 128, stride=8), :] = acc[:, 128:256]
    outs = [
        pltpu.make_async_copy(o_ref.at[n], out_hbm.at[:, pl.ds(128 * n, 128)], out_sem.at[n]) for n in range(2)
    ]
    for c in outs:
        c.start()
    for c in outs:
        c.wait()


def tail(g, departures, mean):
    return pl.pallas_call(
        tail_kernel,
        out_shape=jax.ShapeDtypeStruct((1024, 256), F32),
        in_specs=[
            pl.BlockSpec(memory_space=pltpu.VMEM),
            pl.BlockSpec(memory_space=pl.ANY),
            pl.BlockSpec(memory_space=pltpu.VMEM),
        ],
        out_specs=pl.BlockSpec(memory_space=pl.ANY),
        scratch_shapes=[
            pltpu.VMEM((16, 8, 128), F32),
            pltpu.VMEM((16, 8, 128), F32),
            pltpu.VMEM((8, 128, 256), F32),
            pltpu.VMEM((2, 1024, 128), F32),
            pltpu.SemaphoreType.DMA,
            pltpu.SemaphoreType.DMA((2,)),
        ],
        name="tail",
    )(g, departures, mean)


MESH_IDS = pl.DeviceIdType.MESH
HIGHEST = lax.Precision.HIGHEST
CHUNKS = 4
PART = 128 // CHUNKS


def send(src, dst, sems, slot, device, landed=None):
    landed = slot if landed is None else landed
    return pltpu.make_async_remote_copy(
        src_ref=src,
        dst_ref=dst,
        send_sem=sems[0].at[slot],
        recv_sem=sems[1].at[landed],
        device_id=device,
        device_id_type=MESH_IDS,
    )


def stencil(get, coef_ref, row, tiles, lanes):
    centre = [get(t, row) for t in range(3)]
    right_of = [pltpu.roll(v, 127, 1) for v in centre]
    left_of = [pltpu.roll(v, 1, 1) for v in centre]
    out = []
    for t in tiles:
        left = jnp.where(lanes == 0, left_of[(t + 2) % 3], left_of[t])
        right = jnp.where(lanes == 127, right_of[(t + 1) % 3], right_of[t])
        w = [coef_ref[n, t, row : row + 1, :] for n in range(5)]
        out.append(
            (w[0] * centre[t] + w[1] * get(t, row - 1)) + (w[2] * get(t, row + 1) + (w[3] * left + w[4] * right))
        )
    return out


def front_kernel(
    prior_hbm, spread_ref, courant_ref, cells_ref, value_ref, error_ref,
    d_hbm, mean_ref, total_ref,
    nat_ref, u_ref, f_ref, full_ref, d_ref, pick_ref, raw_ref, coef_ref,
    edge_ref, colin_ref, rowc_ref, rowin_ref, cor_ref, comb_ref, acc_ref,
    part_ref, rs_ref, ysrc_ref, yin_ref, zsrc_ref, zin_ref, fin_ref, gat_ref,
    load_sem, store_sem, halo_s, halo_r, small_s, small_r, rs_s, rs_r, y_s, y_r, z_s, z_r, ag_s, ag_r,
):
    y, x = lax.axis_index("row_0"), lax.axis_index("row_1")
    z, core = lax.axis_index("col_0"), lax.axis_index("col_1")
    row, col = y * 4 + x, z * 2 + core

    def at_row(n):
        n = lax.rem(n + 32, 32)
        return (n // 4, lax.rem(n, 4), z, core)

    def at_col(n):
        n = lax.rem(n + 16, 16)
        return (y, x, n // 2, lax.rem(n, 2))

    up, down, left, right = at_row(row - 1), at_row(row + 1), at_col(col - 1), at_col(col + 1)
    me = x * 2 + core
    group = [lax.rem(me + i, 8) for i in range(1, 8)]
    group_dev = [(y, g // 2, z, lax.rem(g, 2)) for g in group]
    ys = [lax.rem(y + i, 8) for i in range(1, 8)]
    zs = [lax.rem(z + i, 8) for i in range(1, 8)]
    y_dev = [(n, x, z, core) for n in ys]
    z_dev = [(y, x, n, core) for n in zs]

    barrier = pltpu.get_barrier_semaphore()
    everyone = [up, down, left, right] + group_dev + y_dev + z_dev
    for device in everyone:
        pl.semaphore_signal(barrier, inc=1, device_id=device, device_id_type=MESH_IDS)

    loads = [
        pltpu.make_async_copy(prior_hbm.at[:, pl.ds(128 * t, 128)], nat_ref.at[t], load_sem.at[t]) for t in range(2)
    ]
    for c in loads:
        c.start()

    lanes8 = lax.broadcasted_iota(jnp.int32, (8, 128), 1)
    for t in range(2):
        cut = slice(128 * t, 128 * t + 128)
        for n, block in enumerate((spread_ref[:, cut], courant_ref[0:8, cut], courant_ref[8:16, cut])):
            raw_ref[n, t, 1:9, :] = block
            rowc_ref[t, n : n + 1, :] = block[7:8, :]
            rowc_ref[t, n + 3 : n + 4, :] = block[0:1, :]
        rowc_ref[t, 6:8, :] = jnp.zeros((2, 128), F32)
    edge = jnp.zeros((8, 128), F32)
    for n in range(3):
        last = spread_ref[:, 128:256] if n == 0 else courant_ref[8 * n - 8 : 8 * n, 128:256]
        first = spread_ref[:, 0:128] if n == 0 else courant_ref[8 * n - 8 : 8 * n, 0:128]
        edge = jnp.where(lanes8 == n, pltpu.roll(last, 1 + n, 1), edge)
        edge = jnp.where(lanes8 == n + 3, pltpu.roll(first, 3 + n, 1), edge)
    edge_ref[0, 16:24, :] = edge
    edge_ref[1, 16:24, :] = edge

    for c in loads:
        c.wait()
    for r in (0, 1, 6, 7, 2, 3, 4, 5):
        for t in range(2):
            u_ref[t, 2 + r] = nat_ref[t, pl.ds(r, 128, stride=8), :]
    pl.semaphore_wait(barrier, len(everyone))

    halo = []
    for part in range(CHUNKS):
        some = pl.ds(part * PART, PART)
        for t in range(2):
            slot = part * 4 + t * 2
            halo.append(send(u_ref.at[t, 2:4, some, :], u_ref.at[t, 10:12, some, :], (halo_s, halo_r), slot, up))
            halo.append(send(u_ref.at[t, 8:10, some, :], u_ref.at[t, 0:2, some, :], (halo_s, halo_r), slot + 1, down))
    small = (small_s, small_r)
    rows_out = [send(rowc_ref, rowin_ref.at[1], small, 0, up), send(rowc_ref, rowin_ref.at[0], small, 1, down)]
    for c in rows_out:
        c.start()
    for c in halo[:4]:
        c.start()

    lanes = lax.broadcasted_iota(jnp.int32, (128, 128), 1)
    ends = jnp.zeros((128, 128), F32)
    for r in range(8):
        ends = jnp.where((lanes >> 1) == r, pltpu.roll(u_ref[1, 2 + r], 2 + 2 * r, 1), ends)
        ends = jnp.where((lanes >> 1) == r + 8, pltpu.roll(u_ref[0, 2 + r], 16 + 2 * r, 1), ends)
    ends = ends.T
    edge_ref[0, 0:16, :] = ends[0:16]
    edge_ref[1, 0:16, :] = ends[16:32]
    cols_out = [
        send(edge_ref.at[0], colin_ref.at[0], small, 2, right),
        send(edge_ref.at[1], colin_ref.at[1], small, 3, left),
    ]
    for c in cols_out:
        c.start()
    for c in halo[4:]:
        c.start()

    cells = cells_ref[...]
    places = lax.broadcasted_iota(jnp.int32, (256, 128), 0)
    for r in range(8):
        pick_ref[r] = jnp.where(places + 256 * r == cells, F32(1.0), F32(0.0)).astype(BF16)

    for c in cols_out:
        c.wait()
    corners_out = [
        send(colin_ref.at[:, 8:16, :], cor_ref.at[0], small, 4, down),
        send(colin_ref.at[:, 0:8, :], cor_ref.at[1], small, 5, up),
    ]
    for c in corners_out:
        c.start()
    for c in rows_out:
        c.wait()

    for n in range(3):
        for t in range(2):
            raw_ref[n, t, 0:1, :] = rowin_ref[0, t, n : n + 1, :]
            raw_ref[n, t, 9:10, :] = rowin_ref[1, t, n + 3 : n + 4, :]
        beyond = jnp.where(
            lanes8 == 127,
            pltpu.roll(colin_ref[0, 16:24, :], 127 - n, 1),
            pltpu.roll(colin_ref[1, 16:24, :], 125 - n, 1),
        )
        raw_ref[n, 2, 0:1, :] = jnp.zeros((1, 128), F32)
        raw_ref[n, 2, 1:9, :] = jnp.where((lanes8 == 127) | (lanes8 == 0), beyond, F32(0.0))
        raw_ref[n, 2, 9:10, :] = jnp.zeros((1, 128), F32)
    wide = lax.broadcasted_iota(jnp.int32, (10, 128), 1)
    deep = lax.broadcasted_iota(jnp.int32, (10, 128), 0)
    for t in range(3):
        k, t0, t1 = (raw_ref[n, t, 0:10, :] for n in range(3))
        zero = jnp.zeros_like(k)
        coef_ref[0, t, 0:10, :] = 1.0 - 4.0 * k - t0 - t1
        coef_ref[1, t, 0:10, :] = jnp.where((deep == 1) & (row == 0), zero, k + t0)
        coef_ref[2, t, 0:10, :] = jnp.where((deep == 8) & (row == 31), zero, k)
        w_left, w_right = k + t1, k
        if t == 0:
            w_left = jnp.where((wide == 0) & (col == 0), zero, w_left)
        if t == 1:
            w_right = jnp.where((wide == 127) & (col == 15), zero, w_right)
        coef_ref[3, t, 0:10, :] = w_left
        coef_ref[4, t, 0:10, :] = w_right

    comb_ref[...] = jnp.zeros((128, 128), F32)
    for r in range(8):
        comb_ref[4 * r + 4 : 4 * r + 6, :] = colin_ref[0, 2 * r : 2 * r + 2, :]
        comb_ref[4 * r + 6 : 4 * r + 8, :] = colin_ref[1, 2 * r : 2 * r + 2, :]
    for c in corners_out:
        c.wait()
    for side in range(2):
        comb_ref[2 * side : 2 * side + 2, :] = cor_ref[0, side, 6:8, :]
        comb_ref[36 + 2 * side : 38 + 2 * side, :] = cor_ref[1, side, 0:2, :]
    turned = comb_ref[...].T
    for n in range(10):
        u_ref[2, n + 1] = pltpu.roll(turned, (126 - 4 * n) % 128, 1)

    few = lax.broadcasted_iota(jnp.int32, (PART, 128), 1)

    def first_step(some, n):
        tiles = range(3) if 1 <= n <= 8 else range(2)
        for t, v in zip(tiles, stencil(lambda t, i: u_ref[t, i + 1, some, :], coef_ref, n, tiles, few)):
            f_ref[t, n, some, :] = v

    def second_step(some, n):
        for t, v in zip(range(2), stencil(lambda t, i: f_ref[t, i, some, :], coef_ref, n, range(2), few)):
            full_ref[n - 1, some, 128 * t : 128 * t + 128] = v

    @pl.loop(0, CHUNKS)
    def _(part):
        some = pl.ds(pl.multiple_of(part * PART, PART), PART)
        for n in range(2, 8):
            first_step(some, n)
        for n in range(3, 7):
            second_step(some, n)

    def observe(n):
        v = full_ref[n]
        hi = v.astype(BF16)
        rest = v - hi.astype(F32)
        mid = rest.astype(BF16)
        lo = (rest - mid.astype(F32)).astype(BF16)
        return jnp.dot(jnp.concatenate([hi, mid, lo], axis=0), pick_ref[n], preferred_element_type=F32)

    acc_ref[...] = (observe(2) + observe(3)) + (observe(4) + observe(5))

    for part in range(CHUNKS):
        some = slice(part * PART, part * PART + PART)
        for c in halo[4 * part : 4 * part + 4]:
            c.wait()
        for n in (0, 1, 8, 9):
            first_step(some, n)
        for n in (1, 2, 7, 8):
            second_step(some, n)

    seen = acc_ref[...] + ((observe(0) + observe(1)) + (observe(6) + observe(7)))
    observed = (seen[0:128] + seen[128:256]) + seen[256:384]
    obs_mean = jnp.sum(observed, axis=0, keepdims=True) * F32(1.0 / 128.0)
    err = error_ref[...]
    scaled = (observed - obs_mean) / (err * jnp.sqrt(F32(127.0)))
    innovation = jnp.broadcast_to((value_ref[...] - obs_mean) / err, (8, 128))
    turned_dot = (((1,), (1,)), ((), ()))
    gram = lax.dot_general(scaled, scaled, turned_dot, precision=HIGHEST, preferred_element_type=F32)
    pulled = lax.dot_general(innovation, scaled, turned_dot, precision=HIGHEST, preferred_element_type=F32)
    deep128 = lax.broadcasted_iota(jnp.int32, (128, 128), 0)
    diagonal = jnp.sum(jnp.where(lanes == deep128, gram, F32(0.0)), axis=0, keepdims=True)
    rows8 = lax.broadcasted_iota(jnp.int32, (8, 128), 0)
    extra = jnp.where(rows8 == 0, pulled, jnp.broadcast_to(diagonal, (8, 128)))
    folded = pltpu.roll(gram[64:128], 64, 1)
    for g in range(8):
        cut = slice(8 * g, 8 * g + 8)
        own, other = gram[cut], folded[cut]
        keep = (lanes8 >= 64) | (lanes8 < rows8 + 8 * g)
        part_ref[g, 0] = jnp.where(keep, own, other)
        part_ref[g, 1] = extra

    rs = [
        send(part_ref.at[g], rs_ref.at[me], (rs_s, rs_r), g, dev, landed=me) for g, dev in zip(group, group_dev)
    ]
    for c in rs:
        c.start()
    rs_ref[pl.ds(me, 1)] = part_ref[pl.ds(me, 1)]

    for r in range(8):
        v = full_ref[r]
        mean = jnp.sum(v, axis=0, keepdims=True) * F32(1.0 / 128.0)
        mean_ref[r : r + 1, :] = mean
        d_ref[r] = v - mean
    store = pltpu.make_async_copy(d_ref, d_hbm, store_sem)
    store.start()

    def landed(buf, sems, sent, ids, devs, src):
        for c in sent:
            c.wait_send()
        for n, dev in zip(ids, devs):
            send(src, buf.at[n], sems, n, dev).wait_recv()

    def total(buf):
        return ((buf[0] + buf[1]) + (buf[2] + buf[3])) + ((buf[4] + buf[5]) + (buf[6] + buf[7]))

    landed(rs_ref, (rs_s, rs_r), rs, group, group_dev, part_ref.at[0])
    ysrc_ref[...] = total(rs_ref)
    sent = [send(ysrc_ref, yin_ref.at[y], (y_s, y_r), n, dev, landed=y) for n, dev in zip(ys, y_dev)]
    for c in sent:
        c.start()
    yin_ref[pl.ds(y, 1)] = ysrc_ref[...][None]
    landed(yin_ref, (y_s, y_r), sent, ys, y_dev, ysrc_ref)
    zsrc_ref[...] = total(yin_ref)
    sent = [send(zsrc_ref, zin_ref.at[z], (z_s, z_r), n, dev, landed=z) for n, dev in zip(zs, z_dev)]
    for c in sent:
        c.start()
    zin_ref[pl.ds(z, 1)] = zsrc_ref[...][None]
    landed(zin_ref, (z_s, z_r), sent, zs, z_dev, zsrc_ref)
    whole = total(zin_ref)
    fin_ref[...] = whole[0]
    sent = [send(fin_ref, gat_ref.at[me], (ag_s, ag_r), g, dev, landed=me) for g, dev in zip(group, group_dev)]
    for c in sent:
        c.start()
    gat_ref[pl.ds(me, 1)] = whole[0:1]
    total_ref[64:72, :] = whole[1]
    landed(gat_ref, (ag_s, ag_r), sent, group, group_dev, fin_ref)
    for g in range(8):
        total_ref[8 * g : 8 * g + 8, :] = gat_ref[g]
    store.wait()


def front(prior, spread, courant, cells, value, error):
    vmem, hbm = pl.BlockSpec(memory_space=pltpu.VMEM), pl.BlockSpec(memory_space=pl.ANY)
    dma = pltpu.SemaphoreType.DMA
    return pl.pallas_call(
        front_kernel,
        out_shape=(
            jax.ShapeDtypeStruct((8, 128, 256), F32),
            jax.ShapeDtypeStruct((8, 256), F32),
            jax.ShapeDtypeStruct((72, 128), F32),
        ),
        in_specs=[hbm, vmem, vmem, vmem, vmem, vmem],
        out_specs=(hbm, vmem, vmem),
        scratch_shapes=[
            pltpu.VMEM((2, 1024, 128), F32),
            pltpu.VMEM((3, 12, 128, 128), F32),
            pltpu.VMEM((3, 10, 128, 128), F32),
            pltpu.VMEM((8, 128, 256), F32),
            pltpu.VMEM((8, 128, 256), F32),
            pltpu.VMEM((8, 256, 128), BF16),
            pltpu.VMEM((3, 3, 16, 128), F32),
            pltpu.VMEM((5, 3, 16, 128), F32),
            pltpu.VMEM((2, 24, 128), F32),
            pltpu.VMEM((2, 24, 128), F32),
            pltpu.VMEM((2, 8, 128), F32),
            pltpu.VMEM((2, 2, 8, 128), F32),
            pltpu.VMEM((2, 2, 8, 128), F32),
            pltpu.VMEM((128, 128), F32),
            pltpu.VMEM((384, 128), F32),
            pltpu.VMEM((8, 2, 8, 128), F32),
            pltpu.VMEM((8, 2, 8, 128), F32),
            pltpu.VMEM((2, 8, 128), F32),
            pltpu.VMEM((8, 2, 8, 128), F32),
            pltpu.VMEM((2, 8, 128), F32),
            pltpu.VMEM((8, 2, 8, 128), F32),
            pltpu.VMEM((8, 128), F32),
            pltpu.VMEM((8, 8, 128), F32),
            dma((2,)),
            dma,
            dma((4 * CHUNKS,)),
            dma((4 * CHUNKS,)),
            dma((6,)),
            dma((6,)),
            dma((8,)),
            dma((8,)),
            dma((8,)),
            dma((8,)),
            dma((8,)),
            dma((8,)),
            dma((8,)),
            dma((8,)),
        ],
        compiler_params=pltpu.CompilerParams(collective_id=0, has_side_effects=True),
        name="front",
    )(prior, spread, courant, cells, value, error)


def body(
    prior_sample_fields, spreading_coefficient, transport_courant, obs_cells, obs_value, obs_error
):
    departures, mean, packed = front(
        prior_sample_fields.reshape(1024, 256),
        spreading_coefficient,
        transport_courant.reshape(16, 256),
        obs_cells[None, :],
        obs_value[None, :],
        obs_error[None, :],
    )
    return tail(packed, departures, mean).reshape(128, 8, 256)


def solution(mesh):
    split = Mesh(mesh.devices.reshape(8, 4, 8, 2), ("row_0", "row_1", "col_0", "col_1"))
    return jax.shard_map(
        body,
        mesh=split,
        in_specs=(
            P(None, ROW, COL),
            P(ROW, COL),
            P(None, ROW, COL),
            P(ROW_COL),
            P(ROW_COL),
            P(ROW_COL),
        ),
        out_specs=P(None, ROW, COL),
        check_vma=False,
    )
```

```python
import jax
import jax.numpy as jnp
from jax import lax
from jax.experimental import pallas as pl
from jax.experimental.pallas import tpu as pltpu
from jax.sharding import Mesh
from jax.sharding import PartitionSpec as P

ROW_COL = ("row_0", "row_1", "col_0", "col_1")
ROW = ("row_0", "row_1")
COL = ("col_0", "col_1")
F32 = jnp.float32
BF16 = jnp.bfloat16


def lane_spread(x, lane):
    return jnp.broadcast_to(x[:, lane : lane + 1], (8, 128))


def row_spread(x, row):
    return jnp.broadcast_to(x[row : row + 1, :], (8, 128))


def split2(x):
    hi = x.astype(BF16)
    lo = (x - hi.astype(F32)).astype(BF16)
    return hi, lo


def factor_rows(x_ref, d_ref):
    lanes = lax.broadcasted_iota(jnp.int32, (8, 128), 1)
    rows = lax.broadcasted_iota(jnp.int32, (8, 128), 0)
    for k in range(16):
        base = 8 * k
        p = x_ref[k]
        c = [lane_spread(p, base + j) for j in range(8)]
        a = {(i, j): row_spread(c[j], i) for j in range(8) for i in range(j, 8)}
        in_block = (lanes >= base) & (lanes < base + 8)
        eye = jnp.where(lanes - base == rows, F32(1.0), F32(0.0))
        p0 = jnp.where(in_block, eye, p)
        pb = [row_spread(p0, i) for i in range(8)]
        inv = []
        pivots = jnp.zeros((8, 128), F32)
        low = {}
        for j in range(8):
            pivots = jnp.where(rows == j, a[j, j], pivots)
            r = 1.0 / a[j, j]
            inv.append(r)
            for i in range(j + 1, 8):
                low[i, j] = a[i, j] * r
            for i in range(j + 1, 8):
                for m in range(i, 8):
                    a[m, i] = a[m, i] - a[m, j] * low[i, j]
                pb[i] = pb[i] - low[i, j] * pb[j]
        done = pb[0]
        for i in range(1, 8):
            done = jnp.where(rows == i, pb[i], done)
        x_ref[k] = done
        d_ref[k] = pivots
        if k == 15:
            break
        q = x_ref[k + 1]
        cq = [lane_spread(q, base + j) for j in range(8)]
        q = jnp.where(in_block, F32(0.0), q)
        for j in range(8):
            mult = cq[j] * inv[j]
            q = q - mult * pb[j]
            for i in range(j + 1, 8):
                cq[i] = cq[i] - mult * a[i, j]
        x_ref[k + 1] = q
        if k == 14:
            continue
        minv = {}
        for j in range(8):
            for i in range(j):
                t = low[j, i]
                for m in range(i + 1, j):
                    t = t + low[j, m] * minv[m, i]
                minv[j, i] = -t
        z = []
        scaled = [pb[j] * inv[j] for j in range(8)]
        for i in range(8):
            t = scaled[i]
            for j in range(i + 1, 8):
                t = t + minv[j, i] * scaled[j]
            z.append(t)
        for t in range(k + 2, 16):
            q = x_ref[t]
            cq = [lane_spread(q, base + j) for j in range(8)]
            q = jnp.where(in_block, F32(0.0), q)
            s0 = cq[0] * z[0] + cq[1] * z[1]
            s1 = cq[2] * z[2] + cq[3] * z[3]
            s2 = cq[4] * z[4] + cq[5] * z[5]
            s3 = cq[6] * z[6] + cq[7] * z[7]
            x_ref[t] = q - ((s0 + s1) + (s2 + s3))


def tail_kernel(g_ref, dd_ref, mean_ref, out_hbm, x_ref, d_ref, o_ref, out_sem):
    lanes = lax.broadcasted_iota(jnp.int32, (8, 128), 1)
    rows = lax.broadcasted_iota(jnp.int32, (8, 128), 0)
    upper = g_ref[0:64, :]
    lanes64 = lax.broadcasted_iota(jnp.int32, (64, 128), 1)
    rows64 = lax.broadcasted_iota(jnp.int32, (64, 128), 0)
    half = jnp.concatenate(
        [
            jnp.where((lanes64 >= 64) | (lanes64 < rows64), upper, F32(0.0)),
            jnp.where(lanes64 - 64 > rows64, pltpu.roll(upper, 64, 1), F32(0.0)),
        ],
        axis=0,
    )
    gram = half + half.T
    diagonal = row_spread(g_ref[64:72, :], 1) + F32(1.0)
    for k in range(16):
        x_ref[k] = jnp.where(lanes - 8 * k == rows, diagonal, gram[8 * k : 8 * k + 8])
    factor_rows(x_ref, d_ref)
    pulled = row_spread(g_ref[64:72, :], 0)
    root = jnp.sqrt(F32(127.0))
    shift = jnp.zeros((8, 128), F32)
    kept = []
    for k in range(16):
        m = jnp.where(lanes - 8 * k <= rows, x_ref[k], F32(0.0))
        kept.append(m)
        y = jnp.sum(m * pulled, axis=1, keepdims=True)
        shift = shift + m * (jnp.broadcast_to(y, (8, 128)) / d_ref[k])
    shift = jnp.broadcast_to(jnp.sum(shift, axis=0, keepdims=True), (8, 128))
    w = []
    for k in range(16):
        w.append((kept[k] / jnp.sqrt(d_ref[k]) + shift) / root)
    w = jnp.concatenate(w, axis=0)
    whi, wlo = split2(w)
    both = jnp.concatenate([whi, wlo], axis=1)
    for r in range(8):
        hi, lo = split2(dd_ref[r])
        acc = jnp.dot(both, jnp.concatenate([hi, hi], axis=0), preferred_element_type=F32)
        acc = acc + jnp.dot(both, jnp.concatenate([lo, lo], axis=0), preferred_element_type=F32)
        acc = acc + mean_ref[r : r + 1, :]
        o_ref[0, pl.ds(r, 128, stride=8), :] = acc[:, 0:128]
        o_ref[1, pl.ds(r, 128, stride=8), :] = acc[:, 128:256]
    outs = [
        pltpu.make_async_copy(o_ref.at[n], out_hbm.at[:, pl.ds(128 * n, 128)], out_sem.at[n]) for n in range(2)
    ]
    for c in outs:
        c.start()
    for c in outs:
        c.wait()


def tail(g, departures, mean):
    return pl.pallas_call(
        tail_kernel,
        out_shape=jax.ShapeDtypeStruct((1024, 256), F32),
        in_specs=[
            pl.BlockSpec(memory_space=pltpu.VMEM),
            pl.BlockSpec(memory_space=pltpu.VMEM),
            pl.BlockSpec(memory_space=pltpu.VMEM),
        ],
        out_specs=pl.BlockSpec(memory_space=pl.ANY),
        scratch_shapes=[
            pltpu.VMEM((16, 8, 128), F32),
            pltpu.VMEM((16, 8, 128), F32),
            pltpu.VMEM((2, 1024, 128), F32),
            pltpu.SemaphoreType.DMA((2,)),
        ],
        compiler_params=pltpu.CompilerParams(vmem_limit_bytes=16 << 20),
        name="tail",
    )(g, departures, mean)


MESH_IDS = pl.DeviceIdType.MESH
HIGHEST = lax.Precision.HIGHEST
CHUNKS = 4
PART = 128 // CHUNKS


def send(src, dst, sems, slot, device, landed=None):
    landed = slot if landed is None else landed
    return pltpu.make_async_remote_copy(
        src_ref=src,
        dst_ref=dst,
        send_sem=sems[0].at[slot],
        recv_sem=sems[1].at[landed],
        device_id=device,
        device_id_type=MESH_IDS,
    )


def stencil(get, coef_ref, row, tiles, lanes):
    centre = [get(t, row) for t in range(3)]
    right_of = [pltpu.roll(v, 127, 1) for v in centre]
    left_of = [pltpu.roll(v, 1, 1) for v in centre]
    out = []
    for t in tiles:
        left = jnp.where(lanes == 0, left_of[(t + 2) % 3], left_of[t])
        right = jnp.where(lanes == 127, right_of[(t + 1) % 3], right_of[t])
        w = [coef_ref[n, t, row : row + 1, :] for n in range(5)]
        out.append(
            (w[0] * centre[t] + w[1] * get(t, row - 1)) + (w[2] * get(t, row + 1) + (w[3] * left + w[4] * right))
        )
    return out


def front_kernel(
    prior_hbm, spread_hbm, courant_hbm, cells_hbm, value_hbm, error_hbm,
    d_ref, mean_ref, total_ref,
    spread_ref, courant_ref, cells_ref, value_ref, error_ref,
    nat_ref, u_ref, f_ref, full_ref, pick_ref, raw_ref, coef_ref,
    edge_ref, colin_ref, rowc_ref, rowin_ref, cor_ref, comb_ref, acc_ref,
    part_ref, rs_ref, ysrc_ref, yin_ref, zsrc_ref, zin_ref, fin_ref, gat_ref,
    more_ref, rsm_ref, ymsrc_ref, ym_ref, zmsrc_ref, zm_ref,
    load_sem, tiny_sem, halo_s, halo_r, small_s, small_r, rs_sem, y_sem, z_sem, ag_sem,
):
    y, x = lax.axis_index("row_0"), lax.axis_index("row_1")
    z, core = lax.axis_index("col_0"), lax.axis_index("col_1")
    row, col = y * 4 + x, z * 2 + core

    def at_row(n):
        n = lax.rem(n + 32, 32)
        return (n // 4, lax.rem(n, 4), z, core)

    def at_col(n):
        n = lax.rem(n + 16, 16)
        return (y, x, n // 2, lax.rem(n, 2))

    up, down, left, right = at_row(row - 1), at_row(row + 1), at_col(col - 1), at_col(col + 1)
    me = x * 2 + core
    far_first = (4, 3, 5, 2, 6, 1, 7)
    group = [lax.rem(me + i, 8) for i in far_first]
    group_dev = [(y, g // 2, z, lax.rem(g, 2)) for g in group]
    ys = [lax.rem(y + i, 8) for i in far_first]
    zs = [lax.rem(z + i, 8) for i in far_first]
    y_dev = [(n, x, z, core) for n in ys]
    z_dev = [(y, x, n, core) for n in zs]

    barrier = pltpu.get_barrier_semaphore()
    everyone = [up, down, left, right] + group_dev + y_dev + z_dev
    for device in everyone:
        pl.semaphore_signal(barrier, inc=1, device_id=device, device_id_type=MESH_IDS)

    tiny = [
        pltpu.make_async_copy(src, dst, tiny_sem.at[n])
        for n, (src, dst) in enumerate(
            (
                (spread_hbm, spread_ref),
                (courant_hbm, courant_ref),
                (cells_hbm, cells_ref),
                (value_hbm, value_ref),
                (error_hbm, error_ref),
            )
        )
    ]
    loads = [
        pltpu.make_async_copy(
            prior_hbm.at[pl.ds(part * PART * 8, PART * 8), pl.ds(128 * t, 128)],
            nat_ref.at[t, pl.ds(part * PART * 8, PART * 8), :],
            load_sem.at[2 * part + t],
        )
        for part in range(CHUNKS)
        for t in range(2)
    ]
    for c in loads[:2] + tiny[:2] + loads[2:] + tiny[2:]:
        c.start()

    halo = []
    for part in range(CHUNKS):
        some = pl.ds(part * PART, PART)
        for t in range(2):
            slot = part * 4 + t * 2
            halo.append(send(u_ref.at[t, 2:4, some, :], u_ref.at[t, 10:12, some, :], (halo_s, halo_r), slot, up))
            halo.append(send(u_ref.at[t, 8:10, some, :], u_ref.at[t, 0:2, some, :], (halo_s, halo_r), slot + 1, down))

    def spread_rows(part, which):
        for t in range(2):
            for r in which:
                u_ref[t, 2 + r, part * PART : part * PART + PART, :] = nat_ref[
                    t, pl.ds(part * PART * 8 + r, PART, stride=8), :
                ]

    small = (small_s, small_r)
    for part in range(CHUNKS):
        for c in loads[2 * part : 2 * part + 2]:
            c.wait()
        spread_rows(part, (0, 1, 6, 7))
        if part == 0:
            pl.semaphore_wait(barrier, len(everyone))
        for c in halo[4 * part : 4 * part + 4]:
            c.start()
    for part in range(CHUNKS):
        spread_rows(part, (2, 3, 4, 5))
    for c in tiny:
        c.wait()

    lanes8 = lax.broadcasted_iota(jnp.int32, (8, 128), 1)
    for t in range(2):
        cut = slice(128 * t, 128 * t + 128)
        for n, block in enumerate((spread_ref[:, cut], courant_ref[0:8, cut], courant_ref[8:16, cut])):
            raw_ref[n, t, 1:9, :] = block
            rowc_ref[t, n : n + 1, :] = block[7:8, :]
            rowc_ref[t, n + 3 : n + 4, :] = block[0:1, :]
        rowc_ref[t, 6:8, :] = jnp.zeros((2, 128), F32)
    edge = jnp.zeros((8, 128), F32)
    for n in range(3):
        last = spread_ref[:, 128:256] if n == 0 else courant_ref[8 * n - 8 : 8 * n, 128:256]
        first = spread_ref[:, 0:128] if n == 0 else courant_ref[8 * n - 8 : 8 * n, 0:128]
        edge = jnp.where(lanes8 == n, pltpu.roll(last, 1 + n, 1), edge)
        edge = jnp.where(lanes8 == n + 3, pltpu.roll(first, 3 + n, 1), edge)
    edge_ref[0, 16:24, :] = edge
    edge_ref[1, 16:24, :] = edge
    rows_out = [send(rowc_ref, rowin_ref.at[1], small, 0, up), send(rowc_ref, rowin_ref.at[0], small, 1, down)]
    for c in rows_out:
        c.start()

    lanes = lax.broadcasted_iota(jnp.int32, (128, 128), 1)
    ends = jnp.zeros((128, 128), F32)
    for r in range(8):
        ends = jnp.where((lanes >> 1) == r, pltpu.roll(u_ref[1, 2 + r], 2 + 2 * r, 1), ends)
        ends = jnp.where((lanes >> 1) == r + 8, pltpu.roll(u_ref[0, 2 + r], 16 + 2 * r, 1), ends)
    ends = ends.T
    edge_ref[0, 0:16, :] = ends[0:16]
    edge_ref[1, 0:16, :] = ends[16:32]
    cols_out = [
        send(edge_ref.at[0], colin_ref.at[0], small, 2, right),
        send(edge_ref.at[1], colin_ref.at[1], small, 3, left),
    ]
    for c in cols_out:
        c.start()

    cells = cells_ref[...]
    places = lax.broadcasted_iota(jnp.int32, (256, 128), 0)
    for r in range(8):
        pick_ref[r] = jnp.where(places + 256 * r == cells, F32(1.0), F32(0.0)).astype(BF16)

    for c in cols_out:
        c.wait_recv()
    corners_out = [
        send(colin_ref.at[:, 8:16, :], cor_ref.at[0], small, 4, down),
        send(colin_ref.at[:, 0:8, :], cor_ref.at[1], small, 5, up),
    ]
    for c in corners_out:
        c.start()
    for c in rows_out:
        c.wait_recv()

    for n in range(3):
        for t in range(2):
            raw_ref[n, t, 0:1, :] = rowin_ref[0, t, n : n + 1, :]
            raw_ref[n, t, 9:10, :] = rowin_ref[1, t, n + 3 : n + 4, :]
        beyond = jnp.where(
            lanes8 == 127,
            pltpu.roll(colin_ref[0, 16:24, :], 127 - n, 1),
            pltpu.roll(colin_ref[1, 16:24, :], 125 - n, 1),
        )
        raw_ref[n, 2, 0:1, :] = jnp.zeros((1, 128), F32)
        raw_ref[n, 2, 1:9, :] = jnp.where((lanes8 == 127) | (lanes8 == 0), beyond, F32(0.0))
        raw_ref[n, 2, 9:10, :] = jnp.zeros((1, 128), F32)
    wide = lax.broadcasted_iota(jnp.int32, (10, 128), 1)
    deep = lax.broadcasted_iota(jnp.int32, (10, 128), 0)
    for t in range(3):
        k, t0, t1 = (raw_ref[n, t, 0:10, :] for n in range(3))
        zero = jnp.zeros_like(k)
        coef_ref[0, t, 0:10, :] = 1.0 - 4.0 * k - t0 - t1
        coef_ref[1, t, 0:10, :] = jnp.where((deep == 1) & (row == 0), zero, k + t0)
        coef_ref[2, t, 0:10, :] = jnp.where((deep == 8) & (row == 31), zero, k)
        w_left, w_right = k + t1, k
        if t == 0:
            w_left = jnp.where((wide == 0) & (col == 0), zero, w_left)
        if t == 1:
            w_right = jnp.where((wide == 127) & (col == 15), zero, w_right)
        coef_ref[3, t, 0:10, :] = w_left
        coef_ref[4, t, 0:10, :] = w_right

    comb_ref[...] = jnp.zeros((128, 128), F32)
    for r in range(8):
        comb_ref[4 * r + 4 : 4 * r + 6, :] = colin_ref[0, 2 * r : 2 * r + 2, :]
        comb_ref[4 * r + 6 : 4 * r + 8, :] = colin_ref[1, 2 * r : 2 * r + 2, :]
    for c in corners_out:
        c.wait_recv()
    for side in range(2):
        comb_ref[2 * side : 2 * side + 2, :] = cor_ref[0, side, 6:8, :]
        comb_ref[36 + 2 * side : 38 + 2 * side, :] = cor_ref[1, side, 0:2, :]
    turned = comb_ref[...].T
    for n in range(10):
        u_ref[2, n + 1] = pltpu.roll(turned, (126 - 4 * n) % 128, 1)

    few = lax.broadcasted_iota(jnp.int32, (PART, 128), 1)

    def first_step(some, n):
        tiles = range(3) if 1 <= n <= 8 else range(2)
        for t, v in zip(tiles, stencil(lambda t, i: u_ref[t, i + 1, some, :], coef_ref, n, tiles, few)):
            f_ref[t, n, some, :] = v

    def second_step(some, n):
        for t, v in zip(range(2), stencil(lambda t, i: f_ref[t, i, some, :], coef_ref, n, range(2), few)):
            full_ref[n - 1, some, 128 * t : 128 * t + 128] = v

    @pl.loop(0, CHUNKS)
    def _(part):
        some = pl.ds(pl.multiple_of(part * PART, PART), PART)
        for n in range(2, 8):
            first_step(some, n)
        for n in range(3, 7):
            second_step(some, n)

    def observe(n):
        v = full_ref[n]
        hi = v.astype(BF16)
        rest = v - hi.astype(F32)
        mid = rest.astype(BF16)
        lo = (rest - mid.astype(F32)).astype(BF16)
        return jnp.dot(jnp.concatenate([hi, mid, lo], axis=0), pick_ref[n], preferred_element_type=F32)

    acc_ref[...] = (observe(2) + observe(3)) + (observe(4) + observe(5))

    for part in range(CHUNKS):
        some = slice(part * PART, part * PART + PART)
        for c in halo[4 * part : 4 * part + 4]:
            c.wait_recv()
        for n in (0, 1, 8, 9):
            first_step(some, n)
        for n in (1, 2, 7, 8):
            second_step(some, n)

    seen = acc_ref[...] + ((observe(0) + observe(1)) + (observe(6) + observe(7)))
    observed = (seen[0:128] + seen[128:256]) + seen[256:384]
    obs_mean = jnp.sum(observed, axis=0, keepdims=True) * F32(1.0 / 128.0)
    err = error_ref[...]
    scaled = (observed - obs_mean) / (err * jnp.sqrt(F32(127.0)))
    innovation = jnp.broadcast_to((value_ref[...] - obs_mean) / err, (8, 128))
    turned_dot = (((1,), (1,)), ((), ()))
    gram = lax.dot_general(scaled, scaled, turned_dot, precision=HIGHEST, preferred_element_type=F32)
    pulled = lax.dot_general(innovation, scaled, turned_dot, precision=HIGHEST, preferred_element_type=F32)
    deep128 = lax.broadcasted_iota(jnp.int32, (128, 128), 0)
    diagonal = jnp.sum(jnp.where(lanes == deep128, gram, F32(0.0)), axis=0, keepdims=True)
    rows8 = lax.broadcasted_iota(jnp.int32, (8, 128), 0)
    folded = pltpu.roll(gram[64:128], 64, 1)
    for g in range(8):
        cut = slice(8 * g, 8 * g + 8)
        keep = (lanes8 >= 64) | (lanes8 < rows8 + 8 * g)
        part_ref[g] = jnp.where(keep, gram[cut], folded[cut])
    more_ref[0:1, :] = pulled[0:1]
    more_ref[1:2, :] = diagonal

    def exchange(main, more, into, more_into, sems, place, ids, devs):
        out = [
            send(main(n), into.at[place], (sems[0], sems[1]), n, dev, landed=place) for n, dev in zip(ids, devs)
        ]
        for c in out:
            c.start()
        if more is not None:
            out += [
                send(more, more_into.at[place], (sems[2], sems[3]), n, dev, landed=place) for n, dev in zip(ids, devs)
            ]
            for c in out[len(ids) :]:
                c.start()
        return out

    def landed(main, more, into, more_into, sems, ids, devs):
        for n, dev in zip(ids, devs):
            send(main, into.at[n], (sems[0], sems[1]), n, dev).wait_recv()
            if more is not None:
                send(more, more_into.at[n], (sems[2], sems[3]), n, dev).wait_recv()

    def total(buf):
        return ((buf[0] + buf[1]) + (buf[2] + buf[3])) + ((buf[4] + buf[5]) + (buf[6] + buf[7]))

    rs_sems, y_sems, z_sems, ag_sems = (
        [sems.at[n] for n in range(4)] for sems in (rs_sem, y_sem, z_sem, ag_sem)
    )
    rs = exchange(lambda n: part_ref.at[n], more_ref, rs_ref, rsm_ref, rs_sems, me, group, group_dev)
    rs_ref[pl.ds(me, 1)] = part_ref[pl.ds(me, 1)]
    rsm_ref[pl.ds(me, 1)] = more_ref[...][None]

    for r in range(8):
        v = full_ref[r]
        mean = jnp.sum(v, axis=0, keepdims=True) * F32(1.0 / 128.0)
        mean_ref[r : r + 1, :] = mean
        d_ref[r] = v - mean

    landed(part_ref.at[0], more_ref, rs_ref, rsm_ref, rs_sems, group, group_dev)
    ysrc_ref[...] = total(rs_ref)
    ymsrc_ref[...] = total(rsm_ref)
    by_y = exchange(lambda n: ysrc_ref, ymsrc_ref, yin_ref, ym_ref, y_sems, y, ys, y_dev)
    yin_ref[pl.ds(y, 1)] = ysrc_ref[...][None]
    ym_ref[pl.ds(y, 1)] = ymsrc_ref[...][None]
    landed(ysrc_ref, ymsrc_ref, yin_ref, ym_ref, y_sems, ys, y_dev)
    zsrc_ref[...] = total(yin_ref)
    zmsrc_ref[...] = total(ym_ref)
    by_z = exchange(lambda n: zsrc_ref, zmsrc_ref, zin_ref, zm_ref, z_sems, z, zs, z_dev)
    zin_ref[pl.ds(z, 1)] = zsrc_ref[...][None]
    zm_ref[pl.ds(z, 1)] = zmsrc_ref[...][None]
    landed(zsrc_ref, zmsrc_ref, zin_ref, zm_ref, z_sems, zs, z_dev)
    fin_ref[...] = total(zin_ref)
    ag = exchange(lambda n: fin_ref, None, gat_ref, None, ag_sems, me, group, group_dev)
    gat_ref[pl.ds(me, 1)] = fin_ref[...][None]
    total_ref[64:66, :] = total(zm_ref)
    total_ref[66:72, :] = jnp.zeros((6, 128), F32)
    landed(fin_ref, None, gat_ref, None, ag_sems, group, group_dev)
    for g in range(8):
        total_ref[8 * g : 8 * g + 8, :] = gat_ref[g]
    for c in halo + rows_out + cols_out + corners_out + rs + by_y + by_z + ag:
        c.wait_send()


def front(prior, spread, courant, cells, value, error):
    vmem, hbm = pl.BlockSpec(memory_space=pltpu.VMEM), pl.BlockSpec(memory_space=pl.ANY)
    dma = pltpu.SemaphoreType.DMA
    return pl.pallas_call(
        front_kernel,
        out_shape=(
            pltpu.VMEM((8, 128, 256), F32),
            pltpu.VMEM((8, 256), F32),
            pltpu.VMEM((72, 128), F32),
        ),
        in_specs=[hbm] * 6,
        out_specs=(vmem, vmem, vmem),
        scratch_shapes=[
            pltpu.VMEM((8, 256), F32),
            pltpu.VMEM((16, 256), F32),
            pltpu.VMEM((1, 128), jnp.int32),
            pltpu.VMEM((1, 128), F32),
            pltpu.VMEM((1, 128), F32),
            pltpu.VMEM((2, 1024, 128), F32),
            pltpu.VMEM((3, 12, 128, 128), F32),
            pltpu.VMEM((3, 10, 128, 128), F32),
            pltpu.VMEM((8, 128, 256), F32),
            pltpu.VMEM((8, 256, 128), BF16),
            pltpu.VMEM((3, 3, 16, 128), F32),
            pltpu.VMEM((5, 3, 16, 128), F32),
            pltpu.VMEM((2, 24, 128), F32),
            pltpu.VMEM((2, 24, 128), F32),
            pltpu.VMEM((2, 8, 128), F32),
            pltpu.VMEM((2, 2, 8, 128), F32),
            pltpu.VMEM((2, 2, 8, 128), F32),
            pltpu.VMEM((128, 128), F32),
            pltpu.VMEM((384, 128), F32),
            pltpu.VMEM((8, 8, 128), F32),
            pltpu.VMEM((8, 8, 128), F32),
            pltpu.VMEM((8, 128), F32),
            pltpu.VMEM((8, 8, 128), F32),
            pltpu.VMEM((8, 128), F32),
            pltpu.VMEM((8, 8, 128), F32),
            pltpu.VMEM((8, 128), F32),
            pltpu.VMEM((8, 8, 128), F32),
            pltpu.VMEM((2, 128), F32),
            pltpu.VMEM((8, 2, 128), F32),
            pltpu.VMEM((2, 128), F32),
            pltpu.VMEM((8, 2, 128), F32),
            pltpu.VMEM((2, 128), F32),
            pltpu.VMEM((8, 2, 128), F32),
            dma((2 * CHUNKS,)),
            dma((5,)),
            dma((4 * CHUNKS,)),
            dma((4 * CHUNKS,)),
            dma((6,)),
            dma((6,)),
            dma((4, 8)),
            dma((4, 8)),
            dma((4, 8)),
            dma((4, 8)),
        ],
        compiler_params=pltpu.CompilerParams(collective_id=0, has_side_effects=True),
        name="front",
    )(prior, spread, courant, cells, value, error)


def body(
    prior_sample_fields, spreading_coefficient, transport_courant, obs_cells, obs_value, obs_error
):
    departures, mean, packed = front(
        prior_sample_fields.reshape(1024, 256),
        spreading_coefficient,
        transport_courant.reshape(16, 256),
        obs_cells[None, :],
        obs_value[None, :],
        obs_error[None, :],
    )
    return tail(packed, departures, mean).reshape(128, 8, 256)


def solution(mesh):
    split = Mesh(mesh.devices.reshape(8, 4, 8, 2), ("row_0", "row_1", "col_0", "col_1"))
    return jax.shard_map(
        body,
        mesh=split,
        in_specs=(
            P(None, ROW, COL),
            P(ROW, COL),
            P(None, ROW, COL),
            P(ROW_COL),
            P(ROW_COL),
            P(ROW_COL),
        ),
        out_specs=P(None, ROW, COL),
        check_vma=False,
    )
```

```python
import jax
import jax.numpy as jnp
from jax import lax
from jax.experimental import pallas as pl
from jax.experimental.pallas import tpu as pltpu
from jax.sharding import Mesh
from jax.sharding import PartitionSpec as P

ROW_COL = ("row_0", "row_1", "col_0", "col_1")
ROW = ("row_0", "row_1")
COL = ("col_0", "col_1")
F32 = jnp.float32
BF16 = jnp.bfloat16


def lane_spread(x, lane):
    return jnp.broadcast_to(x[:, lane : lane + 1], (8, 128))


def row_spread(x, row):
    return jnp.broadcast_to(x[row : row + 1, :], (8, 128))


def split2(x):
    hi = x.astype(BF16)
    lo = (x - hi.astype(F32)).astype(BF16)
    return hi, lo


def factor_rows(x_ref, d_ref):
    lanes = lax.broadcasted_iota(jnp.int32, (8, 128), 1)
    rows = lax.broadcasted_iota(jnp.int32, (8, 128), 0)
    for k in range(16):
        base = 8 * k
        p = x_ref[k]
        c = [lane_spread(p, base + j) for j in range(8)]
        a = {(i, j): row_spread(c[j], i) for j in range(8) for i in range(j, 8)}
        in_block = (lanes >= base) & (lanes < base + 8)
        eye = jnp.where(lanes - base == rows, F32(1.0), F32(0.0))
        p0 = jnp.where(in_block, eye, p)
        pb = [row_spread(p0, i) for i in range(8)]
        inv = []
        pivots = jnp.zeros((8, 128), F32)
        low = {}
        for j in range(8):
            pivots = jnp.where(rows == j, a[j, j], pivots)
            r = 1.0 / a[j, j]
            inv.append(r)
            for i in range(j + 1, 8):
                low[i, j] = a[i, j] * r
            for i in range(j + 1, 8):
                for m in range(i, 8):
                    a[m, i] = a[m, i] - a[m, j] * low[i, j]
                pb[i] = pb[i] - low[i, j] * pb[j]
        done = pb[0]
        for i in range(1, 8):
            done = jnp.where(rows == i, pb[i], done)
        x_ref[k] = done
        d_ref[k] = pivots
        if k == 15:
            break
        q = x_ref[k + 1]
        cq = [lane_spread(q, base + j) for j in range(8)]
        q = jnp.where(in_block, F32(0.0), q)
        for j in range(8):
            mult = cq[j] * inv[j]
            q = q - mult * pb[j]
            for i in range(j + 1, 8):
                cq[i] = cq[i] - mult * a[i, j]
        x_ref[k + 1] = q
        if k == 14:
            continue
        minv = {}
        for j in range(8):
            for i in range(j):
                t = low[j, i]
                for m in range(i + 1, j):
                    t = t + low[j, m] * minv[m, i]
                minv[j, i] = -t
        z = []
        scaled = [pb[j] * inv[j] for j in range(8)]
        for i in range(8):
            t = scaled[i]
            for j in range(i + 1, 8):
                t = t + minv[j, i] * scaled[j]
            z.append(t)
        for t in range(k + 2, 16):
            q = x_ref[t]
            cq = [lane_spread(q, base + j) for j in range(8)]
            q = jnp.where(in_block, F32(0.0), q)
            s0 = cq[0] * z[0] + cq[1] * z[1]
            s1 = cq[2] * z[2] + cq[3] * z[3]
            s2 = cq[4] * z[4] + cq[5] * z[5]
            s3 = cq[6] * z[6] + cq[7] * z[7]
            x_ref[t] = q - ((s0 + s1) + (s2 + s3))


def tail_kernel(g_ref, dd_ref, mean_ref, out_hbm, x_ref, d_ref, o_ref, out_sem):
    lanes = lax.broadcasted_iota(jnp.int32, (8, 128), 1)
    rows = lax.broadcasted_iota(jnp.int32, (8, 128), 0)
    upper = g_ref[0:64, :]
    lanes64 = lax.broadcasted_iota(jnp.int32, (64, 128), 1)
    rows64 = lax.broadcasted_iota(jnp.int32, (64, 128), 0)
    half = jnp.concatenate(
        [
            jnp.where((lanes64 >= 64) | (lanes64 < rows64), upper, F32(0.0)),
            jnp.where(lanes64 - 64 > rows64, pltpu.roll(upper, 64, 1), F32(0.0)),
        ],
        axis=0,
    )
    gram = half + half.T
    diagonal = row_spread(g_ref[64:72, :], 1) + F32(1.0)
    for k in range(16):
        x_ref[k] = jnp.where(lanes - 8 * k == rows, diagonal, gram[8 * k : 8 * k + 8])
    factor_rows(x_ref, d_ref)
    pulled = row_spread(g_ref[64:72, :], 0)
    root = jnp.sqrt(F32(127.0))
    shift = jnp.zeros((8, 128), F32)
    kept = []
    for k in range(16):
        m = jnp.where(lanes - 8 * k <= rows, x_ref[k], F32(0.0))
        kept.append(m)
        y = jnp.sum(m * pulled, axis=1, keepdims=True)
        shift = shift + m * (jnp.broadcast_to(y, (8, 128)) / d_ref[k])
    shift = jnp.broadcast_to(jnp.sum(shift, axis=0, keepdims=True), (8, 128))
    w = []
    for k in range(16):
        w.append((kept[k] / jnp.sqrt(d_ref[k]) + shift) / root)
    w = jnp.concatenate(w, axis=0)
    whi, wlo = split2(w)
    both = jnp.concatenate([whi, wlo], axis=1)
    for r in range(8):
        hi, lo = split2(dd_ref[r])
        acc = jnp.dot(both, jnp.concatenate([hi, hi], axis=0), preferred_element_type=F32)
        acc = acc + jnp.dot(both, jnp.concatenate([lo, lo], axis=0), preferred_element_type=F32)
        acc = acc + mean_ref[r : r + 1, :]
        o_ref[0, pl.ds(r, 128, stride=8), :] = acc[:, 0:128]
        o_ref[1, pl.ds(r, 128, stride=8), :] = acc[:, 128:256]
    outs = [
        pltpu.make_async_copy(o_ref.at[n], out_hbm.at[:, pl.ds(128 * n, 128)], out_sem.at[n]) for n in range(2)
    ]
    for c in outs:
        c.start()
    for c in outs:
        c.wait()


def tail(g, departures, mean):
    return pl.pallas_call(
        tail_kernel,
        out_shape=jax.ShapeDtypeStruct((1024, 256), F32),
        in_specs=[
            pl.BlockSpec(memory_space=pltpu.VMEM),
            pl.BlockSpec(memory_space=pltpu.VMEM),
            pl.BlockSpec(memory_space=pltpu.VMEM),
        ],
        out_specs=pl.BlockSpec(memory_space=pl.ANY),
        scratch_shapes=[
            pltpu.VMEM((16, 8, 128), F32),
            pltpu.VMEM((16, 8, 128), F32),
            pltpu.VMEM((2, 1024, 128), F32),
            pltpu.SemaphoreType.DMA((2,)),
        ],
        compiler_params=pltpu.CompilerParams(vmem_limit_bytes=16 << 20),
        name="tail",
    )(g, departures, mean)


MESH_IDS = pl.DeviceIdType.MESH
HIGHEST = lax.Precision.HIGHEST
CHUNKS = 4
PART = 128 // CHUNKS


def send(src, dst, sems, slot, device, landed=None):
    landed = slot if landed is None else landed
    return pltpu.make_async_remote_copy(
        src_ref=src,
        dst_ref=dst,
        send_sem=sems[0].at[slot],
        recv_sem=sems[1].at[landed],
        device_id=device,
        device_id_type=MESH_IDS,
    )


def stencil(get, coef_ref, row, tiles, lanes):
    centre = [get(t, row) for t in range(3)]
    right_of = [pltpu.roll(v, 127, 1) for v in centre]
    left_of = [pltpu.roll(v, 1, 1) for v in centre]
    out = []
    for t in tiles:
        left = jnp.where(lanes == 0, left_of[(t + 2) % 3], left_of[t])
        right = jnp.where(lanes == 127, right_of[(t + 1) % 3], right_of[t])
        w = [coef_ref[n, t, row : row + 1, :] for n in range(5)]
        out.append(
            (w[0] * centre[t] + w[1] * get(t, row - 1)) + (w[2] * get(t, row + 1) + (w[3] * left + w[4] * right))
        )
    return out


def front_kernel(
    prior_hbm, spread_hbm, courant_hbm, cells_hbm, value_hbm, error_hbm,
    d_ref, mean_ref, total_ref,
    spread_ref, courant_ref, cells_ref, value_ref, error_ref,
    nat_ref, u_ref, f_ref, full_ref, pick_ref, raw_ref, coef_ref,
    edge_ref, colin_ref, rowc_ref, rowin_ref, cor_ref, comb_ref, acc_ref, give_ref, share_ref, shared_ref,
    part_ref, rs_ref, ysrc_ref, yin_ref, zsrc_ref, zin_ref, fin_ref, gat_ref,
    more_ref, rsm_ref, ymsrc_ref, ym_ref, zmsrc_ref, zm_ref,
    load_sem, tiny_sem, halo_s, halo_r, small_s, small_r, rs_sem, y_sem, z_sem, ag_sem,
):
    y, x = lax.axis_index("row_0"), lax.axis_index("row_1")
    z, core = lax.axis_index("col_0"), lax.axis_index("col_1")
    row, col = y * 4 + x, z * 2 + core

    def at_row(n):
        n = lax.rem(n + 32, 32)
        return (n // 4, lax.rem(n, 4), z, core)

    def at_col(n):
        n = lax.rem(n + 16, 16)
        return (y, x, n // 2, lax.rem(n, 2))

    up, down, left, right = at_row(row - 1), at_row(row + 1), at_col(col - 1), at_col(col + 1)
    me = x * 2 + core
    far_first = (4, 3, 5, 2, 6, 1, 7)
    group = [lax.rem(me + i, 8) for i in far_first]
    group_dev = [(y, g // 2, z, lax.rem(g, 2)) for g in group]
    ys = [lax.rem(y + i, 8) for i in far_first]
    zs = [lax.rem(z + i, 8) for i in far_first]
    y_dev = [(n, x, z, core) for n in ys]
    z_dev = [(y, x, n, core) for n in zs]

    barrier = pltpu.get_barrier_semaphore()
    everyone = [up, down, left, right] + group_dev + y_dev + z_dev
    for device in everyone:
        pl.semaphore_signal(barrier, inc=1, device_id=device, device_id_type=MESH_IDS)

    tiny = [
        pltpu.make_async_copy(src, dst, tiny_sem.at[n])
        for n, (src, dst) in enumerate(
            (
                (spread_hbm, spread_ref),
                (courant_hbm, courant_ref),
                (cells_hbm, cells_ref),
                (value_hbm, value_ref),
                (error_hbm, error_ref),
            )
        )
    ]
    loads = [
        pltpu.make_async_copy(
            prior_hbm.at[pl.ds(part * PART * 8, PART * 8), pl.ds(128 * t, 128)],
            nat_ref.at[t, pl.ds(part * PART * 8, PART * 8), :],
            load_sem.at[2 * part + t],
        )
        for part in range(CHUNKS)
        for t in range(2)
    ]
    for c in loads[:2] + tiny[:2] + loads[2:] + tiny[2:]:
        c.start()

    halo = []
    for part in range(2):
        some = pl.ds(part * 64, 64)
        for t in range(2):
            slot = part * 4 + t * 2
            halo.append(send(u_ref.at[t, 2:4, some, :], u_ref.at[t, 10:12, some, :], (halo_s, halo_r), slot, up))
            halo.append(send(u_ref.at[t, 8:10, some, :], u_ref.at[t, 0:2, some, :], (halo_s, halo_r), slot + 1, down))

    def spread_rows(part, which):
        for t in range(2):
            for r in which:
                u_ref[t, 2 + r, part * PART : part * PART + PART, :] = nat_ref[
                    t, pl.ds(part * PART * 8 + r, PART, stride=8), :
                ]

    small = (small_s, small_r)
    for c in tiny:
        c.wait()

    lanes8 = lax.broadcasted_iota(jnp.int32, (8, 128), 1)
    for t in range(2):
        cut = slice(128 * t, 128 * t + 128)
        for n, block in enumerate((spread_ref[:, cut], courant_ref[0:8, cut], courant_ref[8:16, cut])):
            raw_ref[n, t, 1:9, :] = block
            rowc_ref[t, n : n + 1, :] = block[7:8, :]
            rowc_ref[t, n + 3 : n + 4, :] = block[0:1, :]
            if n < 2:
                rowc_ref[t, n + 6 : n + 7, :] = block[1:2, :]
            if n == 0:
                rowc_ref[t, 8:9, :] = block[6:7, :]
        rowc_ref[t, 9:10, :] = cells_ref[...].astype(F32)
        rowc_ref[t, 10:16, :] = jnp.zeros((6, 128), F32)
    rows_out = [send(rowc_ref, rowin_ref.at[1], small, 0, up), send(rowc_ref, rowin_ref.at[0], small, 1, down)]
    pl.semaphore_wait(barrier, len(everyone))
    for c in rows_out:
        c.start()
    edge = jnp.zeros((8, 128), F32)
    for n in range(3):
        last = spread_ref[:, 128:256] if n == 0 else courant_ref[8 * n - 8 : 8 * n, 128:256]
        first = spread_ref[:, 0:128] if n == 0 else courant_ref[8 * n - 8 : 8 * n, 0:128]
        edge = jnp.where(lanes8 == n, pltpu.roll(last, 1 + n, 1), edge)
        edge = jnp.where(lanes8 == n + 3, pltpu.roll(first, 3 + n, 1), edge)
    edge_ref[0, 16:24, :] = edge
    edge_ref[1, 16:24, :] = edge
    for part in range(CHUNKS):
        for c in loads[2 * part : 2 * part + 2]:
            c.wait()
        spread_rows(part, range(8))

    lanes = lax.broadcasted_iota(jnp.int32, (128, 128), 1)
    ends = jnp.zeros((128, 128), F32)
    for r in range(8):
        ends = jnp.where((lanes >> 1) == r, pltpu.roll(u_ref[1, 2 + r], 2 + 2 * r, 1), ends)
        ends = jnp.where((lanes >> 1) == r + 8, pltpu.roll(u_ref[0, 2 + r], 16 + 2 * r, 1), ends)
    ends = ends.T
    edge_ref[0, 0:16, :] = ends[0:16]
    edge_ref[1, 0:16, :] = ends[16:32]
    cols_out = [
        send(edge_ref.at[0], colin_ref.at[0], small, 2, right),
        send(edge_ref.at[1], colin_ref.at[1], small, 3, left),
    ]
    for c in cols_out:
        c.start()

    cells = cells_ref[...]
    places = lax.broadcasted_iota(jnp.int32, (256, 128), 0)
    for r in range(8):
        pick_ref[r] = jnp.where(places + 256 * r == cells, F32(1.0), F32(0.0)).astype(BF16)

    few = lax.broadcasted_iota(jnp.int32, (PART, 128), 1)
    thin = lax.broadcasted_iota(jnp.int32, (1, 128), 1)

    def sideways(k, t1, t):
        w_left, w_right = k + t1, k
        if t == 0:
            w_left = jnp.where(thin == 0, F32(0.0), w_left)
        else:
            w_right = jnp.where(thin == 127, F32(0.0), w_right)
        return w_left, w_right

    def exact_parts(v):
        hi = v.astype(BF16)
        rest = v - hi.astype(F32)
        mid = rest.astype(BF16)
        lo = (rest - mid.astype(F32)).astype(BF16)
        return jnp.concatenate([hi, mid, lo], axis=0)

    for c in rows_out:
        c.wait_recv()
    for side in range(2):
        a, b = ((8, 9), (3, 2))[side]
        mine = b - 1
        theirs, first = ((1, 3), (0, 0))[side]
        w = []
        for t in range(2):
            k, t0, t1 = (raw_ref[n, t, mine : mine + 1, :] for n in range(3))
            own = (1.0 - 4.0 * k - t0 - t1, k + t0 if side == 0 else k) + sideways(k, t1, t)
            k, t0, t1 = (rowin_ref[theirs, t, first + n : first + n + 1, :] for n in range(3))
            near = (1.0 - 4.0 * k - t0 - t1, k + t0 if side == 0 else k) + sideways(k, t1, t)
            if side == 0:
                far = rowin_ref[theirs, t, 6:7, :] + rowin_ref[theirs, t, 7:8, :]
            else:
                far = rowin_ref[theirs, t, 8:9, :]
            w.append((own, near, far))
        for part in range(CHUNKS):
            some = slice(part * PART, part * PART + PART)
            ub = [u_ref[t, b, some, :] for t in range(2)]
            h = [w[t][1][1] * ub[t] for t in range(2)]
            b_left, b_right = [pltpu.roll(v, 1, 1) for v in ub], [pltpu.roll(v, 127, 1) for v in ub]
            h_left, h_right = [pltpu.roll(v, 1, 1) for v in h], [pltpu.roll(v, 127, 1) for v in h]

            def ends_of(before, after, t):
                if t == 0:
                    return before[0], jnp.where(few == 127, after[1], after[0])
                return jnp.where(few == 0, before[0], before[1]), after[1]

            for t in range(2):
                own, near, far = w[t]
                bl, br = ends_of(b_left, b_right, t)
                hl, hr = ends_of(h_left, h_right, t)
                g = (own[0] * ub[t] + own[1] * u_ref[t, a, some, :]) + (own[2] * bl + own[3] * br)
                cut = slice(128 * t, 128 * t + 128)
                give_ref[0, some, cut] = (near[0] * h[t] + near[1] * g) + (near[2] * hl + near[3] * hr)
                give_ref[1, some, cut] = far * h[t]
        their_cells = rowin_ref[theirs, 0, 9:10, :]
        spots = places.astype(F32)
        got = jnp.zeros((384, 128), F32)
        for n, base in enumerate(((0, 256), (1792, 1536))[side]):
            chosen = jnp.where(spots + F32(base) == their_cells, F32(1.0), F32(0.0)).astype(BF16)
            got = got + jnp.dot(exact_parts(give_ref[n]), chosen, preferred_element_type=F32)
        share_ref[side] = (got[0:128] + got[128:256]) + got[256:384]

    for c in cols_out:
        c.wait_recv()
    corners_out = [
        send(colin_ref.at[:, 8:16, :], cor_ref.at[0], small, 4, down),
        send(colin_ref.at[:, 0:8, :], cor_ref.at[1], small, 5, up),
    ]
    shares_out = [
        send(share_ref.at[0], shared_ref.at[0], small, 6, down),
        send(share_ref.at[1], shared_ref.at[1], small, 7, up),
    ]
    for c in corners_out + shares_out + halo[:4]:
        c.start()

    for n in range(3):
        for t in range(2):
            raw_ref[n, t, 0:1, :] = rowin_ref[0, t, n : n + 1, :]
            raw_ref[n, t, 9:10, :] = rowin_ref[1, t, n + 3 : n + 4, :]
        beyond = jnp.where(
            lanes8 == 127,
            pltpu.roll(colin_ref[0, 16:24, :], 127 - n, 1),
            pltpu.roll(colin_ref[1, 16:24, :], 125 - n, 1),
        )
        raw_ref[n, 2, 0:1, :] = jnp.zeros((1, 128), F32)
        raw_ref[n, 2, 1:9, :] = jnp.where((lanes8 == 127) | (lanes8 == 0), beyond, F32(0.0))
        raw_ref[n, 2, 9:10, :] = jnp.zeros((1, 128), F32)
    wide = lax.broadcasted_iota(jnp.int32, (10, 128), 1)
    deep = lax.broadcasted_iota(jnp.int32, (10, 128), 0)
    for t in range(3):
        k, t0, t1 = (raw_ref[n, t, 0:10, :] for n in range(3))
        zero = jnp.zeros_like(k)
        coef_ref[0, t, 0:10, :] = 1.0 - 4.0 * k - t0 - t1
        coef_ref[1, t, 0:10, :] = jnp.where((deep == 1) & (row == 0), zero, k + t0)
        coef_ref[2, t, 0:10, :] = jnp.where((deep == 8) & (row == 31), zero, k)
        w_left, w_right = k + t1, k
        if t == 0:
            w_left = jnp.where((wide == 0) & (col == 0), zero, w_left)
        if t == 1:
            w_right = jnp.where((wide == 127) & (col == 15), zero, w_right)
        coef_ref[3, t, 0:10, :] = w_left
        coef_ref[4, t, 0:10, :] = w_right

    comb_ref[...] = jnp.zeros((128, 128), F32)
    for r in range(8):
        comb_ref[4 * r + 4 : 4 * r + 6, :] = colin_ref[0, 2 * r : 2 * r + 2, :]
        comb_ref[4 * r + 6 : 4 * r + 8, :] = colin_ref[1, 2 * r : 2 * r + 2, :]
    turned = comb_ref[...].T
    for n in range(1, 9):
        u_ref[2, n + 1] = pltpu.roll(turned, (126 - 4 * n) % 128, 1)

    def first_step(some, n, all_rows):
        tiles = range(3) if 1 <= n <= 8 else range(2)

        def get(t, i):
            if not all_rows and (i in (-1, 10) or (i in (0, 9) and t < 2)):
                return jnp.zeros((PART, 128), F32)
            return u_ref[t, i + 1, some, :]

        for t, v in zip(tiles, stencil(get, coef_ref, n, tiles, few)):
            f_ref[t, n, some, :] = v

    def second_step(some, n):
        for t, v in zip(range(2), stencil(lambda t, i: f_ref[t, i, some, :], coef_ref, n, range(2), few)):
            full_ref[n - 1, some, 128 * t : 128 * t + 128] = v

    @pl.loop(0, CHUNKS)
    def _(part):
        some = pl.ds(pl.multiple_of(part * PART, PART), PART)
        for n in range(2, 8):
            first_step(some, n, False)
        for n in range(3, 7):
            second_step(some, n)

    def observe(n):
        return jnp.dot(exact_parts(full_ref[n]), pick_ref[n], preferred_element_type=F32)

    acc_ref[...] = (observe(2) + observe(3)) + (observe(4) + observe(5))

    for c in corners_out:
        c.wait_recv()
    for side in range(2):
        comb_ref[2 * side : 2 * side + 2, :] = cor_ref[0, side, 6:8, :]
        comb_ref[36 + 2 * side : 38 + 2 * side, :] = cor_ref[1, side, 0:2, :]
    turned = comb_ref[...].T
    for n in (0, 9):
        u_ref[2, n + 1] = pltpu.roll(turned, (126 - 4 * n) % 128, 1)

    def end_rows(some, all_rows):
        for n in (0, 1, 8, 9):
            first_step(some, n, all_rows)
        for n in (1, 2, 7, 8):
            second_step(some, n)

    @pl.loop(0, CHUNKS)
    def _(part):
        end_rows(pl.ds(pl.multiple_of(part * PART, PART), PART), False)

    seen = acc_ref[...] + ((observe(0) + observe(1)) + (observe(6) + observe(7)))
    for c in shares_out:
        c.wait_recv()
    from_up = jnp.where(row == 0, F32(0.0), F32(1.0)) * shared_ref[0]
    from_down = jnp.where(row == 31, F32(0.0), F32(1.0)) * shared_ref[1]
    observed = ((seen[0:128] + seen[128:256]) + seen[256:384]) + (from_up + from_down)
    obs_mean = jnp.sum(observed, axis=0, keepdims=True) * F32(1.0 / 128.0)
    err = error_ref[...]
    scaled = (observed - obs_mean) / (err * jnp.sqrt(F32(127.0)))
    innovation = jnp.broadcast_to((value_ref[...] - obs_mean) / err, (8, 128))
    turned_dot = (((1,), (1,)), ((), ()))
    gram = lax.dot_general(scaled, scaled, turned_dot, precision=HIGHEST, preferred_element_type=F32)
    pulled = lax.dot_general(innovation, scaled, turned_dot, precision=HIGHEST, preferred_element_type=F32)
    deep128 = lax.broadcasted_iota(jnp.int32, (128, 128), 0)
    diagonal = jnp.sum(jnp.where(lanes == deep128, gram, F32(0.0)), axis=0, keepdims=True)
    rows8 = lax.broadcasted_iota(jnp.int32, (8, 128), 0)
    folded = pltpu.roll(gram[64:128], 64, 1)
    for g in range(8):
        cut = slice(8 * g, 8 * g + 8)
        keep = (lanes8 >= 64) | (lanes8 < rows8 + 8 * g)
        part_ref[g] = jnp.where(keep, gram[cut], folded[cut])
    more_ref[0:1, :] = pulled[0:1]
    more_ref[1:2, :] = diagonal

    def exchange(main, more, into, more_into, sems, place, ids, devs):
        out = [
            send(main(n), into.at[place], (sems[0], sems[1]), n, dev, landed=place) for n, dev in zip(ids, devs)
        ]
        for c in out:
            c.start()
        if more is not None:
            out += [
                send(more, more_into.at[place], (sems[2], sems[3]), n, dev, landed=place) for n, dev in zip(ids, devs)
            ]
            for c in out[len(ids) :]:
                c.start()
        return out

    def landed(main, more, into, more_into, sems, ids, devs):
        for n, dev in zip(ids, devs):
            send(main, into.at[n], (sems[0], sems[1]), n, dev).wait_recv()
            if more is not None:
                send(more, more_into.at[n], (sems[2], sems[3]), n, dev).wait_recv()

    def total(buf):
        return ((buf[0] + buf[1]) + (buf[2] + buf[3])) + ((buf[4] + buf[5]) + (buf[6] + buf[7]))

    rs_sems, y_sems, z_sems, ag_sems = (
        [sems.at[n] for n in range(4)] for sems in (rs_sem, y_sem, z_sem, ag_sem)
    )
    rs = exchange(lambda n: part_ref.at[n], more_ref, rs_ref, rsm_ref, rs_sems, me, group, group_dev)
    rs_ref[pl.ds(me, 1)] = part_ref[pl.ds(me, 1)]
    rsm_ref[pl.ds(me, 1)] = more_ref[...][None]

    for c in halo[4:]:
        c.start()

    def depart(rows):
        for r in rows:
            v = full_ref[r]
            mean = jnp.sum(v, axis=0, keepdims=True) * F32(1.0 / 128.0)
            mean_ref[r : r + 1, :] = mean
            d_ref[r] = v - mean

    def finish_rows(half):
        for c in halo[4 * half : 4 * half + 4]:
            c.wait_recv()

        @pl.loop(half * (CHUNKS // 2), (half + 1) * (CHUNKS // 2))
        def _(part):
            end_rows(pl.ds(pl.multiple_of(part * PART, PART), PART), True)

    depart(range(2, 6))

    landed(part_ref.at[0], more_ref, rs_ref, rsm_ref, rs_sems, group, group_dev)
    ysrc_ref[...] = total(rs_ref)
    ymsrc_ref[...] = total(rsm_ref)
    by_y = exchange(lambda n: ysrc_ref, ymsrc_ref, yin_ref, ym_ref, y_sems, y, ys, y_dev)
    yin_ref[pl.ds(y, 1)] = ysrc_ref[...][None]
    ym_ref[pl.ds(y, 1)] = ymsrc_ref[...][None]
    finish_rows(0)
    landed(ysrc_ref, ymsrc_ref, yin_ref, ym_ref, y_sems, ys, y_dev)
    zsrc_ref[...] = total(yin_ref)
    zmsrc_ref[...] = total(ym_ref)
    by_z = exchange(lambda n: zsrc_ref, zmsrc_ref, zin_ref, zm_ref, z_sems, z, zs, z_dev)
    zin_ref[pl.ds(z, 1)] = zsrc_ref[...][None]
    zm_ref[pl.ds(z, 1)] = zmsrc_ref[...][None]
    finish_rows(1)
    depart((0, 1, 6, 7))
    landed(zsrc_ref, zmsrc_ref, zin_ref, zm_ref, z_sems, zs, z_dev)
    fin_ref[...] = total(zin_ref)
    ag = exchange(lambda n: fin_ref, None, gat_ref, None, ag_sems, me, group, group_dev)
    gat_ref[pl.ds(me, 1)] = fin_ref[...][None]
    total_ref[64:66, :] = total(zm_ref)
    total_ref[66:72, :] = jnp.zeros((6, 128), F32)
    landed(fin_ref, None, gat_ref, None, ag_sems, group, group_dev)
    for g in range(8):
        total_ref[8 * g : 8 * g + 8, :] = gat_ref[g]
    for c in halo + rows_out + cols_out + corners_out + shares_out + rs + by_y + by_z + ag:
        c.wait_send()


def front(prior, spread, courant, cells, value, error):
    vmem, hbm = pl.BlockSpec(memory_space=pltpu.VMEM), pl.BlockSpec(memory_space=pl.ANY)
    dma = pltpu.SemaphoreType.DMA
    return pl.pallas_call(
        front_kernel,
        out_shape=(
            pltpu.VMEM((8, 128, 256), F32),
            pltpu.VMEM((8, 256), F32),
            pltpu.VMEM((72, 128), F32),
        ),
        in_specs=[hbm] * 6,
        out_specs=(vmem, vmem, vmem),
        scratch_shapes=[
            pltpu.VMEM((8, 256), F32),
            pltpu.VMEM((16, 256), F32),
            pltpu.VMEM((1, 128), jnp.int32),
            pltpu.VMEM((1, 128), F32),
            pltpu.VMEM((1, 128), F32),
            pltpu.VMEM((2, 1024, 128), F32),
            pltpu.VMEM((3, 12, 128, 128), F32),
            pltpu.VMEM((3, 10, 128, 128), F32),
            pltpu.VMEM((8, 128, 256), F32),
            pltpu.VMEM((8, 256, 128), BF16),
            pltpu.VMEM((3, 3, 16, 128), F32),
            pltpu.VMEM((5, 3, 16, 128), F32),
            pltpu.VMEM((2, 24, 128), F32),
            pltpu.VMEM((2, 24, 128), F32),
            pltpu.VMEM((2, 16, 128), F32),
            pltpu.VMEM((2, 2, 16, 128), F32),
            pltpu.VMEM((2, 2, 8, 128), F32),
            pltpu.VMEM((128, 128), F32),
            pltpu.VMEM((384, 128), F32),
            pltpu.VMEM((2, 128, 256), F32),
            pltpu.VMEM((2, 128, 128), F32),
            pltpu.VMEM((2, 128, 128), F32),
            pltpu.VMEM((8, 8, 128), F32),
            pltpu.VMEM((8, 8, 128), F32),
            pltpu.VMEM((8, 128), F32),
            pltpu.VMEM((8, 8, 128), F32),
            pltpu.VMEM((8, 128), F32),
            pltpu.VMEM((8, 8, 128), F32),
            pltpu.VMEM((8, 128), F32),
            pltpu.VMEM((8, 8, 128), F32),
            pltpu.VMEM((2, 128), F32),
            pltpu.VMEM((8, 2, 128), F32),
            pltpu.VMEM((2, 128), F32),
            pltpu.VMEM((8, 2, 128), F32),
            pltpu.VMEM((2, 128), F32),
            pltpu.VMEM((8, 2, 128), F32),
            dma((2 * CHUNKS,)),
            dma((5,)),
            dma((8,)),
            dma((8,)),
            dma((8,)),
            dma((8,)),
            dma((4, 8)),
            dma((4, 8)),
            dma((4, 8)),
            dma((4, 8)),
        ],
        compiler_params=pltpu.CompilerParams(collective_id=0, has_side_effects=True),
        name="front",
    )(prior, spread, courant, cells, value, error)


def body(
    prior_sample_fields, spreading_coefficient, transport_courant, obs_cells, obs_value, obs_error
):
    departures, mean, packed = front(
        prior_sample_fields.reshape(1024, 256),
        spreading_coefficient,
        transport_courant.reshape(16, 256),
        obs_cells[None, :],
        obs_value[None, :],
        obs_error[None, :],
    )
    return tail(packed, departures, mean).reshape(128, 8, 256)


def solution(mesh):
    split = Mesh(mesh.devices.reshape(8, 4, 8, 2), ("row_0", "row_1", "col_0", "col_1"))
    return jax.shard_map(
        body,
        mesh=split,
        in_specs=(
            P(None, ROW, COL),
            P(ROW, COL),
            P(None, ROW, COL),
            P(ROW_COL),
            P(ROW_COL),
            P(ROW_COL),
        ),
        out_specs=P(None, ROW, COL),
        check_vma=False,
    )
```

```python
import jax
import jax.numpy as jnp
from jax import lax
from jax.experimental import pallas as pl
from jax.experimental.pallas import tpu as pltpu
from jax.sharding import Mesh
from jax.sharding import PartitionSpec as P

ROW_COL = ("row_0", "row_1", "col_0", "col_1")
ROW = ("row_0", "row_1")
COL = ("col_0", "col_1")
F32 = jnp.float32
BF16 = jnp.bfloat16


def lane_spread(x, lane):
    return jnp.broadcast_to(x[:, lane : lane + 1], (8, 128))


def row_spread(x, row):
    return jnp.broadcast_to(x[row : row + 1, :], (8, 128))


def picked_row(x, mask):
    return jnp.broadcast_to(jnp.sum(jnp.where(mask, x, F32(0.0)), axis=0, keepdims=True), (8, 128))


def split2(x):
    hi = x.astype(BF16)
    lo = (x - hi.astype(F32)).astype(BF16)
    return hi, lo


def factor_rows(x_ref, d_ref):
    lanes = lax.broadcasted_iota(jnp.int32, (8, 128), 1)
    rows = lax.broadcasted_iota(jnp.int32, (8, 128), 0)
    for k in range(16):
        base = 8 * k
        p = x_ref[k]
        c = [lane_spread(p, base + j) for j in range(8)]
        a = {(i, j): picked_row(c[j], rows == i) for j in range(8) for i in range(j, 8)}
        in_block = (lanes >= base) & (lanes < base + 8)
        eye = jnp.where(lanes - base == rows, F32(1.0), F32(0.0))
        p0 = jnp.where(in_block, eye, p)
        pb = [row_spread(p0, i) for i in range(8)]
        inv = []
        pivots = jnp.zeros((8, 128), F32)
        low = {}
        for j in range(8):
            pivots = jnp.where(rows == j, a[j, j], pivots)
            r = 1.0 / a[j, j]
            inv.append(r)
            for i in range(j + 1, 8):
                low[i, j] = a[i, j] * r
            for i in range(j + 1, 8):
                for m in range(i, 8):
                    a[m, i] = a[m, i] - a[m, j] * low[i, j]
                pb[i] = pb[i] - low[i, j] * pb[j]
        done = pb[0]
        for i in range(1, 8):
            done = jnp.where(rows == i, pb[i], done)
        x_ref[k] = done
        d_ref[k] = pivots
        if k == 15:
            break
        q = x_ref[k + 1]
        cq = [lane_spread(q, base + j) for j in range(8)]
        q = jnp.where(in_block, F32(0.0), q)
        for j in range(8):
            mult = cq[j] * inv[j]
            q = q - mult * pb[j]
            for i in range(j + 1, 8):
                cq[i] = cq[i] - mult * a[i, j]
        x_ref[k + 1] = q
        if k == 14:
            continue
        minv = {}
        for j in range(8):
            for i in range(j):
                t = low[j, i]
                for m in range(i + 1, j):
                    t = t + low[j, m] * minv[m, i]
                minv[j, i] = -t
        z = []
        scaled = [pb[j] * inv[j] for j in range(8)]
        for i in range(8):
            t = scaled[i]
            for j in range(i + 1, 8):
                t = t + minv[j, i] * scaled[j]
            z.append(t)
        for t in range(k + 2, 16):
            q = x_ref[t]
            cq = [lane_spread(q, base + j) for j in range(8)]
            q = jnp.where(in_block, F32(0.0), q)
            s0 = cq[0] * z[0] + cq[1] * z[1]
            s1 = cq[2] * z[2] + cq[3] * z[3]
            s2 = cq[4] * z[4] + cq[5] * z[5]
            s3 = cq[6] * z[6] + cq[7] * z[7]
            x_ref[t] = q - ((s0 + s1) + (s2 + s3))


def tail_kernel(g_ref, dd_ref, mean_ref, out_hbm, x_ref, d_ref, o_ref, out_sem):
    lanes = lax.broadcasted_iota(jnp.int32, (8, 128), 1)
    rows = lax.broadcasted_iota(jnp.int32, (8, 128), 0)
    upper = g_ref[0:64, :]
    lanes64 = lax.broadcasted_iota(jnp.int32, (64, 128), 1)
    rows64 = lax.broadcasted_iota(jnp.int32, (64, 128), 0)
    half = jnp.concatenate(
        [
            jnp.where((lanes64 >= 64) | (lanes64 < rows64), upper, F32(0.0)),
            jnp.where(lanes64 - 64 > rows64, pltpu.roll(upper, 64, 1), F32(0.0)),
        ],
        axis=0,
    )
    gram = half + half.T
    diagonal = row_spread(g_ref[64:72, :], 1) + F32(1.0)
    for k in range(16):
        x_ref[k] = jnp.where(lanes - 8 * k == rows, diagonal, gram[8 * k : 8 * k + 8])
    factor_rows(x_ref, d_ref)
    pulled = row_spread(g_ref[64:72, :], 0)
    root = jnp.sqrt(F32(127.0))
    shift = jnp.zeros((8, 128), F32)
    kept = []
    for k in range(16):
        m = jnp.where(lanes - 8 * k <= rows, x_ref[k], F32(0.0))
        kept.append(m)
        y = jnp.sum(m * pulled, axis=1, keepdims=True)
        shift = shift + m * (jnp.broadcast_to(y, (8, 128)) / d_ref[k])
    shift = jnp.broadcast_to(jnp.sum(shift, axis=0, keepdims=True), (8, 128))
    w = []
    for k in range(16):
        w.append((kept[k] / jnp.sqrt(d_ref[k]) + shift) / root)
    w = jnp.concatenate(w, axis=0)
    whi, wlo = split2(w)
    both = jnp.concatenate([whi, wlo], axis=1)
    for r in range(8):
        hi, lo = split2(dd_ref[r])
        acc = jnp.dot(both, jnp.concatenate([hi, hi], axis=0), preferred_element_type=F32)
        acc = acc + jnp.dot(both, jnp.concatenate([lo, lo], axis=0), preferred_element_type=F32)
        acc = acc + mean_ref[r : r + 1, :]
        o_ref[0, pl.ds(r, 128, stride=8), :] = acc[:, 0:128]
        o_ref[1, pl.ds(r, 128, stride=8), :] = acc[:, 128:256]
    outs = [
        pltpu.make_async_copy(o_ref.at[n], out_hbm.at[:, pl.ds(128 * n, 128)], out_sem.at[n]) for n in range(2)
    ]
    for c in outs:
        c.start()
    for c in outs:
        c.wait()


def tail(g, departures, mean):
    return pl.pallas_call(
        tail_kernel,
        out_shape=jax.ShapeDtypeStruct((1024, 256), F32),
        in_specs=[
            pl.BlockSpec(memory_space=pltpu.VMEM),
            pl.BlockSpec(memory_space=pltpu.VMEM),
            pl.BlockSpec(memory_space=pltpu.VMEM),
        ],
        out_specs=pl.BlockSpec(memory_space=pl.ANY),
        scratch_shapes=[
            pltpu.VMEM((16, 8, 128), F32),
            pltpu.VMEM((16, 8, 128), F32),
            pltpu.VMEM((2, 1024, 128), F32),
            pltpu.SemaphoreType.DMA((2,)),
        ],
        compiler_params=pltpu.CompilerParams(vmem_limit_bytes=16 << 20),
        name="tail",
    )(g, departures, mean)


MESH_IDS = pl.DeviceIdType.MESH
HIGHEST = lax.Precision.HIGHEST
CHUNKS = 2
PART = 128 // CHUNKS


def send(src, dst, sems, slot, device, landed=None):
    landed = slot if landed is None else landed
    return pltpu.make_async_remote_copy(
        src_ref=src,
        dst_ref=dst,
        send_sem=sems[0].at[slot],
        recv_sem=sems[1].at[landed],
        device_id=device,
        device_id_type=MESH_IDS,
    )


def stencil(get, coef_ref, row, tiles, lanes):
    centre = [get(t, row) for t in range(3)]
    right_of = [pltpu.roll(v, 127, 1) for v in centre]
    left_of = [pltpu.roll(v, 1, 1) for v in centre]
    out = []
    for t in tiles:
        left = jnp.where(lanes == 0, left_of[(t + 2) % 3], left_of[t])
        right = jnp.where(lanes == 127, right_of[(t + 1) % 3], right_of[t])
        w = [coef_ref[n, t, row : row + 1, :] for n in range(5)]
        out.append(
            (w[0] * centre[t] + w[1] * get(t, row - 1)) + (w[2] * get(t, row + 1) + (w[3] * left + w[4] * right))
        )
    return out


def front_kernel(
    prior_hbm, spread_hbm, courant_hbm, cells_hbm, value_hbm, error_hbm,
    d_ref, mean_ref, total_ref,
    spread_ref, courant_ref, cells_ref, value_ref, error_ref,
    nat_ref, u_ref, f_ref, full_ref, pick_ref, raw_ref, coef_ref,
    edge_ref, colin_ref, rowc_ref, rowin_ref, cor_ref, comb_ref, acc_ref, give_ref, share_ref, shared_ref,
    part_ref, rs_ref, ysrc_ref, yin_ref, zsrc_ref, zin_ref, fin_ref, gat_ref,
    more_ref, rsm_ref, ymsrc_ref, ym_ref, zmsrc_ref, zm_ref,
    load_sem, tiny_sem, halo_s, halo_r, small_s, small_r, rs_sem, y_sem, z_sem, ag_sem,
):
    y, x = lax.axis_index("row_0"), lax.axis_index("row_1")
    z, core = lax.axis_index("col_0"), lax.axis_index("col_1")
    row, col = y * 4 + x, z * 2 + core

    def at_row(n):
        n = lax.rem(n + 32, 32)
        return (n // 4, lax.rem(n, 4), z, core)

    def at_col(n):
        n = lax.rem(n + 16, 16)
        return (y, x, n // 2, lax.rem(n, 2))

    up, down, left, right = at_row(row - 1), at_row(row + 1), at_col(col - 1), at_col(col + 1)
    me = x * 2 + core
    far_first = (4, 3, 5, 2, 6, 1, 7)
    group = [lax.rem(me + i, 8) for i in far_first]
    group_dev = [(y, g // 2, z, lax.rem(g, 2)) for g in group]
    ys = [lax.rem(y + i, 8) for i in far_first]
    zs = [lax.rem(z + i, 8) for i in far_first]
    y_dev = [(n, x, z, core) for n in ys]
    z_dev = [(y, x, n, core) for n in zs]

    barrier = pltpu.get_barrier_semaphore()
    everyone = group_dev + y_dev + z_dev
    beside = {"up": up, "down": down, "left": left, "right": right}
    there = {"up": row > 0, "down": row < 31, "left": col > 0, "right": col < 15}
    opposite = {"up": "down", "down": "up", "left": "right", "right": "left"}
    for way, device in beside.items():

        @pl.when(there[way])
        def _():
            pl.semaphore_signal(barrier, inc=1, device_id=device, device_id_type=MESH_IDS)

    for device in everyone:
        pl.semaphore_signal(barrier, inc=1, device_id=device, device_id_type=MESH_IDS)

    def each_way(items, act, turn=lambda way: way):
        for way in beside:
            some = [c for c, w in items if w == way]
            if some:

                @pl.when(there[turn(way)])
                def _():
                    for c in some:
                        act(c)

    def begin(items):
        each_way(items, lambda c: c.start())

    def arrived(items):
        each_way(items, lambda c: c.wait_recv(), lambda way: opposite[way])

    def gone(items):
        each_way(items, lambda c: c.wait_send())

    tiny = [
        pltpu.make_async_copy(src, dst, tiny_sem.at[n])
        for n, (src, dst) in enumerate(
            (
                (spread_hbm, spread_ref),
                (courant_hbm, courant_ref),
                (cells_hbm, cells_ref),
                (value_hbm, value_ref),
                (error_hbm, error_ref),
            )
        )
    ]
    loads = [
        pltpu.make_async_copy(
            prior_hbm.at[pl.ds(part * PART * 8, PART * 8), pl.ds(128 * t, 128)],
            nat_ref.at[t, pl.ds(part * PART * 8, PART * 8), :],
            load_sem.at[2 * part + t],
        )
        for part in range(CHUNKS)
        for t in range(2)
    ]
    for c in loads[:2] + tiny[:2] + loads[2:] + tiny[2:]:
        c.start()

    for side, way in enumerate(("up", "down")):

        @pl.when(jnp.logical_not(there[way]))
        def _():
            rowin_ref[side] = jnp.zeros((2, 16, 128), F32)
            cor_ref[side] = jnp.zeros((2, 8, 128), F32)
            shared_ref[side] = jnp.zeros((128, 128), F32)
            for t in range(2):
                for n in range(2):
                    u_ref[t, 10 * side + n] = jnp.zeros((128, 128), F32)

    for side, way in enumerate(("left", "right")):

        @pl.when(jnp.logical_not(there[way]))
        def _():
            colin_ref[side] = jnp.zeros((24, 128), F32)

    halo = []
    for part in range(2):
        some = pl.ds(part * 64, 64)
        for t in range(2):
            slot = part * 4 + t * 2
            sems = (halo_s, halo_r)
            halo.append((send(u_ref.at[t, 2:4, some, :], u_ref.at[t, 10:12, some, :], sems, slot, up), "up"))
            halo.append((send(u_ref.at[t, 8:10, some, :], u_ref.at[t, 0:2, some, :], sems, slot + 1, down), "down"))

    def spread_rows(part, which):
        for t in range(2):
            for r in which:
                u_ref[t, 2 + r, part * PART : part * PART + PART, :] = nat_ref[
                    t, pl.ds(part * PART * 8 + r, PART, stride=8), :
                ]

    small = (small_s, small_r)
    for c in tiny:
        c.wait()

    lanes8 = lax.broadcasted_iota(jnp.int32, (8, 128), 1)
    for t in range(2):
        cut = slice(128 * t, 128 * t + 128)
        for n, block in enumerate((spread_ref[:, cut], courant_ref[0:8, cut], courant_ref[8:16, cut])):
            raw_ref[n, t, 1:9, :] = block
            rowc_ref[t, n : n + 1, :] = block[7:8, :]
            rowc_ref[t, n + 3 : n + 4, :] = block[0:1, :]
            if n < 2:
                rowc_ref[t, n + 6 : n + 7, :] = block[1:2, :]
            if n == 0:
                rowc_ref[t, 8:9, :] = block[6:7, :]
        rowc_ref[t, 9:10, :] = cells_ref[...].astype(F32)
        rowc_ref[t, 10:16, :] = jnp.zeros((6, 128), F32)
    rows_out = [
        (send(rowc_ref, rowin_ref.at[1], small, 0, up), "up"),
        (send(rowc_ref, rowin_ref.at[0], small, 1, down), "down"),
    ]
    at_border = (32 - row) // 32 + (row + 1) // 32 + (16 - col) // 16 + (col + 1) // 16
    pl.semaphore_wait(barrier, len(everyone) + 4 - at_border)
    begin(rows_out)
    edge = jnp.zeros((8, 128), F32)
    for n in range(3):
        last = spread_ref[:, 128:256] if n == 0 else courant_ref[8 * n - 8 : 8 * n, 128:256]
        first = spread_ref[:, 0:128] if n == 0 else courant_ref[8 * n - 8 : 8 * n, 0:128]
        edge = jnp.where(lanes8 == n, pltpu.roll(last, 1 + n, 1), edge)
        edge = jnp.where(lanes8 == n + 3, pltpu.roll(first, 3 + n, 1), edge)
    edge_ref[0, 16:24, :] = edge
    edge_ref[1, 16:24, :] = edge
    for part in range(CHUNKS):
        for c in loads[2 * part : 2 * part + 2]:
            c.wait()
        spread_rows(part, range(8))

    lanes = lax.broadcasted_iota(jnp.int32, (128, 128), 1)
    ends = jnp.zeros((128, 128), F32)
    for r in range(8):
        ends = jnp.where((lanes >> 1) == r, pltpu.roll(u_ref[1, 2 + r], 2 + 2 * r, 1), ends)
        ends = jnp.where((lanes >> 1) == r + 8, pltpu.roll(u_ref[0, 2 + r], 16 + 2 * r, 1), ends)
    ends = ends.T
    edge_ref[0, 0:16, :] = ends[0:16]
    edge_ref[1, 0:16, :] = ends[16:32]
    cols_out = [
        (send(edge_ref.at[0], colin_ref.at[0], small, 2, right), "right"),
        (send(edge_ref.at[1], colin_ref.at[1], small, 3, left), "left"),
    ]
    begin(cols_out)

    cells = cells_ref[...]
    places = lax.broadcasted_iota(jnp.int32, (256, 128), 0)
    for r in range(8):
        pick_ref[r] = jnp.where(places + 256 * r == cells, F32(1.0), F32(0.0)).astype(BF16)

    few = lax.broadcasted_iota(jnp.int32, (PART, 128), 1)
    thin = lax.broadcasted_iota(jnp.int32, (1, 128), 1)

    def sideways(k, t1, t):
        w_left, w_right = k + t1, k
        if t == 0:
            w_left = jnp.where(thin == 0, F32(0.0), w_left)
        else:
            w_right = jnp.where(thin == 127, F32(0.0), w_right)
        return w_left, w_right

    def exact_parts(v):
        hi = v.astype(BF16)
        rest = v - hi.astype(F32)
        mid = rest.astype(BF16)
        lo = (rest - mid.astype(F32)).astype(BF16)
        return jnp.concatenate([hi, mid, lo], axis=0)

    arrived(rows_out)
    for side in range(2):
        a, b = ((8, 9), (3, 2))[side]
        mine = b - 1
        theirs, first = ((1, 3), (0, 0))[side]
        w = []
        for t in range(2):
            k, t0, t1 = (raw_ref[n, t, mine : mine + 1, :] for n in range(3))
            own = (1.0 - 4.0 * k - t0 - t1, k + t0 if side == 0 else k) + sideways(k, t1, t)
            k, t0, t1 = (rowin_ref[theirs, t, first + n : first + n + 1, :] for n in range(3))
            near = (1.0 - 4.0 * k - t0 - t1, k + t0 if side == 0 else k) + sideways(k, t1, t)
            if side == 0:
                far = rowin_ref[theirs, t, 6:7, :] + rowin_ref[theirs, t, 7:8, :]
            else:
                far = rowin_ref[theirs, t, 8:9, :]
            w.append((own, near, far))
        for part in range(CHUNKS):
            some = slice(part * PART, part * PART + PART)
            ub = [u_ref[t, b, some, :] for t in range(2)]
            h = [w[t][1][1] * ub[t] for t in range(2)]
            b_left, b_right = [pltpu.roll(v, 1, 1) for v in ub], [pltpu.roll(v, 127, 1) for v in ub]
            h_left, h_right = [pltpu.roll(v, 1, 1) for v in h], [pltpu.roll(v, 127, 1) for v in h]

            def ends_of(before, after, t):
                if t == 0:
                    return before[0], jnp.where(few == 127, after[1], after[0])
                return jnp.where(few == 0, before[0], before[1]), after[1]

            for t in range(2):
                own, near, far = w[t]
                bl, br = ends_of(b_left, b_right, t)
                hl, hr = ends_of(h_left, h_right, t)
                g = (own[0] * ub[t] + own[1] * u_ref[t, a, some, :]) + (own[2] * bl + own[3] * br)
                cut = slice(128 * t, 128 * t + 128)
                give_ref[0, some, cut] = (near[0] * h[t] + near[1] * g) + (near[2] * hl + near[3] * hr)
                give_ref[1, some, cut] = far * h[t]
        their_cells = rowin_ref[theirs, 0, 9:10, :]
        spots = places.astype(F32)
        got = jnp.zeros((384, 128), F32)
        for n, base in enumerate(((0, 256), (1792, 1536))[side]):
            chosen = jnp.where(spots + F32(base) == their_cells, F32(1.0), F32(0.0)).astype(BF16)
            got = got + jnp.dot(exact_parts(give_ref[n]), chosen, preferred_element_type=F32)
        share_ref[side] = (got[0:128] + got[128:256]) + got[256:384]

    arrived(cols_out)
    corners_out = [
        (send(colin_ref.at[:, 8:16, :], cor_ref.at[0], small, 4, down), "down"),
        (send(colin_ref.at[:, 0:8, :], cor_ref.at[1], small, 5, up), "up"),
    ]
    shares_out = [
        (send(share_ref.at[0], shared_ref.at[0], small, 6, down), "down"),
        (send(share_ref.at[1], shared_ref.at[1], small, 7, up), "up"),
    ]
    begin(corners_out + shares_out + halo[:4])

    for n in range(3):
        for t in range(2):
            raw_ref[n, t, 0:1, :] = rowin_ref[0, t, n : n + 1, :]
            raw_ref[n, t, 9:10, :] = rowin_ref[1, t, n + 3 : n + 4, :]
        beyond = jnp.where(
            lanes8 == 127,
            pltpu.roll(colin_ref[0, 16:24, :], 127 - n, 1),
            pltpu.roll(colin_ref[1, 16:24, :], 125 - n, 1),
        )
        raw_ref[n, 2, 0:1, :] = jnp.zeros((1, 128), F32)
        raw_ref[n, 2, 1:9, :] = jnp.where((lanes8 == 127) | (lanes8 == 0), beyond, F32(0.0))
        raw_ref[n, 2, 9:10, :] = jnp.zeros((1, 128), F32)
    wide = lax.broadcasted_iota(jnp.int32, (10, 128), 1)
    deep = lax.broadcasted_iota(jnp.int32, (10, 128), 0)
    for t in range(3):
        k, t0, t1 = (raw_ref[n, t, 0:10, :] for n in range(3))
        zero = jnp.zeros_like(k)
        coef_ref[0, t, 0:10, :] = 1.0 - 4.0 * k - t0 - t1
        coef_ref[1, t, 0:10, :] = jnp.where((deep == 1) & (row == 0), zero, k + t0)
        coef_ref[2, t, 0:10, :] = jnp.where((deep == 8) & (row == 31), zero, k)
        w_left, w_right = k + t1, k
        if t == 0:
            w_left = jnp.where((wide == 0) & (col == 0), zero, w_left)
        if t == 1:
            w_right = jnp.where((wide == 127) & (col == 15), zero, w_right)
        coef_ref[3, t, 0:10, :] = w_left
        coef_ref[4, t, 0:10, :] = w_right

    comb_ref[...] = jnp.zeros((128, 128), F32)
    for r in range(8):
        comb_ref[4 * r + 4 : 4 * r + 6, :] = colin_ref[0, 2 * r : 2 * r + 2, :]
        comb_ref[4 * r + 6 : 4 * r + 8, :] = colin_ref[1, 2 * r : 2 * r + 2, :]
    turned = comb_ref[...].T
    for n in range(1, 9):
        u_ref[2, n + 1] = pltpu.roll(turned, (126 - 4 * n) % 128, 1)

    def first_step(some, n, all_rows):
        tiles = range(3) if 1 <= n <= 8 else range(2)

        def get(t, i):
            if not all_rows and (i in (-1, 10) or (i in (0, 9) and t < 2)):
                return jnp.zeros((PART, 128), F32)
            return u_ref[t, i + 1, some, :]

        for t, v in zip(tiles, stencil(get, coef_ref, n, tiles, few)):
            f_ref[t, n, some, :] = v

    def second_step(some, n):
        for t, v in zip(range(2), stencil(lambda t, i: f_ref[t, i, some, :], coef_ref, n, range(2), few)):
            full_ref[n - 1, some, 128 * t : 128 * t + 128] = v

    @pl.loop(0, CHUNKS)
    def _(part):
        some = pl.ds(pl.multiple_of(part * PART, PART), PART)
        for n in range(2, 8):
            first_step(some, n, False)
        for n in range(3, 7):
            second_step(some, n)

    def observe(n):
        return jnp.dot(exact_parts(full_ref[n]), pick_ref[n], preferred_element_type=F32)

    acc_ref[...] = (observe(2) + observe(3)) + (observe(4) + observe(5))

    arrived(corners_out)
    for side in range(2):
        comb_ref[2 * side : 2 * side + 2, :] = cor_ref[0, side, 6:8, :]
        comb_ref[36 + 2 * side : 38 + 2 * side, :] = cor_ref[1, side, 0:2, :]
    turned = comb_ref[...].T
    for n in (0, 9):
        u_ref[2, n + 1] = pltpu.roll(turned, (126 - 4 * n) % 128, 1)

    def end_rows(some, all_rows):
        for n in (0, 1, 8, 9):
            first_step(some, n, all_rows)
        for n in (1, 2, 7, 8):
            second_step(some, n)

    @pl.loop(0, CHUNKS)
    def _(part):
        end_rows(pl.ds(pl.multiple_of(part * PART, PART), PART), False)

    seen = acc_ref[...] + ((observe(0) + observe(1)) + (observe(6) + observe(7)))
    arrived(shares_out)
    observed = ((seen[0:128] + seen[128:256]) + seen[256:384]) + (shared_ref[0] + shared_ref[1])
    obs_mean = jnp.sum(observed, axis=0, keepdims=True) * F32(1.0 / 128.0)
    err = error_ref[...]
    scaled = (observed - obs_mean) / (err * jnp.sqrt(F32(127.0)))
    innovation = jnp.broadcast_to((value_ref[...] - obs_mean) / err, (8, 128))
    turned_dot = (((1,), (1,)), ((), ()))
    gram = lax.dot_general(scaled, scaled, turned_dot, precision=HIGHEST, preferred_element_type=F32)
    pulled = lax.dot_general(innovation, scaled, turned_dot, precision=HIGHEST, preferred_element_type=F32)
    deep128 = lax.broadcasted_iota(jnp.int32, (128, 128), 0)
    diagonal = jnp.sum(jnp.where(lanes == deep128, gram, F32(0.0)), axis=0, keepdims=True)
    rows8 = lax.broadcasted_iota(jnp.int32, (8, 128), 0)
    folded = pltpu.roll(gram[64:128], 64, 1)
    for g in range(8):
        cut = slice(8 * g, 8 * g + 8)
        keep = (lanes8 >= 64) | (lanes8 < rows8 + 8 * g)
        part_ref[g] = jnp.where(keep, gram[cut], folded[cut])
    more_ref[0:1, :] = pulled[0:1]
    more_ref[1:2, :] = diagonal

    def exchange(main, more, into, more_into, sems, place, ids, devs):
        out = [
            send(main(n), into.at[place], (sems[0], sems[1]), n, dev, landed=place) for n, dev in zip(ids, devs)
        ]
        for c in out:
            c.start()
        if more is not None:
            out += [
                send(more, more_into.at[place], (sems[2], sems[3]), n, dev, landed=place) for n, dev in zip(ids, devs)
            ]
            for c in out[len(ids) :]:
                c.start()
        return out

    def landed(main, more, into, more_into, sems, ids, devs):
        for n, dev in zip(ids, devs):
            send(main, into.at[n], (sems[0], sems[1]), n, dev).wait_recv()
            if more is not None:
                send(more, more_into.at[n], (sems[2], sems[3]), n, dev).wait_recv()

    def total(buf):
        return ((buf[0] + buf[1]) + (buf[2] + buf[3])) + ((buf[4] + buf[5]) + (buf[6] + buf[7]))

    rs_sems, y_sems, z_sems, ag_sems = (
        [sems.at[n] for n in range(4)] for sems in (rs_sem, y_sem, z_sem, ag_sem)
    )
    rs = exchange(lambda n: part_ref.at[n], more_ref, rs_ref, rsm_ref, rs_sems, me, group, group_dev)
    rs_ref[pl.ds(me, 1)] = part_ref[pl.ds(me, 1)]
    rsm_ref[pl.ds(me, 1)] = more_ref[...][None]

    begin(halo[4:])

    def depart(rows):
        for r in rows:
            v = full_ref[r]
            mean = jnp.sum(v, axis=0, keepdims=True) * F32(1.0 / 128.0)
            mean_ref[r : r + 1, :] = mean
            d_ref[r] = v - mean

    def finish_rows(half):
        arrived(halo[4 * half : 4 * half + 4])

        @pl.loop(half * (CHUNKS // 2), (half + 1) * (CHUNKS // 2))
        def _(part):
            end_rows(pl.ds(pl.multiple_of(part * PART, PART), PART), True)

    depart(range(2, 6))

    landed(part_ref.at[0], more_ref, rs_ref, rsm_ref, rs_sems, group, group_dev)
    ysrc_ref[...] = total(rs_ref)
    ymsrc_ref[...] = total(rsm_ref)
    by_y = exchange(lambda n: ysrc_ref, ymsrc_ref, yin_ref, ym_ref, y_sems, y, ys, y_dev)
    yin_ref[pl.ds(y, 1)] = ysrc_ref[...][None]
    ym_ref[pl.ds(y, 1)] = ymsrc_ref[...][None]
    finish_rows(0)
    landed(ysrc_ref, ymsrc_ref, yin_ref, ym_ref, y_sems, ys, y_dev)
    zsrc_ref[...] = total(yin_ref)
    zmsrc_ref[...] = total(ym_ref)
    by_z = exchange(lambda n: zsrc_ref, zmsrc_ref, zin_ref, zm_ref, z_sems, z, zs, z_dev)
    zin_ref[pl.ds(z, 1)] = zsrc_ref[...][None]
    zm_ref[pl.ds(z, 1)] = zmsrc_ref[...][None]
    finish_rows(1)
    depart((0, 1, 6, 7))
    landed(zsrc_ref, zmsrc_ref, zin_ref, zm_ref, z_sems, zs, z_dev)
    fin_ref[...] = total(zin_ref)
    ag = exchange(lambda n: fin_ref, None, gat_ref, None, ag_sems, me, group, group_dev)
    gat_ref[pl.ds(me, 1)] = fin_ref[...][None]
    total_ref[64:66, :] = total(zm_ref)
    total_ref[66:72, :] = jnp.zeros((6, 128), F32)
    landed(fin_ref, None, gat_ref, None, ag_sems, group, group_dev)
    for g in range(8):
        total_ref[8 * g : 8 * g + 8, :] = gat_ref[g]
    gone(halo + rows_out + cols_out + corners_out + shares_out)
    for c in rs + by_y + by_z + ag:
        c.wait_send()


def front(prior, spread, courant, cells, value, error):
    vmem, hbm = pl.BlockSpec(memory_space=pltpu.VMEM), pl.BlockSpec(memory_space=pl.ANY)
    dma = pltpu.SemaphoreType.DMA
    return pl.pallas_call(
        front_kernel,
        out_shape=(
            pltpu.VMEM((8, 128, 256), F32),
            pltpu.VMEM((8, 256), F32),
            pltpu.VMEM((72, 128), F32),
        ),
        in_specs=[hbm] * 6,
        out_specs=(vmem, vmem, vmem),
        scratch_shapes=[
            pltpu.VMEM((8, 256), F32),
            pltpu.VMEM((16, 256), F32),
            pltpu.VMEM((1, 128), jnp.int32),
            pltpu.VMEM((1, 128), F32),
            pltpu.VMEM((1, 128), F32),
            pltpu.VMEM((2, 1024, 128), F32),
            pltpu.VMEM((3, 12, 128, 128), F32),
            pltpu.VMEM((3, 10, 128, 128), F32),
            pltpu.VMEM((8, 128, 256), F32),
            pltpu.VMEM((8, 256, 128), BF16),
            pltpu.VMEM((3, 3, 16, 128), F32),
            pltpu.VMEM((5, 3, 16, 128), F32),
            pltpu.VMEM((2, 24, 128), F32),
            pltpu.VMEM((2, 24, 128), F32),
            pltpu.VMEM((2, 16, 128), F32),
            pltpu.VMEM((2, 2, 16, 128), F32),
            pltpu.VMEM((2, 2, 8, 128), F32),
            pltpu.VMEM((128, 128), F32),
            pltpu.VMEM((384, 128), F32),
            pltpu.VMEM((2, 128, 256), F32),
            pltpu.VMEM((2, 128, 128), F32),
            pltpu.VMEM((2, 128, 128), F32),
            pltpu.VMEM((8, 8, 128), F32),
            pltpu.VMEM((8, 8, 128), F32),
            pltpu.VMEM((8, 128), F32),
            pltpu.VMEM((8, 8, 128), F32),
            pltpu.VMEM((8, 128), F32),
            pltpu.VMEM((8, 8, 128), F32),
            pltpu.VMEM((8, 128), F32),
            pltpu.VMEM((8, 8, 128), F32),
            pltpu.VMEM((2, 128), F32),
            pltpu.VMEM((8, 2, 128), F32),
            pltpu.VMEM((2, 128), F32),
            pltpu.VMEM((8, 2, 128), F32),
            pltpu.VMEM((2, 128), F32),
            pltpu.VMEM((8, 2, 128), F32),
            dma((2 * CHUNKS,)),
            dma((5,)),
            dma((8,)),
            dma((8,)),
            dma((8,)),
            dma((8,)),
            dma((4, 8)),
            dma((4, 8)),
            dma((4, 8)),
            dma((4, 8)),
        ],
        compiler_params=pltpu.CompilerParams(collective_id=0, has_side_effects=True),
        name="front",
    )(prior, spread, courant, cells, value, error)


def body(
    prior_sample_fields, spreading_coefficient, transport_courant, obs_cells, obs_value, obs_error
):
    departures, mean, packed = front(
        prior_sample_fields.reshape(1024, 256),
        spreading_coefficient,
        transport_courant.reshape(16, 256),
        obs_cells[None, :],
        obs_value[None, :],
        obs_error[None, :],
    )
    return tail(packed, departures, mean).reshape(128, 8, 256)


def solution(mesh):
    split = Mesh(mesh.devices.reshape(8, 4, 8, 2), ("row_0", "row_1", "col_0", "col_1"))
    return jax.shard_map(
        body,
        mesh=split,
        in_specs=(
            P(None, ROW, COL),
            P(ROW, COL),
            P(None, ROW, COL),
            P(ROW_COL),
            P(ROW_COL),
            P(ROW_COL),
        ),
        out_specs=P(None, ROW, COL),
        check_vma=False,
    )
```

```python
import jax
import jax.numpy as jnp
from jax import lax
from jax.experimental import pallas as pl
from jax.experimental.pallas import tpu as pltpu
from jax.sharding import Mesh
from jax.sharding import PartitionSpec as P

ROW_COL = ("row_0", "row_1", "col_0", "col_1")
ROW = ("row_0", "row_1")
COL = ("col_0", "col_1")
F32 = jnp.float32
BF16 = jnp.bfloat16


def lane_spread(x, lane):
    return jnp.broadcast_to(x[:, lane : lane + 1], (8, 128))


def row_spread(x, row):
    return jnp.broadcast_to(x[row : row + 1, :], (8, 128))


def picked_row(x, mask):
    return jnp.broadcast_to(jnp.sum(jnp.where(mask, x, F32(0.0)), axis=0, keepdims=True), (8, 128))


def split2(x):
    hi = x.astype(BF16)
    lo = (x - hi.astype(F32)).astype(BF16)
    return hi, lo


def factor_rows(x_ref, d_ref):
    lanes = lax.broadcasted_iota(jnp.int32, (8, 128), 1)
    rows = lax.broadcasted_iota(jnp.int32, (8, 128), 0)
    for k in range(16):
        base = 8 * k
        p = x_ref[k]
        c = [lane_spread(p, base + j) for j in range(8)]
        a = {(i, j): picked_row(c[j], rows == i) for j in range(8) for i in range(j, 8)}
        in_block = (lanes >= base) & (lanes < base + 8)
        eye = jnp.where(lanes - base == rows, F32(1.0), F32(0.0))
        p0 = jnp.where(in_block, eye, p)
        pb = [row_spread(p0, i) for i in range(8)]
        inv = []
        pivots = jnp.zeros((8, 128), F32)
        low = {}
        for j in range(8):
            pivots = jnp.where(rows == j, a[j, j], pivots)
            r = 1.0 / a[j, j]
            inv.append(r)
            for i in range(j + 1, 8):
                low[i, j] = a[i, j] * r
            for i in range(j + 1, 8):
                for m in range(i, 8):
                    a[m, i] = a[m, i] - a[m, j] * low[i, j]
                pb[i] = pb[i] - low[i, j] * pb[j]
        done = pb[0]
        for i in range(1, 8):
            done = jnp.where(rows == i, pb[i], done)
        x_ref[k] = done
        d_ref[k] = pivots
        if k == 15:
            break
        q = x_ref[k + 1]
        cq = [lane_spread(q, base + j) for j in range(8)]
        q = jnp.where(in_block, F32(0.0), q)
        for j in range(8):
            mult = cq[j] * inv[j]
            q = q - mult * pb[j]
            for i in range(j + 1, 8):
                cq[i] = cq[i] - mult * a[i, j]
        x_ref[k + 1] = q
        if k == 14:
            continue
        minv = {}
        for j in range(8):
            for i in range(j):
                t = low[j, i]
                for m in range(i + 1, j):
                    t = t + low[j, m] * minv[m, i]
                minv[j, i] = -t
        z = []
        scaled = [pb[j] * inv[j] for j in range(8)]
        for i in range(8):
            t = scaled[i]
            for j in range(i + 1, 8):
                t = t + minv[j, i] * scaled[j]
            z.append(t)
        for t in range(k + 2, 16):
            q = x_ref[t]
            cq = [lane_spread(q, base + j) for j in range(8)]
            q = jnp.where(in_block, F32(0.0), q)
            s0 = cq[0] * z[0] + cq[1] * z[1]
            s1 = cq[2] * z[2] + cq[3] * z[3]
            s2 = cq[4] * z[4] + cq[5] * z[5]
            s3 = cq[6] * z[6] + cq[7] * z[7]
            x_ref[t] = q - ((s0 + s1) + (s2 + s3))


def tail_kernel(g_ref, dd_ref, mean_ref, out_hbm, x_ref, d_ref, o_ref, out_sem):
    lanes = lax.broadcasted_iota(jnp.int32, (8, 128), 1)
    rows = lax.broadcasted_iota(jnp.int32, (8, 128), 0)
    upper = g_ref[0:64, :]
    lanes64 = lax.broadcasted_iota(jnp.int32, (64, 128), 1)
    rows64 = lax.broadcasted_iota(jnp.int32, (64, 128), 0)
    half = jnp.concatenate(
        [
            jnp.where((lanes64 >= 64) | (lanes64 < rows64), upper, F32(0.0)),
            jnp.where(lanes64 - 64 > rows64, pltpu.roll(upper, 64, 1), F32(0.0)),
        ],
        axis=0,
    )
    gram = half + half.T
    diagonal = row_spread(g_ref[64:72, :], 1) + F32(1.0)
    for k in range(16):
        x_ref[k] = jnp.where(lanes - 8 * k == rows, diagonal, gram[8 * k : 8 * k + 8])
    factor_rows(x_ref, d_ref)
    pulled = row_spread(g_ref[64:72, :], 0)
    root = jnp.sqrt(F32(127.0))
    shift = jnp.zeros((8, 128), F32)
    kept = []
    for k in range(16):
        m = jnp.where(lanes - 8 * k <= rows, x_ref[k], F32(0.0))
        kept.append(m)
        y = jnp.sum(m * pulled, axis=1, keepdims=True)
        shift = shift + m * (jnp.broadcast_to(y, (8, 128)) / d_ref[k])
    shift = jnp.broadcast_to(jnp.sum(shift, axis=0, keepdims=True), (8, 128))
    w = []
    for k in range(16):
        w.append((kept[k] / jnp.sqrt(d_ref[k]) + shift) / root)
    w = jnp.concatenate(w, axis=0)
    whi, wlo = split2(w)
    both = jnp.concatenate([whi, wlo], axis=1)
    for r in range(8):
        hi, lo = split2(dd_ref[r])
        acc = jnp.dot(both, jnp.concatenate([hi, hi], axis=0), preferred_element_type=F32)
        acc = acc + jnp.dot(both, jnp.concatenate([lo, lo], axis=0), preferred_element_type=F32)
        acc = acc + mean_ref[r : r + 1, :]
        o_ref[0, pl.ds(r, 128, stride=8), :] = acc[:, 0:128]
        o_ref[1, pl.ds(r, 128, stride=8), :] = acc[:, 128:256]
    outs = [
        pltpu.make_async_copy(o_ref.at[n], out_hbm.at[:, pl.ds(128 * n, 128)], out_sem.at[n]) for n in range(2)
    ]
    for c in outs:
        c.start()
    for c in outs:
        c.wait()


def tail(g, departures, mean):
    return pl.pallas_call(
        tail_kernel,
        out_shape=jax.ShapeDtypeStruct((1024, 256), F32),
        in_specs=[
            pl.BlockSpec(memory_space=pltpu.VMEM),
            pl.BlockSpec(memory_space=pltpu.VMEM),
            pl.BlockSpec(memory_space=pltpu.VMEM),
        ],
        out_specs=pl.BlockSpec(memory_space=pl.ANY),
        scratch_shapes=[
            pltpu.VMEM((16, 8, 128), F32),
            pltpu.VMEM((16, 8, 128), F32),
            pltpu.VMEM((2, 1024, 128), F32),
            pltpu.SemaphoreType.DMA((2,)),
        ],
        compiler_params=pltpu.CompilerParams(vmem_limit_bytes=16 << 20),
        name="tail",
    )(g, departures, mean)


MESH_IDS = pl.DeviceIdType.MESH
HIGHEST = lax.Precision.HIGHEST
CHUNKS = 2
PART = 128 // CHUNKS


def send(src, dst, sems, slot, device, landed=None):
    landed = slot if landed is None else landed
    return pltpu.make_async_remote_copy(
        src_ref=src,
        dst_ref=dst,
        send_sem=sems[0].at[slot],
        recv_sem=sems[1].at[landed],
        device_id=device,
        device_id_type=MESH_IDS,
    )


def stencil(get, coef_ref, row, tiles, lanes):
    centre = [get(t, row) for t in range(3)]
    right_of = [pltpu.roll(v, 127, 1) for v in centre]
    left_of = [pltpu.roll(v, 1, 1) for v in centre]
    out = []
    for t in tiles:
        left = jnp.where(lanes == 0, left_of[(t + 2) % 3], left_of[t])
        right = jnp.where(lanes == 127, right_of[(t + 1) % 3], right_of[t])
        w = [coef_ref[n, t, row : row + 1, :] for n in range(5)]
        out.append(
            (w[0] * centre[t] + w[1] * get(t, row - 1)) + (w[2] * get(t, row + 1) + (w[3] * left + w[4] * right))
        )
    return out


def front_kernel(
    prior_hbm, spread_hbm, courant_hbm, cells_hbm, value_hbm, error_hbm,
    d_ref, mean_ref, total_ref,
    spread_ref, courant_ref, cells_ref, value_ref, error_ref,
    nat_ref, u_ref, f_ref, full_ref, pick_ref, raw_ref, coef_ref,
    edge_ref, colin_ref, rowc_ref, rowin_ref, cor_ref, comb_ref, acc_ref, give_ref, share_ref, shared_ref,
    part_ref, rs_ref, ysrc_ref, yin_ref, zsrc_ref, zin_ref, fin_ref, gat_ref,
    load_sem, tiny_sem, halo_s, halo_r, small_s, small_r, rs_sem, y_sem, z_sem, ag_sem,
):
    y, x = lax.axis_index("row_0"), lax.axis_index("row_1")
    z, core = lax.axis_index("col_0"), lax.axis_index("col_1")
    row, col = y * 4 + x, z * 2 + core

    def at_row(n):
        n = lax.rem(n + 32, 32)
        return (n // 4, lax.rem(n, 4), z, core)

    def at_col(n):
        n = lax.rem(n + 16, 16)
        return (y, x, n // 2, lax.rem(n, 2))

    def at_both(m, n):
        return at_row(m)[:2] + at_col(n)[2:]

    up, down, left, right = at_row(row - 1), at_row(row + 1), at_col(col - 1), at_col(col + 1)
    me = x * 2 + core
    far_first = (4, 3, 5, 2, 6, 1, 7)
    group = [lax.rem(me + i, 8) for i in far_first]
    group_dev = [(y, g // 2, z, lax.rem(g, 2)) for g in group]
    ys = [lax.rem(y + i, 8) for i in far_first]
    zs = [lax.rem(z + i, 8) for i in far_first]
    y_dev = [(n, x, z, core) for n in ys]
    z_dev = [(y, x, n, core) for n in zs]

    barrier = pltpu.get_barrier_semaphore()
    everyone = group_dev + y_dev + z_dev
    beside = {
        "up": up,
        "down": down,
        "left": left,
        "right": right,
        "up left": at_both(row - 1, col - 1),
        "up right": at_both(row - 1, col + 1),
        "down left": at_both(row + 1, col - 1),
        "down right": at_both(row + 1, col + 1),
    }
    there = {"up": row > 0, "down": row < 31, "left": col > 0, "right": col < 15}
    opposite = {"up": "down", "down": "up", "left": "right", "right": "left"}
    for v in ("up", "down"):
        for h in ("left", "right"):
            there[f"{v} {h}"] = there[v] & there[h]
            opposite[f"{v} {h}"] = f"{opposite[v]} {opposite[h]}"
    for way, device in beside.items():

        @pl.when(there[way])
        def _():
            pl.semaphore_signal(barrier, inc=1, device_id=device, device_id_type=MESH_IDS)

    for device in everyone:
        pl.semaphore_signal(barrier, inc=1, device_id=device, device_id_type=MESH_IDS)

    def each_way(items, act, turn=lambda way: way):
        for way in beside:
            some = [c for c, w in items if w == way]
            if some:

                @pl.when(there[turn(way)])
                def _():
                    for c in some:
                        act(c)

    def begin(items):
        each_way(items, lambda c: c.start())

    def arrived(items):
        each_way(items, lambda c: c.wait_recv(), lambda way: opposite[way])

    def gone(items):
        each_way(items, lambda c: c.wait_send())

    tiny = [
        pltpu.make_async_copy(src, dst, tiny_sem.at[n])
        for n, (src, dst) in enumerate(
            (
                (spread_hbm, spread_ref),
                (courant_hbm, courant_ref),
                (cells_hbm, cells_ref),
                (value_hbm, value_ref),
                (error_hbm, error_ref),
            )
        )
    ]
    loads = [
        pltpu.make_async_copy(
            prior_hbm.at[pl.ds(part * PART * 8, PART * 8), pl.ds(128 * t, 128)],
            nat_ref.at[t, pl.ds(part * PART * 8, PART * 8), :],
            load_sem.at[2 * part + t],
        )
        for part in range(CHUNKS)
        for t in range(2)
    ]
    for c in loads[:2] + tiny[:2] + loads[2:] + tiny[2:]:
        c.start()

    for side, way in enumerate(("up", "down")):

        @pl.when(jnp.logical_not(there[way]))
        def _():
            rowin_ref[side] = jnp.zeros((2, 16, 128), F32)
            shared_ref[side] = jnp.zeros((128, 128), F32)
            for t in range(2):
                for n in range(2):
                    u_ref[t, 10 * side + n] = jnp.zeros((128, 128), F32)

    for side, way in enumerate(("left", "right")):

        @pl.when(jnp.logical_not(there[way]))
        def _():
            colin_ref[side] = jnp.zeros((24, 128), F32)

    halo = []
    for part in range(2):
        some = pl.ds(part * 64, 64)
        for t in range(2):
            slot = part * 4 + t * 2
            sems = (halo_s, halo_r)
            halo.append((send(u_ref.at[t, 2:4, some, :], u_ref.at[t, 10:12, some, :], sems, slot, up), "up"))
            halo.append((send(u_ref.at[t, 8:10, some, :], u_ref.at[t, 0:2, some, :], sems, slot + 1, down), "down"))

    def spread_rows(part, which):
        for t in range(2):
            for r in which:
                u_ref[t, 2 + r, part * PART : part * PART + PART, :] = nat_ref[
                    t, pl.ds(part * PART * 8 + r, PART, stride=8), :
                ]

    for v in range(2):
        for h in range(2):

            @pl.when(jnp.logical_not(there[("up", "down")[v] + (" left", " right")[h]]))
            def _():
                cor_ref[v, h] = jnp.zeros((8, 128), F32)

    small = (small_s, small_r)
    for c in tiny:
        c.wait()

    lanes8 = lax.broadcasted_iota(jnp.int32, (8, 128), 1)
    for t in range(2):
        cut = slice(128 * t, 128 * t + 128)
        for n, block in enumerate((spread_ref[:, cut], courant_ref[0:8, cut], courant_ref[8:16, cut])):
            raw_ref[n, t, 1:9, :] = block
            rowc_ref[t, n : n + 1, :] = block[7:8, :]
            rowc_ref[t, n + 3 : n + 4, :] = block[0:1, :]
            if n < 2:
                rowc_ref[t, n + 6 : n + 7, :] = block[1:2, :]
            if n == 0:
                rowc_ref[t, 8:9, :] = block[6:7, :]
        rowc_ref[t, 9:10, :] = cells_ref[...].astype(F32)
        rowc_ref[t, 10:16, :] = jnp.zeros((6, 128), F32)
    rows_out = [
        (send(rowc_ref, rowin_ref.at[1], small, 0, up), "up"),
        (send(rowc_ref, rowin_ref.at[0], small, 1, down), "down"),
    ]
    rows_near = 2 - (32 - row) // 32 - (row + 1) // 32
    cols_near = 2 - (16 - col) // 16 - (col + 1) // 16
    pl.semaphore_wait(barrier, len(everyone) + rows_near + cols_near + rows_near * cols_near)
    begin(rows_out)
    edge = jnp.zeros((8, 128), F32)
    for n in range(3):
        last = spread_ref[:, 128:256] if n == 0 else courant_ref[8 * n - 8 : 8 * n, 128:256]
        first = spread_ref[:, 0:128] if n == 0 else courant_ref[8 * n - 8 : 8 * n, 0:128]
        edge = jnp.where(lanes8 == n, pltpu.roll(last, 1 + n, 1), edge)
        edge = jnp.where(lanes8 == n + 3, pltpu.roll(first, 3 + n, 1), edge)
    edge_ref[0, 16:24, :] = edge
    edge_ref[1, 16:24, :] = edge
    for part in range(CHUNKS):
        for c in loads[2 * part : 2 * part + 2]:
            c.wait()
        spread_rows(part, range(8))

    lanes = lax.broadcasted_iota(jnp.int32, (128, 128), 1)
    ends = jnp.zeros((128, 128), F32)
    for r in range(8):
        ends = jnp.where((lanes >> 1) == r, pltpu.roll(u_ref[1, 2 + r], 2 + 2 * r, 1), ends)
        ends = jnp.where((lanes >> 1) == r + 8, pltpu.roll(u_ref[0, 2 + r], 16 + 2 * r, 1), ends)
    ends = ends.T
    edge_ref[0, 0:16, :] = ends[0:16]
    edge_ref[1, 0:16, :] = ends[16:32]
    cols_out = [
        (send(edge_ref.at[0], colin_ref.at[0], small, 2, right), "right"),
        (send(edge_ref.at[1], colin_ref.at[1], small, 3, left), "left"),
    ]
    corners_out = [
        (send(edge_ref.at[0, 8:16, :], cor_ref.at[0, 0], small, 4, beside["down right"]), "down right"),
        (send(edge_ref.at[1, 8:16, :], cor_ref.at[0, 1], small, 5, beside["down left"]), "down left"),
        (send(edge_ref.at[0, 0:8, :], cor_ref.at[1, 0], small, 8, beside["up right"]), "up right"),
        (send(edge_ref.at[1, 0:8, :], cor_ref.at[1, 1], small, 9, beside["up left"]), "up left"),
    ]
    begin(cols_out + corners_out)
    begin(halo[:4])

    cells = cells_ref[...]
    places = lax.broadcasted_iota(jnp.int32, (256, 128), 0)
    for r in range(8):
        pick_ref[r] = jnp.where(places + 256 * r == cells, F32(1.0), F32(0.0)).astype(BF16)

    few = lax.broadcasted_iota(jnp.int32, (PART, 128), 1)
    thin = lax.broadcasted_iota(jnp.int32, (1, 128), 1)

    def sideways(k, t1, t):
        w_left, w_right = k + t1, k
        if t == 0:
            w_left = jnp.where(thin == 0, F32(0.0), w_left)
        else:
            w_right = jnp.where(thin == 127, F32(0.0), w_right)
        return w_left, w_right

    def exact_parts(v):
        hi = v.astype(BF16)
        rest = v - hi.astype(F32)
        mid = rest.astype(BF16)
        lo = (rest - mid.astype(F32)).astype(BF16)
        return jnp.concatenate([hi, mid, lo], axis=0)

    arrived(rows_out)
    for side in range(2):
        a, b = ((8, 9), (3, 2))[side]
        mine = b - 1
        theirs, first = ((1, 3), (0, 0))[side]
        w = []
        for t in range(2):
            k, t0, t1 = (raw_ref[n, t, mine : mine + 1, :] for n in range(3))
            own = (1.0 - 4.0 * k - t0 - t1, k + t0 if side == 0 else k) + sideways(k, t1, t)
            k, t0, t1 = (rowin_ref[theirs, t, first + n : first + n + 1, :] for n in range(3))
            near = (1.0 - 4.0 * k - t0 - t1, k + t0 if side == 0 else k) + sideways(k, t1, t)
            if side == 0:
                far = rowin_ref[theirs, t, 6:7, :] + rowin_ref[theirs, t, 7:8, :]
            else:
                far = rowin_ref[theirs, t, 8:9, :]
            w.append((own, near, far))
        for part in range(CHUNKS):
            some = slice(part * PART, part * PART + PART)
            ub = [u_ref[t, b, some, :] for t in range(2)]
            h = [w[t][1][1] * ub[t] for t in range(2)]
            b_left, b_right = [pltpu.roll(v, 1, 1) for v in ub], [pltpu.roll(v, 127, 1) for v in ub]
            h_left, h_right = [pltpu.roll(v, 1, 1) for v in h], [pltpu.roll(v, 127, 1) for v in h]

            def ends_of(before, after, t):
                if t == 0:
                    return before[0], jnp.where(few == 127, after[1], after[0])
                return jnp.where(few == 0, before[0], before[1]), after[1]

            for t in range(2):
                own, near, far = w[t]
                bl, br = ends_of(b_left, b_right, t)
                hl, hr = ends_of(h_left, h_right, t)
                g = (own[0] * ub[t] + own[1] * u_ref[t, a, some, :]) + (own[2] * bl + own[3] * br)
                cut = slice(128 * t, 128 * t + 128)
                give_ref[0, some, cut] = (near[0] * h[t] + near[1] * g) + (near[2] * hl + near[3] * hr)
                give_ref[1, some, cut] = far * h[t]
        their_cells = rowin_ref[theirs, 0, 9:10, :]
        spots = places.astype(F32)
        got = jnp.zeros((384, 128), F32)
        for n, base in enumerate(((0, 256), (1792, 1536))[side]):
            chosen = jnp.where(spots + F32(base) == their_cells, F32(1.0), F32(0.0)).astype(BF16)
            got = got + jnp.dot(exact_parts(give_ref[n]), chosen, preferred_element_type=F32)
        share_ref[side] = (got[0:128] + got[128:256]) + got[256:384]

    shares_out = [
        (send(share_ref.at[0], shared_ref.at[0], small, 6, down), "down"),
        (send(share_ref.at[1], shared_ref.at[1], small, 7, up), "up"),
    ]
    begin(shares_out)
    begin(halo[4:])
    arrived(cols_out)

    for n in range(3):
        for t in range(2):
            raw_ref[n, t, 0:1, :] = rowin_ref[0, t, n : n + 1, :]
            raw_ref[n, t, 9:10, :] = rowin_ref[1, t, n + 3 : n + 4, :]
        beyond = jnp.where(
            lanes8 == 127,
            pltpu.roll(colin_ref[0, 16:24, :], 127 - n, 1),
            pltpu.roll(colin_ref[1, 16:24, :], 125 - n, 1),
        )
        raw_ref[n, 2, 0:1, :] = jnp.zeros((1, 128), F32)
        raw_ref[n, 2, 1:9, :] = jnp.where((lanes8 == 127) | (lanes8 == 0), beyond, F32(0.0))
        raw_ref[n, 2, 9:10, :] = jnp.zeros((1, 128), F32)
    wide = lax.broadcasted_iota(jnp.int32, (10, 128), 1)
    deep = lax.broadcasted_iota(jnp.int32, (10, 128), 0)
    for t in range(3):
        k, t0, t1 = (raw_ref[n, t, 0:10, :] for n in range(3))
        zero = jnp.zeros_like(k)
        coef_ref[0, t, 0:10, :] = 1.0 - 4.0 * k - t0 - t1
        coef_ref[1, t, 0:10, :] = jnp.where((deep == 1) & (row == 0), zero, k + t0)
        coef_ref[2, t, 0:10, :] = jnp.where((deep == 8) & (row == 31), zero, k)
        w_left, w_right = k + t1, k
        if t == 0:
            w_left = jnp.where((wide == 0) & (col == 0), zero, w_left)
        if t == 1:
            w_right = jnp.where((wide == 127) & (col == 15), zero, w_right)
        coef_ref[3, t, 0:10, :] = w_left
        coef_ref[4, t, 0:10, :] = w_right

    comb_ref[...] = jnp.zeros((128, 128), F32)
    for r in range(8):
        comb_ref[4 * r + 4 : 4 * r + 6, :] = colin_ref[0, 2 * r : 2 * r + 2, :]
        comb_ref[4 * r + 6 : 4 * r + 8, :] = colin_ref[1, 2 * r : 2 * r + 2, :]
    turned = comb_ref[...].T
    for n in range(1, 9):
        u_ref[2, n + 1] = pltpu.roll(turned, (126 - 4 * n) % 128, 1)

    def first_step(some, n, all_rows):
        tiles = range(3) if 1 <= n <= 8 else range(2)

        def get(t, i):
            if not all_rows and (i in (-1, 10) or (i in (0, 9) and t < 2)):
                return jnp.zeros((PART, 128), F32)
            return u_ref[t, i + 1, some, :]

        for t, v in zip(tiles, stencil(get, coef_ref, n, tiles, few)):
            f_ref[t, n, some, :] = v

    def second_step(some, n):
        for t, v in zip(range(2), stencil(lambda t, i: f_ref[t, i, some, :], coef_ref, n, range(2), few)):
            full_ref[n - 1, some, 128 * t : 128 * t + 128] = v

    @pl.loop(0, CHUNKS)
    def _(part):
        some = pl.ds(pl.multiple_of(part * PART, PART), PART)
        for n in range(2, 8):
            first_step(some, n, False)
        for n in range(3, 7):
            second_step(some, n)

    def observe(n):
        return jnp.dot(exact_parts(full_ref[n]), pick_ref[n], preferred_element_type=F32)

    acc_ref[...] = (observe(2) + observe(3)) + (observe(4) + observe(5))

    arrived(corners_out)
    for side in range(2):
        comb_ref[2 * side : 2 * side + 2, :] = cor_ref[0, side, 6:8, :]
        comb_ref[36 + 2 * side : 38 + 2 * side, :] = cor_ref[1, side, 0:2, :]
    turned = comb_ref[...].T
    for n in (0, 9):
        u_ref[2, n + 1] = pltpu.roll(turned, (126 - 4 * n) % 128, 1)

    def end_rows(some, all_rows):
        for n in (0, 1, 8, 9):
            first_step(some, n, all_rows)
        for n in (1, 2, 7, 8):
            second_step(some, n)

    @pl.loop(0, CHUNKS)
    def _(part):
        end_rows(pl.ds(pl.multiple_of(part * PART, PART), PART), False)

    seen = acc_ref[...] + ((observe(0) + observe(1)) + (observe(6) + observe(7)))
    arrived(shares_out)
    observed = ((seen[0:128] + seen[128:256]) + seen[256:384]) + (shared_ref[0] + shared_ref[1])
    obs_mean = jnp.sum(observed, axis=0, keepdims=True) * F32(1.0 / 128.0)
    err = error_ref[...]
    scaled = (observed - obs_mean) / (err * jnp.sqrt(F32(127.0)))
    innovation = jnp.broadcast_to((value_ref[...] - obs_mean) / err, (8, 128))
    turned_dot = (((1,), (1,)), ((), ()))
    gram = lax.dot_general(scaled, scaled, turned_dot, precision=HIGHEST, preferred_element_type=F32)
    pulled = lax.dot_general(innovation, scaled, turned_dot, precision=HIGHEST, preferred_element_type=F32)
    deep128 = lax.broadcasted_iota(jnp.int32, (128, 128), 0)
    diagonal = jnp.sum(jnp.where(lanes == deep128, gram, F32(0.0)), axis=0, keepdims=True)
    rows8 = lax.broadcasted_iota(jnp.int32, (8, 128), 0)
    folded = pltpu.roll(gram[64:128], 64, 1)
    for g in range(8):
        cut = slice(8 * g, 8 * g + 8)
        keep = (lanes8 >= 64) | (lanes8 < rows8 + 8 * g)
        part_ref[g, 0:8, :] = jnp.where(keep, gram[cut], folded[cut])
        part_ref[g, 8:9, :] = pulled[0:1]
        part_ref[g, 9:10, :] = diagonal

    def exchange(main, into, sems, place, ids, devs):
        out = [send(main(n), into.at[place], (sems.at[0], sems.at[1]), n, dev, landed=place) for n, dev in zip(ids, devs)]
        for c in out:
            c.start()
        return out

    def landed(main, into, sems, ids, devs):
        for n, dev in zip(ids, devs):
            send(main, into.at[n], (sems.at[0], sems.at[1]), n, dev).wait_recv()

    def total(buf):
        return ((buf[0] + buf[1]) + (buf[2] + buf[3])) + ((buf[4] + buf[5]) + (buf[6] + buf[7]))

    rs = exchange(lambda n: part_ref.at[n], rs_ref, rs_sem, me, group, group_dev)
    rs_ref[pl.ds(me, 1)] = part_ref[pl.ds(me, 1)]

    def depart(rows):
        for r in rows:
            v = full_ref[r]
            mean = jnp.sum(v, axis=0, keepdims=True) * F32(1.0 / 128.0)
            mean_ref[r : r + 1, :] = mean
            d_ref[r] = v - mean

    def finish_rows(half):
        arrived(halo[4 * half : 4 * half + 4])

        @pl.loop(half * (CHUNKS // 2), (half + 1) * (CHUNKS // 2))
        def _(part):
            end_rows(pl.ds(pl.multiple_of(part * PART, PART), PART), True)

    depart(range(2, 6))

    landed(part_ref.at[0], rs_ref, rs_sem, group, group_dev)
    ysrc_ref[...] = total(rs_ref)
    by_y = exchange(lambda n: ysrc_ref, yin_ref, y_sem, y, ys, y_dev)
    yin_ref[pl.ds(y, 1)] = ysrc_ref[...][None]
    finish_rows(0)
    landed(ysrc_ref, yin_ref, y_sem, ys, y_dev)
    zsrc_ref[...] = total(yin_ref)
    by_z = exchange(lambda n: zsrc_ref, zin_ref, z_sem, z, zs, z_dev)
    zin_ref[pl.ds(z, 1)] = zsrc_ref[...][None]
    finish_rows(1)
    depart((0, 1, 6, 7))
    landed(zsrc_ref, zin_ref, z_sem, zs, z_dev)
    whole = total(zin_ref)
    fin_ref[...] = whole[0:8]
    ag = exchange(lambda n: fin_ref, gat_ref, ag_sem, me, group, group_dev)
    gat_ref[pl.ds(me, 1)] = fin_ref[...][None]
    total_ref[64:66, :] = whole[8:10]
    total_ref[66:72, :] = jnp.zeros((6, 128), F32)
    landed(fin_ref, gat_ref, ag_sem, group, group_dev)
    for g in range(8):
        total_ref[8 * g : 8 * g + 8, :] = gat_ref[g]
    gone(halo + rows_out + cols_out + corners_out + shares_out)
    for c in rs + by_y + by_z + ag:
        c.wait_send()


def front(prior, spread, courant, cells, value, error):
    vmem, hbm = pl.BlockSpec(memory_space=pltpu.VMEM), pl.BlockSpec(memory_space=pl.ANY)
    dma = pltpu.SemaphoreType.DMA
    return pl.pallas_call(
        front_kernel,
        out_shape=(
            pltpu.VMEM((8, 128, 256), F32),
            pltpu.VMEM((8, 256), F32),
            pltpu.VMEM((72, 128), F32),
        ),
        in_specs=[hbm] * 6,
        out_specs=(vmem, vmem, vmem),
        scratch_shapes=[
            pltpu.VMEM((8, 256), F32),
            pltpu.VMEM((16, 256), F32),
            pltpu.VMEM((1, 128), jnp.int32),
            pltpu.VMEM((1, 128), F32),
            pltpu.VMEM((1, 128), F32),
            pltpu.VMEM((2, 1024, 128), F32),
            pltpu.VMEM((3, 12, 128, 128), F32),
            pltpu.VMEM((3, 10, 128, 128), F32),
            pltpu.VMEM((8, 128, 256), F32),
            pltpu.VMEM((8, 256, 128), BF16),
            pltpu.VMEM((3, 3, 16, 128), F32),
            pltpu.VMEM((5, 3, 16, 128), F32),
            pltpu.VMEM((2, 24, 128), F32),
            pltpu.VMEM((2, 24, 128), F32),
            pltpu.VMEM((2, 16, 128), F32),
            pltpu.VMEM((2, 2, 16, 128), F32),
            pltpu.VMEM((2, 2, 8, 128), F32),
            pltpu.VMEM((128, 128), F32),
            pltpu.VMEM((384, 128), F32),
            pltpu.VMEM((2, 128, 256), F32),
            pltpu.VMEM((2, 128, 128), F32),
            pltpu.VMEM((2, 128, 128), F32),
            pltpu.VMEM((8, 10, 128), F32),
            pltpu.VMEM((8, 10, 128), F32),
            pltpu.VMEM((10, 128), F32),
            pltpu.VMEM((8, 10, 128), F32),
            pltpu.VMEM((10, 128), F32),
            pltpu.VMEM((8, 10, 128), F32),
            pltpu.VMEM((8, 128), F32),
            pltpu.VMEM((8, 8, 128), F32),
            dma((2 * CHUNKS,)),
            dma((5,)),
            dma((8,)),
            dma((8,)),
            dma((10,)),
            dma((10,)),
            dma((2, 8)),
            dma((2, 8)),
            dma((2, 8)),
            dma((2, 8)),
        ],
        compiler_params=pltpu.CompilerParams(collective_id=0, has_side_effects=True),
        name="front",
    )(prior, spread, courant, cells, value, error)


def body(
    prior_sample_fields, spreading_coefficient, transport_courant, obs_cells, obs_value, obs_error
):
    departures, mean, packed = front(
        prior_sample_fields.reshape(1024, 256),
        spreading_coefficient,
        transport_courant.reshape(16, 256),
        obs_cells[None, :],
        obs_value[None, :],
        obs_error[None, :],
    )
    return tail(packed, departures, mean).reshape(128, 8, 256)


def solution(mesh):
    split = Mesh(mesh.devices.reshape(8, 4, 8, 2), ("row_0", "row_1", "col_0", "col_1"))
    return jax.shard_map(
        body,
        mesh=split,
        in_specs=(
            P(None, ROW, COL),
            P(ROW, COL),
            P(None, ROW, COL),
            P(ROW_COL),
            P(ROW_COL),
            P(ROW_COL),
        ),
        out_specs=P(None, ROW, COL),
        check_vma=False,
    )
```

```python
import jax
import jax.numpy as jnp
from jax import lax
from jax.experimental import pallas as pl
from jax.experimental.pallas import tpu as pltpu
from jax.sharding import Mesh
from jax.sharding import PartitionSpec as P

ROW_COL = ("row_0", "row_1", "col_0", "col_1")
ROW = ("row_0", "row_1")
COL = ("col_0", "col_1")
F32 = jnp.float32
BF16 = jnp.bfloat16


def lane_spread(x, lane):
    return jnp.broadcast_to(x[:, lane : lane + 1], (8, 128))


def row_spread(x, row):
    return jnp.broadcast_to(x[row : row + 1, :], (8, 128))


def picked_row(x, mask):
    return jnp.broadcast_to(jnp.sum(jnp.where(mask, x, F32(0.0)), axis=0, keepdims=True), (8, 128))


def split2(x):
    hi = x.astype(BF16)
    lo = (x - hi.astype(F32)).astype(BF16)
    return hi, lo


def factor_rows(x_ref, d_ref):
    lanes = lax.broadcasted_iota(jnp.int32, (8, 128), 1)
    rows = lax.broadcasted_iota(jnp.int32, (8, 128), 0)
    for k in range(16):
        base = 8 * k
        p = x_ref[k]
        c = [lane_spread(p, base + j) for j in range(8)]
        a = {(i, j): picked_row(c[j], rows == i) for j in range(8) for i in range(j, 8)}
        in_block = (lanes >= base) & (lanes < base + 8)
        eye = jnp.where(lanes - base == rows, F32(1.0), F32(0.0))
        p0 = jnp.where(in_block, eye, p)
        pb = [row_spread(p0, i) for i in range(8)]
        inv = []
        pivots = jnp.zeros((8, 128), F32)
        low = {}
        for j in range(8):
            pivots = jnp.where(rows == j, a[j, j], pivots)
            r = 1.0 / a[j, j]
            inv.append(r)
            for i in range(j + 1, 8):
                low[i, j] = a[i, j] * r
            for i in range(j + 1, 8):
                for m in range(i, 8):
                    a[m, i] = a[m, i] - a[m, j] * low[i, j]
                pb[i] = pb[i] - low[i, j] * pb[j]
        done = pb[0]
        for i in range(1, 8):
            done = jnp.where(rows == i, pb[i], done)
        x_ref[k] = done
        d_ref[k] = pivots
        if k == 15:
            break
        q = x_ref[k + 1]
        cq = [lane_spread(q, base + j) for j in range(8)]
        q = jnp.where(in_block, F32(0.0), q)
        for j in range(8):
            mult = cq[j] * inv[j]
            q = q - mult * pb[j]
            for i in range(j + 1, 8):
                cq[i] = cq[i] - mult * a[i, j]
        x_ref[k + 1] = q
        if k == 14:
            continue
        minv = {}
        for j in range(8):
            for i in range(j):
                t = low[j, i]
                for m in range(i + 1, j):
                    t = t + low[j, m] * minv[m, i]
                minv[j, i] = -t
        z = []
        scaled = [pb[j] * inv[j] for j in range(8)]
        for i in range(8):
            t = scaled[i]
            for j in range(i + 1, 8):
                t = t + minv[j, i] * scaled[j]
            z.append(t)
        for t in range(k + 2, 16):
            q = x_ref[t]
            cq = [lane_spread(q, base + j) for j in range(8)]
            q = jnp.where(in_block, F32(0.0), q)
            s0 = cq[0] * z[0] + cq[1] * z[1]
            s1 = cq[2] * z[2] + cq[3] * z[3]
            s2 = cq[4] * z[4] + cq[5] * z[5]
            s3 = cq[6] * z[6] + cq[7] * z[7]
            x_ref[t] = q - ((s0 + s1) + (s2 + s3))


def tail_kernel(g_ref, dd_ref, mean_ref, out_hbm, x_ref, d_ref, o_ref, out_sem):
    lanes = lax.broadcasted_iota(jnp.int32, (8, 128), 1)
    rows = lax.broadcasted_iota(jnp.int32, (8, 128), 0)
    upper = g_ref[0:64, :]
    lanes64 = lax.broadcasted_iota(jnp.int32, (64, 128), 1)
    rows64 = lax.broadcasted_iota(jnp.int32, (64, 128), 0)
    half = jnp.concatenate(
        [
            jnp.where((lanes64 >= 64) | (lanes64 < rows64), upper, F32(0.0)),
            jnp.where(lanes64 - 64 > rows64, pltpu.roll(upper, 64, 1), F32(0.0)),
        ],
        axis=0,
    )
    gram = half + half.T
    diagonal = row_spread(g_ref[64:72, :], 1) + F32(1.0)
    for k in range(16):
        x_ref[k] = jnp.where(lanes - 8 * k == rows, diagonal, gram[8 * k : 8 * k + 8])
    factor_rows(x_ref, d_ref)
    pulled = row_spread(g_ref[64:72, :], 0)
    root = jnp.sqrt(F32(127.0))
    shift = jnp.zeros((8, 128), F32)
    kept = []
    for k in range(16):
        m = jnp.where(lanes - 8 * k <= rows, x_ref[k], F32(0.0))
        kept.append(m)
        y = jnp.sum(m * pulled, axis=1, keepdims=True)
        shift = shift + m * (jnp.broadcast_to(y, (8, 128)) / d_ref[k])
    shift = jnp.broadcast_to(jnp.sum(shift, axis=0, keepdims=True), (8, 128))
    w = []
    for k in range(16):
        w.append((kept[k] / jnp.sqrt(d_ref[k]) + shift) / root)
    w = jnp.concatenate(w, axis=0)
    whi, wlo = split2(w)
    both = jnp.concatenate([whi, wlo], axis=1)
    for r in range(8):
        hi, lo = split2(dd_ref[r])
        acc = jnp.dot(both, jnp.concatenate([hi, hi], axis=0), preferred_element_type=F32)
        acc = acc + jnp.dot(both, jnp.concatenate([lo, lo], axis=0), preferred_element_type=F32)
        acc = acc + mean_ref[r : r + 1, :]
        o_ref[0, pl.ds(r, 128, stride=8), :] = acc[:, 0:128]
        o_ref[1, pl.ds(r, 128, stride=8), :] = acc[:, 128:256]
    outs = [
        pltpu.make_async_copy(o_ref.at[n], out_hbm.at[:, pl.ds(128 * n, 128)], out_sem.at[n]) for n in range(2)
    ]
    for c in outs:
        c.start()
    for c in outs:
        c.wait()


def tail(g, departures, mean):
    return pl.pallas_call(
        tail_kernel,
        out_shape=jax.ShapeDtypeStruct((1024, 256), F32),
        in_specs=[
            pl.BlockSpec(memory_space=pltpu.VMEM),
            pl.BlockSpec(memory_space=pltpu.VMEM),
            pl.BlockSpec(memory_space=pltpu.VMEM),
        ],
        out_specs=pl.BlockSpec(memory_space=pl.ANY),
        scratch_shapes=[
            pltpu.VMEM((16, 8, 128), F32),
            pltpu.VMEM((16, 8, 128), F32),
            pltpu.VMEM((2, 1024, 128), F32),
            pltpu.SemaphoreType.DMA((2,)),
        ],
        compiler_params=pltpu.CompilerParams(vmem_limit_bytes=16 << 20),
        name="tail",
    )(g, departures, mean)


MESH_IDS = pl.DeviceIdType.MESH
HIGHEST = lax.Precision.HIGHEST
CHUNKS = 2
PART = 128 // CHUNKS


def send(src, dst, sems, slot, device, landed=None):
    landed = slot if landed is None else landed
    return pltpu.make_async_remote_copy(
        src_ref=src,
        dst_ref=dst,
        send_sem=sems[0].at[slot],
        recv_sem=sems[1].at[landed],
        device_id=device,
        device_id_type=MESH_IDS,
    )


def stencil(get, coef_ref, row, tiles, lanes):
    centre = [get(t, row) for t in range(3)]
    right_of = [pltpu.roll(v, 127, 1) for v in centre]
    left_of = [pltpu.roll(v, 1, 1) for v in centre]
    out = []
    for t in tiles:
        left = jnp.where(lanes == 0, left_of[(t + 2) % 3], left_of[t])
        right = jnp.where(lanes == 127, right_of[(t + 1) % 3], right_of[t])
        w = [coef_ref[n, t, row : row + 1, :] for n in range(5)]
        out.append(
            (w[0] * centre[t] + w[1] * get(t, row - 1)) + (w[2] * get(t, row + 1) + (w[3] * left + w[4] * right))
        )
    return out


def front_kernel(
    prior_hbm, spread_hbm, courant_hbm, cells_hbm, value_hbm, error_hbm,
    d_ref, mean_ref, total_ref,
    spread_ref, courant_ref, cells_ref, value_ref, error_ref,
    nat_ref, u_ref, f_ref, full_ref, pick_ref, raw_ref, coef_ref,
    edge_ref, colin_ref, rowc_ref, rowin_ref, cor_ref, comb_ref, acc_ref, give_ref, share_ref, shared_ref,
    part_ref, rs_ref, ysrc_ref, yin_ref, zsrc_ref, zin_ref, fin_ref, gat_ref,
    load_sem, tiny_sem, halo_s, halo_r, small_s, small_r, rs_sem, y_sem, z_sem, ag_sem,
):
    y, x = lax.axis_index("row_0"), lax.axis_index("row_1")
    z, core = lax.axis_index("col_0"), lax.axis_index("col_1")
    row, col = y * 4 + x, z * 2 + core

    def at_row(n):
        n = lax.rem(n + 32, 32)
        return (n // 4, lax.rem(n, 4), z, core)

    def at_col(n):
        n = lax.rem(n + 16, 16)
        return (y, x, n // 2, lax.rem(n, 2))

    def at_both(m, n):
        return at_row(m)[:2] + at_col(n)[2:]

    up, down, left, right = at_row(row - 1), at_row(row + 1), at_col(col - 1), at_col(col + 1)
    me = x * 2 + core
    far_first = (4, 3, 5, 2, 6, 1, 7)
    group = [lax.rem(me + i, 8) for i in far_first]
    group_dev = [(y, g // 2, z, lax.rem(g, 2)) for g in group]
    ys = [lax.rem(y + i, 8) for i in far_first]
    zs = [lax.rem(z + i, 8) for i in far_first]
    y_dev = [(n, x, z, core) for n in ys]
    z_dev = [(y, x, n, core) for n in zs]

    barrier = pltpu.get_barrier_semaphore()
    everyone = group_dev + y_dev + z_dev
    beside = {
        "up": up,
        "down": down,
        "left": left,
        "right": right,
        "up left": at_both(row - 1, col - 1),
        "up right": at_both(row - 1, col + 1),
        "down left": at_both(row + 1, col - 1),
        "down right": at_both(row + 1, col + 1),
    }
    there = {"up": row > 0, "down": row < 31, "left": col > 0, "right": col < 15}
    opposite = {"up": "down", "down": "up", "left": "right", "right": "left"}
    for v in ("up", "down"):
        for h in ("left", "right"):
            there[f"{v} {h}"] = there[v] & there[h]
            opposite[f"{v} {h}"] = f"{opposite[v]} {opposite[h]}"
    for way, device in beside.items():

        @pl.when(there[way])
        def _():
            pl.semaphore_signal(barrier, inc=1, device_id=device, device_id_type=MESH_IDS)

    for device in everyone:
        pl.semaphore_signal(barrier, inc=1, device_id=device, device_id_type=MESH_IDS)

    def each_way(items, act, turn=lambda way: way):
        for way in beside:
            some = [c for c, w in items if w == way]
            if some:

                @pl.when(there[turn(way)])
                def _():
                    for c in some:
                        act(c)

    def begin(items):
        each_way(items, lambda c: c.start())

    def arrived(items):
        each_way(items, lambda c: c.wait_recv(), lambda way: opposite[way])

    def gone(items):
        each_way(items, lambda c: c.wait_send())

    tiny = [
        pltpu.make_async_copy(src, dst, tiny_sem.at[n])
        for n, (src, dst) in enumerate(
            (
                (spread_hbm, spread_ref),
                (courant_hbm, courant_ref),
                (cells_hbm, cells_ref),
                (value_hbm, value_ref),
                (error_hbm, error_ref),
            )
        )
    ]
    loads = [
        pltpu.make_async_copy(
            prior_hbm.at[pl.ds(part * PART * 8, PART * 8), pl.ds(128 * t, 128)],
            nat_ref.at[t, pl.ds(part * PART * 8, PART * 8), :],
            load_sem.at[2 * part + t],
        )
        for part in range(CHUNKS)
        for t in range(2)
    ]
    for c in loads[:2] + tiny[:2] + loads[2:] + tiny[2:]:
        c.start()

    for side, way in enumerate(("up", "down")):

        @pl.when(jnp.logical_not(there[way]))
        def _():
            rowin_ref[side] = jnp.zeros((2, 8, 128), F32)
            shared_ref[side] = jnp.zeros((128, 128), F32)
            for t in range(2):
                for n in range(2):
                    u_ref[t, 10 * side + n] = jnp.zeros((128, 128), F32)

    for side, way in enumerate(("left", "right")):

        @pl.when(jnp.logical_not(there[way]))
        def _():
            colin_ref[side] = jnp.zeros((24, 128), F32)

    halo = []
    for part in range(2):
        some = pl.ds(part * 64, 64)
        for t in range(2):
            slot = part * 4 + t * 2
            sems = (halo_s, halo_r)
            halo.append((send(u_ref.at[t, 2:4, some, :], u_ref.at[t, 10:12, some, :], sems, slot, up), "up"))
            halo.append((send(u_ref.at[t, 8:10, some, :], u_ref.at[t, 0:2, some, :], sems, slot + 1, down), "down"))

    def spread_rows(part, which):
        for t in range(2):
            for r in which:
                u_ref[t, 2 + r, part * PART : part * PART + PART, :] = nat_ref[
                    t, pl.ds(part * PART * 8 + r, PART, stride=8), :
                ]

    for v in range(2):
        for h in range(2):

            @pl.when(jnp.logical_not(there[("up", "down")[v] + (" left", " right")[h]]))
            def _():
                cor_ref[v, h] = jnp.zeros((8, 128), F32)

    small = (small_s, small_r)
    for c in tiny:
        c.wait()

    lanes8 = lax.broadcasted_iota(jnp.int32, (8, 128), 1)
    for t in range(2):
        cut = slice(128 * t, 128 * t + 128)
        for n, block in enumerate((spread_ref[:, cut], courant_ref[0:8, cut], courant_ref[8:16, cut])):
            raw_ref[n, t, 1:9, :] = block
            rowc_ref[0, t, n : n + 1, :] = block[0:1, :]
            rowc_ref[1, t, n : n + 1, :] = block[7:8, :]
            if n < 2:
                rowc_ref[0, t, n + 3 : n + 4, :] = block[1:2, :]
            if n == 0:
                rowc_ref[1, t, 3:4, :] = block[6:7, :]
        for way in range(2):
            rowc_ref[way, t, 5:6, :] = cells_ref[...].astype(F32)
            rowc_ref[way, t, 6:8, :] = jnp.zeros((2, 128), F32)
        rowc_ref[1, t, 4:5, :] = jnp.zeros((1, 128), F32)
    rows_out = [
        (send(rowc_ref.at[0], rowin_ref.at[1], small, 0, up), "up"),
        (send(rowc_ref.at[1], rowin_ref.at[0], small, 1, down), "down"),
    ]
    rows_near = 2 - (32 - row) // 32 - (row + 1) // 32
    cols_near = 2 - (16 - col) // 16 - (col + 1) // 16
    pl.semaphore_wait(barrier, len(everyone) + rows_near + cols_near + rows_near * cols_near)
    begin(rows_out)
    edge = jnp.zeros((8, 128), F32)
    for n in range(3):
        last = spread_ref[:, 128:256] if n == 0 else courant_ref[8 * n - 8 : 8 * n, 128:256]
        first = spread_ref[:, 0:128] if n == 0 else courant_ref[8 * n - 8 : 8 * n, 0:128]
        edge = jnp.where(lanes8 == n, pltpu.roll(last, 1 + n, 1), edge)
        edge = jnp.where(lanes8 == n + 3, pltpu.roll(first, 3 + n, 1), edge)
    edge_ref[0, 16:24, :] = edge
    edge_ref[1, 16:24, :] = edge
    for part in range(CHUNKS):
        for c in loads[2 * part : 2 * part + 2]:
            c.wait()
        spread_rows(part, range(8))

    lanes = lax.broadcasted_iota(jnp.int32, (128, 128), 1)
    ends = jnp.zeros((128, 128), F32)
    for r in range(8):
        ends = jnp.where((lanes >> 1) == r, pltpu.roll(u_ref[1, 2 + r], 2 + 2 * r, 1), ends)
        ends = jnp.where((lanes >> 1) == r + 8, pltpu.roll(u_ref[0, 2 + r], 16 + 2 * r, 1), ends)
    ends = ends.T
    edge_ref[0, 0:16, :] = ends[0:16]
    edge_ref[1, 0:16, :] = ends[16:32]
    cols_out = [
        (send(edge_ref.at[0], colin_ref.at[0], small, 2, right), "right"),
        (send(edge_ref.at[1], colin_ref.at[1], small, 3, left), "left"),
    ]
    corners_out = [
        (send(edge_ref.at[0, 8:16, :], cor_ref.at[0, 0], small, 4, beside["down right"]), "down right"),
        (send(edge_ref.at[1, 8:16, :], cor_ref.at[0, 1], small, 5, beside["down left"]), "down left"),
        (send(edge_ref.at[0, 0:8, :], cor_ref.at[1, 0], small, 8, beside["up right"]), "up right"),
        (send(edge_ref.at[1, 0:8, :], cor_ref.at[1, 1], small, 9, beside["up left"]), "up left"),
    ]
    begin(cols_out + corners_out)
    begin(halo[:4])

    cells = cells_ref[...]
    places = lax.broadcasted_iota(jnp.int32, (256, 128), 0)
    for r in range(8):
        pick_ref[r] = jnp.where(places + 256 * r == cells, F32(1.0), F32(0.0)).astype(BF16)

    few = lax.broadcasted_iota(jnp.int32, (PART, 128), 1)
    thin = lax.broadcasted_iota(jnp.int32, (1, 128), 1)

    def sideways(k, t1, t):
        w_left, w_right = k + t1, k
        if t == 0:
            w_left = jnp.where(thin == 0, F32(0.0), w_left)
        else:
            w_right = jnp.where(thin == 127, F32(0.0), w_right)
        return w_left, w_right

    def exact_parts(v):
        hi = v.astype(BF16)
        rest = v - hi.astype(F32)
        mid = rest.astype(BF16)
        lo = (rest - mid.astype(F32)).astype(BF16)
        return jnp.concatenate([hi, mid, lo], axis=0)

    arrived(rows_out)
    shares_out = [
        (send(share_ref.at[0], shared_ref.at[0], small, 6, down), "down"),
        (send(share_ref.at[1], shared_ref.at[1], small, 7, up), "up"),
    ]
    for side in range(2):
        a, b = ((8, 9), (3, 2))[side]
        mine = b - 1
        theirs = 1 - side
        w = []
        for t in range(2):
            k, t0, t1 = (raw_ref[n, t, mine : mine + 1, :] for n in range(3))
            own = (1.0 - 4.0 * k - t0 - t1, k + t0 if side == 0 else k) + sideways(k, t1, t)
            k, t0, t1 = (rowin_ref[theirs, t, n : n + 1, :] for n in range(3))
            near = (1.0 - 4.0 * k - t0 - t1, k + t0 if side == 0 else k) + sideways(k, t1, t)
            if side == 0:
                far = rowin_ref[theirs, t, 3:4, :] + rowin_ref[theirs, t, 4:5, :]
            else:
                far = rowin_ref[theirs, t, 3:4, :]
            w.append((own, near, far))
        for part in range(CHUNKS):
            some = slice(part * PART, part * PART + PART)
            ub = [u_ref[t, b, some, :] for t in range(2)]
            h = [w[t][1][1] * ub[t] for t in range(2)]
            b_left, b_right = [pltpu.roll(v, 1, 1) for v in ub], [pltpu.roll(v, 127, 1) for v in ub]
            h_left, h_right = [pltpu.roll(v, 1, 1) for v in h], [pltpu.roll(v, 127, 1) for v in h]

            def ends_of(before, after, t):
                if t == 0:
                    return before[0], jnp.where(few == 127, after[1], after[0])
                return jnp.where(few == 0, before[0], before[1]), after[1]

            for t in range(2):
                own, near, far = w[t]
                bl, br = ends_of(b_left, b_right, t)
                hl, hr = ends_of(h_left, h_right, t)
                g = (own[0] * ub[t] + own[1] * u_ref[t, a, some, :]) + (own[2] * bl + own[3] * br)
                cut = slice(128 * t, 128 * t + 128)
                give_ref[0, some, cut] = (near[0] * h[t] + near[1] * g) + (near[2] * hl + near[3] * hr)
                give_ref[1, some, cut] = far * h[t]
        their_cells = rowin_ref[theirs, 0, 5:6, :]
        spots = places.astype(F32)
        got = jnp.zeros((384, 128), F32)
        for n, base in enumerate(((0, 256), (1792, 1536))[side]):
            chosen = jnp.where(spots + F32(base) == their_cells, F32(1.0), F32(0.0)).astype(BF16)
            got = got + jnp.dot(exact_parts(give_ref[n]), chosen, preferred_element_type=F32)
        share_ref[side] = (got[0:128] + got[128:256]) + got[256:384]
        begin(shares_out[side : side + 1])

    begin(halo[4:])
    arrived(cols_out)

    for n in range(3):
        for t in range(2):
            raw_ref[n, t, 0:1, :] = rowin_ref[0, t, n : n + 1, :]
            raw_ref[n, t, 9:10, :] = rowin_ref[1, t, n : n + 1, :]
        beyond = jnp.where(
            lanes8 == 127,
            pltpu.roll(colin_ref[0, 16:24, :], 127 - n, 1),
            pltpu.roll(colin_ref[1, 16:24, :], 125 - n, 1),
        )
        raw_ref[n, 2, 0:1, :] = jnp.zeros((1, 128), F32)
        raw_ref[n, 2, 1:9, :] = jnp.where((lanes8 == 127) | (lanes8 == 0), beyond, F32(0.0))
        raw_ref[n, 2, 9:10, :] = jnp.zeros((1, 128), F32)
    wide = lax.broadcasted_iota(jnp.int32, (10, 128), 1)
    deep = lax.broadcasted_iota(jnp.int32, (10, 128), 0)
    for t in range(3):
        k, t0, t1 = (raw_ref[n, t, 0:10, :] for n in range(3))
        zero = jnp.zeros_like(k)
        coef_ref[0, t, 0:10, :] = 1.0 - 4.0 * k - t0 - t1
        coef_ref[1, t, 0:10, :] = jnp.where((deep == 1) & (row == 0), zero, k + t0)
        coef_ref[2, t, 0:10, :] = jnp.where((deep == 8) & (row == 31), zero, k)
        w_left, w_right = k + t1, k
        if t == 0:
            w_left = jnp.where((wide == 0) & (col == 0), zero, w_left)
        if t == 1:
            w_right = jnp.where((wide == 127) & (col == 15), zero, w_right)
        coef_ref[3, t, 0:10, :] = w_left
        coef_ref[4, t, 0:10, :] = w_right

    comb_ref[...] = jnp.zeros((128, 128), F32)
    for r in range(8):
        comb_ref[4 * r + 4 : 4 * r + 6, :] = colin_ref[0, 2 * r : 2 * r + 2, :]
        comb_ref[4 * r + 6 : 4 * r + 8, :] = colin_ref[1, 2 * r : 2 * r + 2, :]
    turned = comb_ref[...].T
    for n in range(1, 9):
        u_ref[2, n + 1] = pltpu.roll(turned, (126 - 4 * n) % 128, 1)

    def first_step(some, n, all_rows):
        tiles = range(3) if 1 <= n <= 8 else range(2)

        def get(t, i):
            if not all_rows and (i in (-1, 10) or (i in (0, 9) and t < 2)):
                return jnp.zeros((PART, 128), F32)
            return u_ref[t, i + 1, some, :]

        for t, v in zip(tiles, stencil(get, coef_ref, n, tiles, few)):
            f_ref[t, n, some, :] = v

    def second_step(some, n):
        for t, v in zip(range(2), stencil(lambda t, i: f_ref[t, i, some, :], coef_ref, n, range(2), few)):
            full_ref[n - 1, some, 128 * t : 128 * t + 128] = v

    @pl.loop(0, CHUNKS)
    def _(part):
        some = pl.ds(pl.multiple_of(part * PART, PART), PART)
        for n in range(2, 8):
            first_step(some, n, False)
        for n in range(3, 7):
            second_step(some, n)

    def observe(n):
        return jnp.dot(exact_parts(full_ref[n]), pick_ref[n], preferred_element_type=F32)

    acc_ref[...] = (observe(2) + observe(3)) + (observe(4) + observe(5))

    arrived(corners_out)
    for side in range(2):
        comb_ref[2 * side : 2 * side + 2, :] = cor_ref[0, side, 6:8, :]
        comb_ref[36 + 2 * side : 38 + 2 * side, :] = cor_ref[1, side, 0:2, :]
    turned = comb_ref[...].T
    for n in (0, 9):
        u_ref[2, n + 1] = pltpu.roll(turned, (126 - 4 * n) % 128, 1)

    def end_rows(some, all_rows):
        for n in (0, 1, 8, 9):
            first_step(some, n, all_rows)
        for n in (1, 2, 7, 8):
            second_step(some, n)

    @pl.loop(0, CHUNKS)
    def _(part):
        end_rows(pl.ds(pl.multiple_of(part * PART, PART), PART), False)

    seen = acc_ref[...] + ((observe(0) + observe(1)) + (observe(6) + observe(7)))
    arrived(shares_out)
    observed = ((seen[0:128] + seen[128:256]) + seen[256:384]) + (shared_ref[0] + shared_ref[1])
    obs_mean = jnp.sum(observed, axis=0, keepdims=True) * F32(1.0 / 128.0)
    err = error_ref[...]
    scaled = (observed - obs_mean) / (err * jnp.sqrt(F32(127.0)))
    innovation = jnp.broadcast_to((value_ref[...] - obs_mean) / err, (8, 128))
    turned_dot = (((1,), (1,)), ((), ()))
    gram = lax.dot_general(scaled, scaled, turned_dot, precision=HIGHEST, preferred_element_type=F32)
    pulled = lax.dot_general(innovation, scaled, turned_dot, precision=HIGHEST, preferred_element_type=F32)
    deep128 = lax.broadcasted_iota(jnp.int32, (128, 128), 0)
    diagonal = jnp.sum(jnp.where(lanes == deep128, gram, F32(0.0)), axis=0, keepdims=True)
    rows8 = lax.broadcasted_iota(jnp.int32, (8, 128), 0)
    folded = pltpu.roll(gram[64:128], 64, 1)
    for g in range(8):
        cut = slice(8 * g, 8 * g + 8)
        keep = (lanes8 >= 64) | (lanes8 < rows8 + 8 * g)
        part_ref[g, 0:8, :] = jnp.where(keep, gram[cut], folded[cut])
        part_ref[g, 8:9, :] = pulled[0:1]
        part_ref[g, 9:10, :] = diagonal

    def exchange(main, into, sems, place, ids, devs):
        out = [send(main(n), into.at[place], (sems.at[0], sems.at[1]), n, dev, landed=place) for n, dev in zip(ids, devs)]
        for c in out:
            c.start()
        return out

    def landed(main, into, sems, ids, devs):
        for n, dev in zip(ids, devs):
            send(main, into.at[n], (sems.at[0], sems.at[1]), n, dev).wait_recv()

    def total(buf):
        return ((buf[0] + buf[1]) + (buf[2] + buf[3])) + ((buf[4] + buf[5]) + (buf[6] + buf[7]))

    rs = exchange(lambda n: part_ref.at[n], rs_ref, rs_sem, me, group, group_dev)
    rs_ref[pl.ds(me, 1)] = part_ref[pl.ds(me, 1)]

    def depart(rows):
        for r in rows:
            v = full_ref[r]
            mean = jnp.sum(v, axis=0, keepdims=True) * F32(1.0 / 128.0)
            mean_ref[r : r + 1, :] = mean
            d_ref[r] = v - mean

    def finish_rows(half):
        arrived(halo[4 * half : 4 * half + 4])

        @pl.loop(half * (CHUNKS // 2), (half + 1) * (CHUNKS // 2))
        def _(part):
            end_rows(pl.ds(pl.multiple_of(part * PART, PART), PART), True)

    depart(range(2, 6))

    landed(part_ref.at[0], rs_ref, rs_sem, group, group_dev)
    ysrc_ref[...] = total(rs_ref)
    by_y = exchange(lambda n: ysrc_ref, yin_ref, y_sem, y, ys, y_dev)
    yin_ref[pl.ds(y, 1)] = ysrc_ref[...][None]
    finish_rows(0)
    landed(ysrc_ref, yin_ref, y_sem, ys, y_dev)
    zsrc_ref[...] = total(yin_ref)
    by_z = exchange(lambda n: zsrc_ref, zin_ref, z_sem, z, zs, z_dev)
    zin_ref[pl.ds(z, 1)] = zsrc_ref[...][None]
    finish_rows(1)
    depart((0, 1, 6, 7))
    landed(zsrc_ref, zin_ref, z_sem, zs, z_dev)
    whole = total(zin_ref)
    fin_ref[...] = whole[0:8]
    ag = exchange(lambda n: fin_ref, gat_ref, ag_sem, me, group, group_dev)
    gat_ref[pl.ds(me, 1)] = fin_ref[...][None]
    total_ref[64:66, :] = whole[8:10]
    total_ref[66:72, :] = jnp.zeros((6, 128), F32)
    landed(fin_ref, gat_ref, ag_sem, group, group_dev)
    for g in range(8):
        total_ref[8 * g : 8 * g + 8, :] = gat_ref[g]
    gone(halo + rows_out + cols_out + corners_out + shares_out)
    for c in rs + by_y + by_z + ag:
        c.wait_send()


def front(prior, spread, courant, cells, value, error):
    vmem, hbm = pl.BlockSpec(memory_space=pltpu.VMEM), pl.BlockSpec(memory_space=pl.ANY)
    dma = pltpu.SemaphoreType.DMA
    return pl.pallas_call(
        front_kernel,
        out_shape=(
            pltpu.VMEM((8, 128, 256), F32),
            pltpu.VMEM((8, 256), F32),
            pltpu.VMEM((72, 128), F32),
        ),
        in_specs=[hbm] * 6,
        out_specs=(vmem, vmem, vmem),
        scratch_shapes=[
            pltpu.VMEM((8, 256), F32),
            pltpu.VMEM((16, 256), F32),
            pltpu.VMEM((1, 128), jnp.int32),
            pltpu.VMEM((1, 128), F32),
            pltpu.VMEM((1, 128), F32),
            pltpu.VMEM((2, 1024, 128), F32),
            pltpu.VMEM((3, 12, 128, 128), F32),
            pltpu.VMEM((3, 10, 128, 128), F32),
            pltpu.VMEM((8, 128, 256), F32),
            pltpu.VMEM((8, 256, 128), BF16),
            pltpu.VMEM((3, 3, 16, 128), F32),
            pltpu.VMEM((5, 3, 16, 128), F32),
            pltpu.VMEM((2, 24, 128), F32),
            pltpu.VMEM((2, 24, 128), F32),
            pltpu.VMEM((2, 2, 8, 128), F32),
            pltpu.VMEM((2, 2, 8, 128), F32),
            pltpu.VMEM((2, 2, 8, 128), F32),
            pltpu.VMEM((128, 128), F32),
            pltpu.VMEM((384, 128), F32),
            pltpu.VMEM((2, 128, 256), F32),
            pltpu.VMEM((2, 128, 128), F32),
            pltpu.VMEM((2, 128, 128), F32),
            pltpu.VMEM((8, 10, 128), F32),
            pltpu.VMEM((8, 10, 128), F32),
            pltpu.VMEM((10, 128), F32),
            pltpu.VMEM((8, 10, 128), F32),
            pltpu.VMEM((10, 128), F32),
            pltpu.VMEM((8, 10, 128), F32),
            pltpu.VMEM((8, 128), F32),
            pltpu.VMEM((8, 8, 128), F32),
            dma((2 * CHUNKS,)),
            dma((5,)),
            dma((8,)),
            dma((8,)),
            dma((10,)),
            dma((10,)),
            dma((2, 8)),
            dma((2, 8)),
            dma((2, 8)),
            dma((2, 8)),
        ],
        compiler_params=pltpu.CompilerParams(collective_id=0, has_side_effects=True),
        name="front",
    )(prior, spread, courant, cells, value, error)


def body(
    prior_sample_fields, spreading_coefficient, transport_courant, obs_cells, obs_value, obs_error
):
    departures, mean, packed = front(
        prior_sample_fields.reshape(1024, 256),
        spreading_coefficient,
        transport_courant.reshape(16, 256),
        obs_cells[None, :],
        obs_value[None, :],
        obs_error[None, :],
    )
    return tail(packed, departures, mean).reshape(128, 8, 256)


def solution(mesh):
    split = Mesh(mesh.devices.reshape(8, 4, 8, 2), ("row_0", "row_1", "col_0", "col_1"))
    return jax.shard_map(
        body,
        mesh=split,
        in_specs=(
            P(None, ROW, COL),
            P(ROW, COL),
            P(None, ROW, COL),
            P(ROW_COL),
            P(ROW_COL),
            P(ROW_COL),
        ),
        out_specs=P(None, ROW, COL),
        check_vma=False,
    )
```
